256 devices in a mesh: tm: 4 (over x_hi, core), space: 64 (over z, x_lo, y).
Axes of the slice: x: 4 (x_hi: 2, x_lo: 2; x = x_hi * 2 + x_lo), y: 4, z: 8, core: 2. Of those that a mesh axis runs over, the one named last changes fastest.
Arguments:
- queries: bfloat16 [4, 4, 64, 32, 1536], P('tm', None, 'space'), may hold values from -30 to 30
- key_states: bfloat16 [4, 4, 64, 32, 1536], P('tm', None, 'space'), may hold values from -30 to 30, as said below
- value_states: bfloat16 [4, 4, 64, 32, 1536], P('tm', None, 'space'), may hold values from -6 to 6
- conv_weight: float32 [3, 3, 3, 1536], replicated, may hold values from -0.3125 to 0.3125
Outputs:
- mixed: bfloat16 [4, 4, 64, 32, 1536], P('tm', None, 'space')
The draws below stay inside these ranges and needn't reach their ends.
Inputs may be any that keep to these rules, and one draw needn't show every extreme that they name: `key_states`: entries are real-valued keys.
All inputs are finite; a program needn't handle non-finite values.
Results may differ from the reference program's by a relative error of at most 0.0088.
Values may be sent and summed in bfloat16 or wider, within the bound.
No kernel may reach another device: no remote copies, remote signals or barrier semaphores. Data moves between devices by JAX's collectives and lax.ppermute only.
A program may use at most 192 MiB of HBM per device.

```python
import jax
import jax.numpy as jnp
from jax import lax

HEADS = 24
HEAD_DIM = 64
D = 1536
FRAMES = 4
ROWS_DEV = 1
COLUMNS = 32
AGENT_DEV = 4
GROUPS = 4
ROWS = 64
AGENTS = 256
N_SPACE = 64


def draw_queries(key, part):
    region_key, noise_key = jax.random.split(jax.random.fold_in(key, 11))
    region = 0.5 * jax.random.normal(region_key, (GROUPS, AGENTS, D), jnp.float32)
    shape = (GROUPS, FRAMES, ROWS, COLUMNS, D)
    noise = 4.0 * jax.random.normal(noise_key, shape, jnp.float32)
    spread = region.reshape(GROUPS, 1, ROWS // ROWS_DEV, 1, AGENT_DEV, 1, D)
    spread = jnp.broadcast_to(spread, (GROUPS, FRAMES, ROWS // ROWS_DEV, ROWS_DEV, AGENT_DEV, COLUMNS // AGENT_DEV, D)).reshape(shape)
    return jnp.clip(spread + noise, -30.0, 30.0).astype(jnp.bfloat16)


def draw_key_states(key, part):
    noise_key = jax.random.fold_in(key, 13)
    shape = (GROUPS, FRAMES, ROWS, COLUMNS, D)
    states = 5.0 * jax.random.normal(noise_key, shape, jnp.float32)
    return jnp.clip(states, -30.0, 30.0).astype(jnp.bfloat16)


def shard_levels(rng, shape, cuts, smallest, top_value):
    def one(position, shards_of):
        draws = jax.random.uniform(jax.random.fold_in(jax.random.fold_in(rng, 6), position), (shards_of,), jnp.float32, smallest / len(cuts), top_value / len(cuts))
        return jnp.repeat(jnp.exp(draws), shape[position] // shards_of).reshape((-1,) + (1,) * (len(shape) - position - 1))

    factor_of = one(*cuts[0])
    for cut in cuts[1:]:
        factor_of = factor_of * one(*cut)
    return factor_of


def scatter_about(rng, shape, scale, reach, shards=(), held_as=jnp.bfloat16):
    drawn = jax.random.normal(rng, shape, jnp.float32) * scale
    if len(shards) > 0:
        drawn = shard_levels(rng, shape, shards, -0.22, 0.18) * drawn
    return jnp.clip(drawn, min=-reach, max=reach).astype(held_as)


def setup_inputs(seed: int = 0) -> dict:
    splits = jax.random.split(jax.random.key(seed), 5)
    return {
        "queries": draw_queries(jax.random.fold_in(splits[4], 71), 0),
        "key_states": draw_key_states(jax.random.fold_in(splits[4], 71), 0),
        "value_states": scatter_about(splits[2], (GROUPS, FRAMES, ROWS, COLUMNS, D), 1.0, 6.0, ((0, 4), (2, 64))),
        "conv_weight": scatter_about(splits[3], (3, 3, 3, D), 432 ** -0.5, 0.3125, (), jnp.float32),
    }


def mix_local(window, conv_weight):
    shape = (window.shape[0] - 2, window.shape[1] - 2, window.shape[2] - 2, window.shape[3])
    total = jnp.zeros(shape, jnp.float32)
    for time_off in range(3):
        for row_off in range(3):
            for col_off in range(3):
                piece = window[time_off:time_off + shape[0], row_off:row_off + shape[1], col_off:col_off + shape[2]]
                total = total + piece.astype(jnp.float32) * conv_weight[time_off, row_off, col_off]
    return total


def head_pass(inputs):
    query_head, key_head, value_head, agent_head = inputs
    inv_root = HEAD_DIM ** -0.5
    scores = jnp.dot(agent_head, key_head.T, preferred_element_type=jnp.float32) * inv_root
    weights = jnp.exp(scores - jnp.max(scores, axis=1, keepdims=True))
    totals = jnp.sum(weights, axis=1, keepdims=True)
    agent_values = (jnp.dot(weights.astype(jnp.bfloat16), value_head, preferred_element_type=jnp.float32) / totals).astype(jnp.bfloat16)
    query_scores = jnp.dot(query_head, agent_head.T, preferred_element_type=jnp.float32) * inv_root
    probs = jax.nn.softmax(query_scores, axis=1).astype(jnp.bfloat16)
    return jnp.dot(probs, agent_values, preferred_element_type=jnp.float32)


def split_heads(array, count):
    return array.reshape(count, HEADS, HEAD_DIM).transpose(1, 0, 2)


def reference(queries, key_states, value_states, conv_weight):
    timed = jnp.pad(value_states.reshape(GROUPS * FRAMES, ROWS, COLUMNS, D), ((1, 1), (0, 0), (0, 0), (0, 0)))

    def group_pass(inputs):
        group_query, group_key, group_value, group_index = inputs
        tokens = FRAMES * ROWS * COLUMNS
        pooled = jnp.mean(group_query.reshape(FRAMES, N_SPACE, ROWS_DEV, AGENT_DEV, COLUMNS // AGENT_DEV, D), axis=(0, 2, 4), dtype=jnp.float32)
        agents = pooled.reshape(AGENTS, D).astype(jnp.bfloat16)
        heads_out = lax.map(head_pass, (split_heads(group_query, tokens), split_heads(group_key, tokens), split_heads(group_value, tokens), split_heads(agents, AGENTS)))
        attended = heads_out.transpose(1, 0, 2).reshape(FRAMES, ROWS, COLUMNS, D)
        frames_cut = lax.dynamic_slice_in_dim(timed, group_index * FRAMES, FRAMES + 2, 0)
        window = jnp.pad(frames_cut, ((0, 0), (1, 1), (1, 1), (0, 0)))
        local_mix = mix_local(window, conv_weight)
        return (attended + local_mix).astype(jnp.bfloat16)

    return lax.map(group_pass, (queries, key_states, value_states, jnp.arange(GROUPS, dtype=jnp.int32)))
```

```python
import jax
import jax.numpy as jnp
from jax import lax
from jax.experimental import pallas as pl
from jax.experimental.pallas import tpu as pltpu
from jax.sharding import Mesh
from jax.sharding import PartitionSpec as P

HEADS = 24
HEAD_DIM = 64
D = 1536
FRAMES = 4
COLUMNS = 32
TOKENS = FRAMES * COLUMNS
AGENT_DEV = 4
PLANES = 8
TILES = 8
AGENTS = 256
GROUP_HEADS = HEADS // TILES
GROUP = GROUP_HEADS * HEAD_DIM
HALF = GROUP // 2
K_ROW = GROUP
V_ROW = 2 * GROUP
H_ROW = 3 * GROUP
SENT = H_ROW + HALF
STATS = 16
INV_ROOT = HEAD_DIM ** (-0.5)
F32 = jnp.float32
BF16 = jnp.bfloat16


def call(kernel, out_shape, us, *args):
    cost = pl.CostEstimate(flops=int(us * 3.0e8), bytes_accessed=int(us * 2.0e6), transcendentals=0)
    return pl.pallas_call(kernel, out_shape=out_shape, cost_estimate=cost)(*args)


def pool_kernel(q_ref, out_ref):
    shape = (8, TOKENS)
    token = lax.broadcasted_iota(jnp.int32, shape, 1)
    agent = lax.broadcasted_iota(jnp.int32, shape, 0)
    width = COLUMNS // AGENT_DEV
    pick = ((token % COLUMNS) // width == agent).astype(F32).astype(BF16)
    sums = jnp.dot(pick, q_ref[...], preferred_element_type=F32)
    pooled = (sums[:AGENT_DEV] * (1.0 / (FRAMES * width))).astype(BF16)
    for tile in range(TILES):
        part = pooled[:, tile * GROUP : (tile + 1) * GROUP]
        for plane in range(PLANES):
            out_ref[plane * TILES + tile] = part


def pack_kernel(q_ref, k_ref, v_ref, before_ref, after_ref, out_ref):
    for row, ref in ((0, q_ref), (K_ROW, k_ref), (V_ROW, v_ref)):
        flipped = ref[...].T
        for tile in range(TILES):
            out_ref[tile, row : row + GROUP, :] = flipped[tile * GROUP : (tile + 1) * GROUP]
    edges = jnp.concatenate([before_ref[...], after_ref[...]], axis=0).T
    for tile in range(TILES):
        low = edges[tile * GROUP : tile * GROUP + HALF]
        high = edges[tile * GROUP + HALF : (tile + 1) * GROUP]
        out_ref[tile, H_ROW:, :] = jnp.concatenate([low, high], axis=1)


def rows_of(x_ref, start, size):
    return jnp.concatenate([x_ref[s, start : start + size, :] for s in range(TILES)], axis=1)


def agent_kernel(a_ref, x_ref, out_ref):
    columns = []
    lane = lax.broadcasted_iota(jnp.int32, (AGENTS, HEAD_DIM), 1)
    stats = jnp.zeros((AGENTS, HEAD_DIM), F32)
    for h in range(GROUP_HEADS):
        keys = rows_of(x_ref, K_ROW + h * HEAD_DIM, HEAD_DIM)
        values = rows_of(x_ref, V_ROW + h * HEAD_DIM, HEAD_DIM)
        agents = a_ref[:, h * HEAD_DIM : (h + 1) * HEAD_DIM]
        scores = jnp.dot(agents, keys, preferred_element_type=F32) * INV_ROOT
        peak = jnp.max(scores, axis=1, keepdims=True)
        weights = jnp.exp(scores - peak)
        total = jnp.sum(weights, axis=1, keepdims=True)
        acc = lax.dot_general(
            weights.astype(BF16), values, (((1,), (1,)), ((), ())), preferred_element_type=F32
        )
        columns.append(acc / total)
        left = peak + jnp.log(total)
        for piece in range(3):
            short = left.astype(BF16).astype(F32)
            left = left - short
            stats = jnp.where(lane == piece * GROUP_HEADS + h, short, stats)
    flipped = jnp.concatenate(columns + [stats], axis=1).T
    out_ref[...] = flipped[: GROUP + STATS].astype(BF16)


def query_kernel(a_ref, x_ref, e_ref, total_ref):
    for h in range(GROUP_HEADS):
        queries = rows_of(x_ref, h * HEAD_DIM, HEAD_DIM)
        agents = a_ref[:, h * HEAD_DIM : (h + 1) * HEAD_DIM]
        scores = jnp.dot(agents, queries, preferred_element_type=F32) * INV_ROOT
        weights = jnp.exp(scores - jnp.max(scores, axis=0, keepdims=True))
        total_ref[h : h + 1, :] = jnp.sum(weights, axis=0, keepdims=True)
        e_ref[h] = weights.astype(BF16)


def conv_kernel(x_ref, above_ref, below_ref, w_ref, out_ref):
    tall = 16
    lane = lax.broadcasted_iota(jnp.int32, (tall, TOKENS), 1)
    column = lane % COLUMNS
    first, last = lane < COLUMNS, lane >= TOKENS - COLUMNS

    def frames_of(r, at, edge_at, low):
        if r < 0:
            cells, edge = above_ref[pl.ds(at, tall), :], above_ref[pl.ds(GROUP + edge_at, tall), :]
        elif r == TILES:
            cells, edge = below_ref[pl.ds(at, tall), :], below_ref[pl.ds(GROUP + edge_at, tall), :]
        else:
            cells = x_ref[r, pl.ds(V_ROW + at, tall), :]
            edge = x_ref[r, pl.ds(H_ROW + edge_at, tall), :]
        cells, edge = cells.astype(F32), edge.astype(F32)
        turned = pltpu.roll(edge, TOKENS // 2, 1)
        before, after = (edge, turned) if low else (turned, edge)
        return (
            jnp.where(first, before, pltpu.roll(cells, COLUMNS, 1)),
            cells,
            jnp.where(last, after, pltpu.roll(cells, TOKENS - COLUMNS, 1)),
        )

    for low in (True, False):

        def step(i, carry, low=low):
            edge_at = pl.multiple_of(i * tall, tall)
            at = pl.multiple_of(edge_at + (0 if low else HALF), tall)
            w = w_ref[pl.ds(at, tall), :]
            taps = [jnp.broadcast_to(w[:, n : n + 1], (tall, TOKENS)) for n in range(27)]
            rows = {r: frames_of(r, at, edge_at, low) for r in range(-1, 2)}
            for r in range(TILES):
                if r > 0:
                    rows[r + 1] = frames_of(r + 1, at, edge_at, low)
                sums = []
                for k in range(3):
                    total = None
                    for j in range(3):
                        for i3 in range(3):
                            term = rows[r + j - 1][i3] * taps[i3 * 9 + j * 3 + k]
                            total = term if total is None else total + term
                    sums.append(total)
                left = jnp.where(column == 0, 0.0, pltpu.roll(sums[0], 1, 1))
                right = jnp.where(column == COLUMNS - 1, 0.0, pltpu.roll(sums[2], TOKENS - 1, 1))
                out_ref[r, pl.ds(at, tall), :] = left + sums[1] + right
            return carry

        lax.fori_loop(0, HALF // tall, step, 0)


def mix_kernel(parts_ref, e_ref, total_ref, local_ref, out_ref):
    logs = []
    for z in range(PLANES):
        pieces = parts_ref[z, GROUP : GROUP + STATS, :].astype(F32)
        n = GROUP_HEADS
        logs.append(pieces[:n] + pieces[n : 2 * n] + pieces[2 * n : 3 * n])
    peak = logs[0]
    for log in logs[1:]:
        peak = jnp.maximum(peak, log)
    shares = [jnp.exp(log - peak) for log in logs]
    whole = sum(shares[1:], shares[0])
    shares = [share / whole for share in shares]
    for h in range(GROUP_HEADS):
        rows = slice(h * HEAD_DIM, (h + 1) * HEAD_DIM)
        values = None
        for z in range(PLANES):
            term = parts_ref[z, rows, :].astype(F32) * shares[z][h : h + 1]
            values = term if values is None else values + term
        mixed = jnp.dot(values.astype(BF16), e_ref[h], preferred_element_type=F32)
        mixed = mixed / total_ref[h : h + 1, :]
        for s in range(TILES):
            cells = mixed[:, s * TOKENS : (s + 1) * TOKENS]
            out_ref[s, rows, :] = (cells + local_ref[s, rows, :]).astype(BF16)


def unpack_kernel(x_ref, out_ref):
    out_ref[...] = x_ref[...].reshape(D, TOKENS).T


def on_device(queries, key_states, value_states, conv_weight):
    q = queries.reshape(TOKENS, D)
    k = key_states.reshape(TOKENS, D)
    v = value_states.reshape(TOKENS, D)
    groups = lax.axis_size("tm")
    ends = groups - 1
    before = lax.ppermute(v[TOKENS - COLUMNS :], "tm", [(i, i + 1) for i in range(ends)])
    after = lax.ppermute(v[:COLUMNS], "tm", [(i + 1, i) for i in range(ends)])

    pooled = call(pool_kernel, jax.ShapeDtypeStruct((PLANES * TILES, AGENT_DEV, GROUP), BF16), 1.0, q)
    agents = lax.all_to_all(pooled, ("z", "xy"), 0, 0).reshape(AGENTS, GROUP)

    packed = call(
        pack_kernel, jax.ShapeDtypeStruct((TILES, SENT, TOKENS), BF16), 3.0, q, k, v, before, after
    )
    x = lax.all_to_all(packed, "xy", 0, 0)

    above = lax.ppermute(x[TILES - 1, V_ROW:], "z", [(i, i + 1) for i in range(PLANES - 1)])
    below = lax.ppermute(x[0, V_ROW:], "z", [(i + 1, i) for i in range(PLANES - 1)])

    part = call(
        agent_kernel, jax.ShapeDtypeStruct((GROUP + STATS, AGENTS), BF16), 4.0, agents, x
    )
    parts = lax.all_to_all(jnp.broadcast_to(part[None], (PLANES, *part.shape)), "z", 0, 0)

    weights, totals = call(
        query_kernel,
        (
            jax.ShapeDtypeStruct((GROUP_HEADS, AGENTS, TILES * TOKENS), BF16),
            jax.ShapeDtypeStruct((8, TILES * TOKENS), F32),
        ),
        4.0,
        agents,
        x,
    )
    taps = lax.dynamic_index_in_dim(
        conv_weight.reshape(27, TILES, GROUP), lax.axis_index("xy"), 1, keepdims=False
    ).T
    local = call(
        conv_kernel, jax.ShapeDtypeStruct((TILES, GROUP, TOKENS), F32), 6.0, x, above, below, taps
    )
    mixed = call(
        mix_kernel,
        jax.ShapeDtypeStruct((TILES, GROUP, TOKENS), BF16),
        3.0,
        parts,
        weights,
        totals,
        local,
    )
    mine = lax.all_to_all(mixed, "xy", 0, 0)
    out = call(unpack_kernel, jax.ShapeDtypeStruct((TOKENS, D), BF16), 1.0, mine)
    return out.reshape(value_states.shape)


def solution(mesh):
    devices = mesh.devices
    fine = Mesh(devices.reshape(devices.shape[0], PLANES, TILES), ("tm", "z", "xy"))
    spec = P("tm", None, ("z", "xy"), None, None)
    return jax.shard_map(
        on_device,
        mesh=fine,
        in_specs=(spec, spec, spec, P()),
        out_specs=spec,
        check_vma=False,
    )
```

```python
import jax
import jax.numpy as jnp
from jax import lax
from jax.experimental import pallas as pl
from jax.experimental.pallas import tpu as pltpu
from jax.sharding import Mesh
from jax.sharding import PartitionSpec as P


HEADS = 24
HEAD_DIM = 64
D = 1536
FRAMES = 4
COLUMNS = 32
TOKENS = FRAMES * COLUMNS
AGENT_DEV = 4
PLANES = 8
TILES = 8
AGENTS = 256
GROUP_HEADS = HEADS // TILES
GROUP = GROUP_HEADS * HEAD_DIM
K_ROW = GROUP
V_ROW = 2 * GROUP
SENT = 3 * GROUP
PLANE_AGENTS = TILES * AGENT_DEV
EDGE_ROWS = TILES + 2
EDGE = 3 * TOKENS
STATS = 16
GRANT = 6 * 1024 * 1024
INV_ROOT = HEAD_DIM ** (-0.5)
F32 = jnp.float32
BF16 = jnp.bfloat16


VMEM = pl.BlockSpec(memory_space=pltpu.VMEM)

SMEM = pl.BlockSpec(memory_space=pltpu.SMEM)


def call(kernel, out_shape, us, *args, scalars=(), scratch=()):
    cost = pl.CostEstimate(flops=int(us * 3.0e8), bytes_accessed=int(us * 2.0e6), transcendentals=0)
    many = isinstance(out_shape, tuple)
    return pl.pallas_call(
        kernel,
        out_shape=out_shape,
        in_specs=[SMEM] * len(scalars) + [VMEM] * len(args),
        out_specs=(VMEM,) * len(out_shape) if many else VMEM,
        scratch_shapes=list(scratch),
        cost_estimate=cost,
        compiler_params=pltpu.CompilerParams(vmem_limit_bytes=GRANT),
    )(*scalars, *args)


def exchange(x, axes):
    return lax.all_to_all(x, axes, 0, 0)


def shift(x, axis, step):
    count = lax.axis_size(axis)
    pairs = [(i, i + step) for i in range(count) if 0 <= i + step < count]
    return lax.ppermute(x, axis, pairs)


def pool_kernel(q_ref, out_ref):
    shape = (8, TOKENS)
    token = lax.broadcasted_iota(jnp.int32, shape, 1)
    agent = lax.broadcasted_iota(jnp.int32, shape, 0)
    width = COLUMNS // AGENT_DEV
    pick = ((token % COLUMNS) // width == agent).astype(F32).astype(BF16)
    sums = jnp.dot(pick, q_ref[...], preferred_element_type=F32)
    pooled = (sums[:AGENT_DEV] * (1.0 / (FRAMES * width))).astype(BF16)
    for tile in range(TILES):
        out_ref[tile] = pooled[:, tile * GROUP : (tile + 1) * GROUP]


def pack_kernel(q_ref, k_ref, v_ref, out_ref):
    for row, ref in ((0, q_ref), (K_ROW, k_ref), (V_ROW, v_ref)):
        flipped = ref[...].T
        for tile in range(TILES):
            out_ref[tile, row : row + GROUP, :] = flipped[tile * GROUP : (tile + 1) * GROUP]


def rows_of(x_ref, start, size):
    return jnp.concatenate([x_ref[s, start : start + size, :] for s in range(TILES)], axis=1)


def agent_kernel(z_ref, *refs):
    came, (x_ref, out_ref, a_ref) = refs[:PLANES], refs[PLANES:]
    for hop, ref in enumerate(came):
        z = lax.rem(z_ref[0] + PLANES - hop, PLANES)
        a_ref[pl.ds(pl.multiple_of(z * PLANE_AGENTS, PLANE_AGENTS), PLANE_AGENTS), :] = ref[...]
    columns = []
    lane = lax.broadcasted_iota(jnp.int32, (AGENTS, HEAD_DIM), 1)
    stats = jnp.zeros((AGENTS, HEAD_DIM), F32)
    for h in range(GROUP_HEADS):
        keys = rows_of(x_ref, K_ROW + h * HEAD_DIM, HEAD_DIM)
        values = rows_of(x_ref, V_ROW + h * HEAD_DIM, HEAD_DIM)
        agents = a_ref[:, h * HEAD_DIM : (h + 1) * HEAD_DIM]
        scores = jnp.dot(agents, keys, preferred_element_type=F32) * INV_ROOT
        peak = jnp.max(scores, axis=1, keepdims=True)
        weights = jnp.exp(scores - peak)
        total = jnp.sum(weights, axis=1, keepdims=True)
        acc = lax.dot_general(
            weights.astype(BF16), values, (((1,), (1,)), ((), ())), preferred_element_type=F32
        )
        columns.append(acc / total)
        left = peak + jnp.log(total)
        for piece in range(3):
            short = left.astype(BF16).astype(F32)
            left = left - short
            stats = jnp.where(lane == piece * GROUP_HEADS + h, short, stats)
    flipped = jnp.concatenate(columns + [stats], axis=1).T
    part = flipped[: GROUP + STATS].astype(BF16)
    for z in range(PLANES):
        out_ref[z] = part


def query_kernel(a_ref, x_ref, e_ref, total_ref):
    for h in range(GROUP_HEADS):
        queries = rows_of(x_ref, h * HEAD_DIM, HEAD_DIM)
        agents = a_ref[:, h * HEAD_DIM : (h + 1) * HEAD_DIM]
        scores = jnp.dot(agents, queries, preferred_element_type=F32) * INV_ROOT
        weights = jnp.exp(scores - jnp.max(scores, axis=0, keepdims=True))
        total_ref[h : h + 1, :] = jnp.sum(weights, axis=0, keepdims=True)
        e_ref[h] = weights.astype(BF16)


def edge_kernel(x_ref, above_ref, below_ref, last_ref, first_ref):
    spot = lax.broadcasted_iota(jnp.int32, (GROUP, TOKENS), 1) // COLUMNS
    for block in range(EDGE // TOKENS):
        last = first = jnp.zeros((GROUP, TOKENS), F32)
        for j in range(FRAMES):
            row = block * FRAMES + j
            if row >= EDGE_ROWS:
                break
            if row == 0:
                cells = above_ref[...]
            elif row == EDGE_ROWS - 1:
                cells = below_ref[...]
            else:
                cells = x_ref[row - 1, V_ROW:, :]
            cells = cells.astype(F32)
            late = cells if j == FRAMES - 1 else pltpu.roll(cells, (j + 1) * COLUMNS, 1)
            early = cells if j == 0 else pltpu.roll(cells, j * COLUMNS, 1)
            last = jnp.where(spot == j, late, last)
            first = jnp.where(spot == j, early, first)
        lanes = slice(block * TOKENS, (block + 1) * TOKENS)
        last_ref[:, lanes] = last.astype(BF16)
        first_ref[:, lanes] = first.astype(BF16)


def conv_kernel(x_ref, above_ref, below_ref, before_ref, after_ref, w_ref, out_ref):
    tall = 16
    lane = lax.broadcasted_iota(jnp.int32, (tall, TOKENS), 1)
    column = lane % COLUMNS
    head, tail = lane < COLUMNS, lane >= TOKENS - COLUMNS

    def turned(cells, by):
        by %= TOKENS
        return cells if by == 0 else pltpu.roll(cells, by, 1)

    def frames_of(r, at):
        if r < 0:
            cells = above_ref[pl.ds(at, tall), :]
        elif r == TILES:
            cells = below_ref[pl.ds(at, tall), :]
        else:
            cells = x_ref[r, pl.ds(V_ROW + at, tall), :]
        cells = cells.astype(F32)
        block, j = divmod(r + 1, FRAMES)
        lanes = slice(block * TOKENS, (block + 1) * TOKENS)
        before = turned(before_ref[pl.ds(at, tall), lanes].astype(F32), -j * COLUMNS)
        after = turned(after_ref[pl.ds(at, tall), lanes].astype(F32), (FRAMES - 1 - j) * COLUMNS)
        return (
            jnp.where(head, before, turned(cells, COLUMNS)),
            cells,
            jnp.where(tail, after, turned(cells, -COLUMNS)),
        )

    def step(i, carry):
        at = pl.multiple_of(i * tall, tall)
        w = w_ref[pl.ds(at, tall), :]
        taps = [jnp.broadcast_to(w[:, n : n + 1], (tall, TOKENS)) for n in range(27)]
        rows = {r: frames_of(r, at) for r in range(-1, 1)}
        for r in range(TILES):
            rows[r + 1] = frames_of(r + 1, at)
            sums = []
            for k in range(3):
                total = None
                for j in range(3):
                    for i3 in range(3):
                        term = rows[r + j - 1][i3] * taps[i3 * 9 + j * 3 + k]
                        total = term if total is None else total + term
                sums.append(total)
            left = jnp.where(column == 0, 0.0, pltpu.roll(sums[0], 1, 1))
            right = jnp.where(column == COLUMNS - 1, 0.0, pltpu.roll(sums[2], TOKENS - 1, 1))
            out_ref[r, pl.ds(at, tall), :] = left + sums[1] + right
        return carry

    lax.fori_loop(0, GROUP // tall, step, 0)


def mix_kernel(parts_ref, e_ref, total_ref, local_ref, out_ref):
    logs = []
    for z in range(PLANES):
        pieces = parts_ref[z, GROUP : GROUP + STATS, :].astype(F32)
        n = GROUP_HEADS
        logs.append(pieces[:n] + pieces[n : 2 * n] + pieces[2 * n : 3 * n])
    peak = logs[0]
    for log in logs[1:]:
        peak = jnp.maximum(peak, log)
    shares = [jnp.exp(log - peak) for log in logs]
    whole = sum(shares[1:], shares[0])
    shares = [share / whole for share in shares]
    for h in range(GROUP_HEADS):
        rows = slice(h * HEAD_DIM, (h + 1) * HEAD_DIM)
        values = None
        for z in range(PLANES):
            term = parts_ref[z, rows, :].astype(F32) * shares[z][h : h + 1]
            values = term if values is None else values + term
        mixed = jnp.dot(values.astype(BF16), e_ref[h], preferred_element_type=F32)
        mixed = mixed / total_ref[h : h + 1, :]
        for s in range(TILES):
            cells = mixed[:, s * TOKENS : (s + 1) * TOKENS]
            out_ref[s, rows, :] = (cells + local_ref[s, rows, :]).astype(BF16)


def unpack_kernel(x_ref, out_ref):
    out_ref[...] = x_ref[...].reshape(D, TOKENS).T


def turn(x, axis, step):
    count = lax.axis_size(axis)
    return lax.ppermute(x, axis, [(i, (i + step) % count) for i in range(count)])


def body(queries, key_states, value_states, conv_weight):
    q = queries.reshape(TOKENS, D)
    k = key_states.reshape(TOKENS, D)
    v = value_states.reshape(TOKENS, D)
    shape = jax.ShapeDtypeStruct
    pooled = call(pool_kernel, shape((TILES, AGENT_DEV, GROUP), BF16), 1.0, q)
    packed = call(pack_kernel, shape((TILES, SENT, TOKENS), BF16), 3.0, q, k, v)
    own = exchange(pooled, "xy").reshape(PLANE_AGENTS, GROUP)
    x = exchange(packed, "xy")
    came = [own] + [turn(own, "z", n) for n in range(1, PLANES)]

    above = shift(x[TILES - 1, V_ROW:], "z", 1)
    below = shift(x[0, V_ROW:], "z", -1)

    part, agents = call(
        agent_kernel,
        (shape((PLANES, GROUP + STATS, AGENTS), BF16), shape((AGENTS, GROUP), BF16)),
        4.0,
        *came,
        x,
        scalars=(lax.axis_index("z").astype(jnp.int32).reshape(1),),
    )
    parts = exchange(part, "z")

    rim = shape((GROUP, EDGE), BF16)
    last, first = call(edge_kernel, (rim, rim), 1.0, x, above, below)
    before = shift(last, "tm", 1)
    after = shift(first, "tm", -1)
    weights, totals = call(
        query_kernel,
        (
            shape((GROUP_HEADS, AGENTS, TILES * TOKENS), BF16),
            shape((8, TILES * TOKENS), F32),
        ),
        4.0,
        agents,
        x,
    )
    taps = lax.dynamic_index_in_dim(
        conv_weight.reshape(27, TILES, GROUP), lax.axis_index("xy"), 1, keepdims=False
    ).T
    local = call(
        conv_kernel, shape((TILES, GROUP, TOKENS), F32), 6.0, x, above, below, before, after, taps
    )
    mixed = call(
        mix_kernel, shape((TILES, GROUP, TOKENS), BF16), 3.0, parts, weights, totals, local
    )
    mine = exchange(mixed, "xy")
    out = call(unpack_kernel, shape((TOKENS, D), BF16), 1.0, mine)
    return out.reshape(value_states.shape)


def solution(mesh):
    devices = mesh.devices
    fine = Mesh(devices.reshape(devices.shape[0], PLANES, TILES), ("tm", "z", "xy"))
    spec = P("tm", None, ("z", "xy"), None, None)
    return jax.shard_map(
        body,
        mesh=fine,
        in_specs=(spec, spec, spec, P()),
        out_specs=spec,
        check_vma=False,
    )
```

```python
import jax
import jax.numpy as jnp
from jax import lax
from jax.experimental import pallas as pl
from jax.experimental.pallas import tpu as pltpu
from jax.sharding import Mesh
from jax.sharding import PartitionSpec as P


HEADS = 24
HEAD_DIM = 64
D = 1536
FRAMES = 4
COLUMNS = 32
TOKENS = FRAMES * COLUMNS
AGENT_DEV = 4
PLANES = 8
TILES = 8
AGENTS = 256
GROUP_HEADS = HEADS // TILES
GROUP = GROUP_HEADS * HEAD_DIM
K_ROW = GROUP
V_ROW = 2 * GROUP
SENT = 3 * GROUP
PLANE_AGENTS = TILES * AGENT_DEV
EDGE_ROWS = TILES + 2
EDGE = 3 * TOKENS
STATS = 16
GRANT = 6 * 1024 * 1024
ALL = 60 * 1024 * 1024
INV_ROOT = HEAD_DIM ** (-0.5)
F32 = jnp.float32
BF16 = jnp.bfloat16


VMEM = pl.BlockSpec(memory_space=pltpu.VMEM)

SMEM = pl.BlockSpec(memory_space=pltpu.SMEM)
HBM = pl.BlockSpec(memory_space=pltpu.HBM)


def call(kernel, out_shape, us, *args, scalars=(), scratch=(), far=False):
    cost = pl.CostEstimate(flops=int(us * 3.0e8), bytes_accessed=int(us * 2.0e6), transcendentals=0)
    many = isinstance(out_shape, tuple)
    return pl.pallas_call(
        kernel,
        out_shape=out_shape,
        in_specs=[SMEM] * len(scalars) + [HBM if far else VMEM] * len(args),
        out_specs=(VMEM,) * len(out_shape) if many else HBM if far else VMEM,
        scratch_shapes=list(scratch),
        cost_estimate=cost,
        compiler_params=pltpu.CompilerParams(vmem_limit_bytes=ALL if far else GRANT),
    )(*scalars, *args)


def exchange(x, axes):
    return lax.all_to_all(x, axes, 0, 0)


def shift(x, axis, step):
    count = lax.axis_size(axis)
    pairs = [(i, i + step) for i in range(count) if 0 <= i + step < count]
    return lax.ppermute(x, axis, pairs)


def pool_kernel(q_ref, out_ref):
    shape = (8, TOKENS)
    token = lax.broadcasted_iota(jnp.int32, shape, 1)
    agent = lax.broadcasted_iota(jnp.int32, shape, 0)
    width = COLUMNS // AGENT_DEV
    pick = ((token % COLUMNS) // width == agent).astype(F32).astype(BF16)
    sums = jnp.dot(pick, q_ref[...], preferred_element_type=F32)
    pooled = (sums[:AGENT_DEV] * (1.0 / (FRAMES * width))).astype(BF16)
    for tile in range(TILES):
        out_ref[tile] = pooled[:, tile * GROUP : (tile + 1) * GROUP]


def pack_kernel(q_ref, k_ref, v_ref, out_ref, came, turned, in_sems, out_sems):
    refs = (q_ref, k_ref, v_ref)
    loads = [pltpu.make_async_copy(ref, came.at[n], in_sems.at[n]) for n, ref in enumerate(refs)]
    for load in loads:
        load.start()
    stores = []
    for n, load in enumerate(loads):
        load.wait()
        flipped = came[n].T
        for tile in range(TILES):
            turned[n, tile] = flipped[tile * GROUP : (tile + 1) * GROUP]
        rows = pl.ds(n * GROUP, GROUP)
        store = pltpu.make_async_copy(turned.at[n], out_ref.at[:, rows, :], out_sems.at[n])
        store.start()
        stores.append(store)
    for store in stores:
        store.wait()


def rows_of(x_ref, start, size):
    return jnp.concatenate([x_ref[s, start : start + size, :] for s in range(TILES)], axis=1)


def agent_kernel(z_ref, *refs):
    came, (x_ref, out_ref, a_ref) = refs[:PLANES], refs[PLANES:]
    for hop, ref in enumerate(came):
        z = lax.rem(z_ref[0] + PLANES - hop, PLANES)
        a_ref[pl.ds(pl.multiple_of(z * PLANE_AGENTS, PLANE_AGENTS), PLANE_AGENTS), :] = ref[...]
    columns = []
    lane = lax.broadcasted_iota(jnp.int32, (AGENTS, HEAD_DIM), 1)
    stats = jnp.zeros((AGENTS, HEAD_DIM), F32)
    for h in range(GROUP_HEADS):
        keys = rows_of(x_ref, K_ROW + h * HEAD_DIM, HEAD_DIM)
        values = rows_of(x_ref, V_ROW + h * HEAD_DIM, HEAD_DIM)
        agents = a_ref[:, h * HEAD_DIM : (h + 1) * HEAD_DIM]
        scores = jnp.dot(agents, keys, preferred_element_type=F32) * INV_ROOT
        peak = jnp.max(scores, axis=1, keepdims=True)
        weights = jnp.exp(scores - peak)
        total = jnp.sum(weights, axis=1, keepdims=True)
        acc = lax.dot_general(
            weights.astype(BF16), values, (((1,), (1,)), ((), ())), preferred_element_type=F32
        )
        columns.append(acc / total)
        left = peak + jnp.log(total)
        for piece in range(3):
            short = left.astype(BF16).astype(F32)
            left = left - short
            stats = jnp.where(lane == piece * GROUP_HEADS + h, short, stats)
    flipped = jnp.concatenate(columns + [stats], axis=1).T
    part = flipped[: GROUP + STATS].astype(BF16)
    for z in range(PLANES):
        out_ref[z] = part


def query_kernel(a_ref, x_ref, *refs):
    e_refs, total_ref = refs[:GROUP_HEADS], refs[GROUP_HEADS]
    for h in range(GROUP_HEADS):
        queries = rows_of(x_ref, h * HEAD_DIM, HEAD_DIM)
        agents = a_ref[:, h * HEAD_DIM : (h + 1) * HEAD_DIM]
        scores = jnp.dot(agents, queries, preferred_element_type=F32) * INV_ROOT
        weights = jnp.exp(scores - jnp.max(scores, axis=0, keepdims=True))
        total_ref[h : h + 1, :] = jnp.sum(weights, axis=0, keepdims=True)
        e_refs[h][...] = weights.astype(BF16)


def edge_kernel(x_ref, above_ref, below_ref, last_ref, first_ref):
    spot = lax.broadcasted_iota(jnp.int32, (GROUP, TOKENS), 1) // COLUMNS
    for block in range(EDGE // TOKENS):
        last = first = jnp.zeros((GROUP, TOKENS), F32)
        for j in range(FRAMES):
            row = block * FRAMES + j
            if row >= EDGE_ROWS:
                break
            if row == 0:
                cells = above_ref[...]
            elif row == EDGE_ROWS - 1:
                cells = below_ref[...]
            else:
                cells = x_ref[row - 1, V_ROW:, :]
            cells = cells.astype(F32)
            late = cells if j == FRAMES - 1 else pltpu.roll(cells, (j + 1) * COLUMNS, 1)
            early = cells if j == 0 else pltpu.roll(cells, j * COLUMNS, 1)
            last = jnp.where(spot == j, late, last)
            first = jnp.where(spot == j, early, first)
        lanes = slice(block * TOKENS, (block + 1) * TOKENS)
        last_ref[:, lanes] = last.astype(BF16)
        first_ref[:, lanes] = first.astype(BF16)


def conv_kernel(x_ref, above_ref, below_ref, before_ref, after_ref, w_ref, out_ref):
    tall = 16
    lane = lax.broadcasted_iota(jnp.int32, (tall, TOKENS), 1)
    column = lane % COLUMNS
    head, tail = lane < COLUMNS, lane >= TOKENS - COLUMNS

    def turned(cells, by):
        by %= TOKENS
        return cells if by == 0 else pltpu.roll(cells, by, 1)

    def frames_of(r, at):
        if r < 0:
            cells = above_ref[pl.ds(at, tall), :]
        elif r == TILES:
            cells = below_ref[pl.ds(at, tall), :]
        else:
            cells = x_ref[r, pl.ds(V_ROW + at, tall), :]
        cells = cells.astype(F32)
        block, j = divmod(r + 1, FRAMES)
        lanes = slice(block * TOKENS, (block + 1) * TOKENS)
        before = turned(before_ref[pl.ds(at, tall), lanes].astype(F32), -j * COLUMNS)
        after = turned(after_ref[pl.ds(at, tall), lanes].astype(F32), (FRAMES - 1 - j) * COLUMNS)
        return (
            jnp.where(head, before, turned(cells, COLUMNS)),
            cells,
            jnp.where(tail, after, turned(cells, -COLUMNS)),
        )

    def step(i, carry):
        at = pl.multiple_of(i * tall, tall)
        w = w_ref[pl.ds(at, tall), :]
        taps = [jnp.broadcast_to(w[:, n : n + 1], (tall, TOKENS)) for n in range(27)]
        rows = {r: frames_of(r, at) for r in range(-1, 1)}
        for r in range(TILES):
            rows[r + 1] = frames_of(r + 1, at)
            sums = []
            for k in range(3):
                total = None
                for j in range(3):
                    for i3 in range(3):
                        term = rows[r + j - 1][i3] * taps[i3 * 9 + j * 3 + k]
                        total = term if total is None else total + term
                sums.append(total)
            left = jnp.where(column == 0, 0.0, pltpu.roll(sums[0], 1, 1))
            right = jnp.where(column == COLUMNS - 1, 0.0, pltpu.roll(sums[2], TOKENS - 1, 1))
            out_ref[r, pl.ds(at, tall), :] = left + sums[1] + right
        return carry

    lax.fori_loop(0, GROUP // tall, step, 0)


def mix_kernel(parts_ref, *refs):
    e_refs, (total_ref, local_ref, out_ref) = refs[:GROUP_HEADS], refs[GROUP_HEADS:]
    logs = []
    for z in range(PLANES):
        pieces = parts_ref[z, GROUP : GROUP + STATS, :].astype(F32)
        n = GROUP_HEADS
        logs.append(pieces[:n] + pieces[n : 2 * n] + pieces[2 * n : 3 * n])
    peak = logs[0]
    for log in logs[1:]:
        peak = jnp.maximum(peak, log)
    shares = [jnp.exp(log - peak) for log in logs]
    whole = sum(shares[1:], shares[0])
    shares = [share / whole for share in shares]
    for h in range(GROUP_HEADS):
        rows = slice(h * HEAD_DIM, (h + 1) * HEAD_DIM)
        values = None
        for z in range(PLANES):
            term = parts_ref[z, rows, :].astype(F32) * shares[z][h : h + 1]
            values = term if values is None else values + term
        mixed = jnp.dot(values.astype(BF16), e_refs[h][...], preferred_element_type=F32)
        mixed = mixed / total_ref[h : h + 1, :]
        for s in range(TILES):
            cells = mixed[:, s * TOKENS : (s + 1) * TOKENS]
            out_ref[s, rows, :] = (cells + local_ref[s, rows, :]).astype(BF16)


def unpack_kernel(x_ref, out_ref):
    out_ref[...] = x_ref[...].reshape(D, TOKENS).T


def turn(x, axis, step):
    count = lax.axis_size(axis)
    return lax.ppermute(x, axis, [(i, (i + step) % count) for i in range(count)])


def body(queries, key_states, value_states, conv_weight):
    q = queries.reshape(TOKENS, D)
    k = key_states.reshape(TOKENS, D)
    v = value_states.reshape(TOKENS, D)
    shape = jax.ShapeDtypeStruct
    pooled = call(pool_kernel, shape((TILES, AGENT_DEV, GROUP), BF16), 1.0, q)
    packed = call(
        pack_kernel,
        shape((TILES, SENT, TOKENS), BF16),
        3.0,
        q,
        k,
        v,
        scratch=(
            pltpu.VMEM((3, TOKENS, D), BF16),
            pltpu.VMEM((3, TILES, GROUP, TOKENS), BF16),
            pltpu.SemaphoreType.DMA((3,)),
            pltpu.SemaphoreType.DMA((3,)),
        ),
        far=True,
    )
    own = exchange(pooled, "xy").reshape(PLANE_AGENTS, GROUP)
    x = exchange(packed, "xy")
    came = [own] + [turn(own, "z", n) for n in range(1, PLANES)]

    above = shift(x[TILES - 1, V_ROW:], "z", 1)
    below = shift(x[0, V_ROW:], "z", -1)

    part, agents = call(
        agent_kernel,
        (shape((PLANES, GROUP + STATS, AGENTS), BF16), shape((AGENTS, GROUP), BF16)),
        4.0,
        *came,
        x,
        scalars=(lax.axis_index("z").astype(jnp.int32).reshape(1),),
    )
    parts = exchange(part, "z")

    rim = shape((GROUP, EDGE), BF16)
    last, first = call(edge_kernel, (rim, rim), 1.0, x, above, below)
    before = shift(last, "tm", 1)
    after = shift(first, "tm", -1)
    *weights, totals = call(
        query_kernel,
        (
            *(shape((AGENTS, TILES * TOKENS), BF16) for _ in range(GROUP_HEADS)),
            shape((8, TILES * TOKENS), F32),
        ),
        4.0,
        agents,
        x,
    )
    taps = lax.dynamic_index_in_dim(
        conv_weight.reshape(27, TILES, GROUP), lax.axis_index("xy"), 1, keepdims=False
    ).T
    local = call(
        conv_kernel, shape((TILES, GROUP, TOKENS), F32), 6.0, x, above, below, before, after, taps
    )
    mixed = call(
        mix_kernel, shape((TILES, GROUP, TOKENS), BF16), 3.0, parts, *weights, totals, local
    )
    mine = exchange(mixed, "xy")
    out = call(unpack_kernel, shape((TOKENS, D), BF16), 1.0, mine)
    return out.reshape(value_states.shape)


def solution(mesh):
    devices = mesh.devices
    fine = Mesh(devices.reshape(devices.shape[0], PLANES, TILES), ("tm", "z", "xy"))
    spec = P("tm", None, ("z", "xy"), None, None)
    return jax.shard_map(
        body,
        mesh=fine,
        in_specs=(spec, spec, spec, P()),
        out_specs=spec,
        check_vma=False,
    )
```

```python
import jax
import jax.numpy as jnp
from jax import lax
from jax.experimental import pallas as pl
from jax.experimental.pallas import tpu as pltpu
from jax.sharding import Mesh
from jax.sharding import PartitionSpec as P


HEADS = 24
HEAD_DIM = 64
D = 1536
FRAMES = 4
COLUMNS = 32
TOKENS = FRAMES * COLUMNS
AGENT_DEV = 4
PLANES = 8
TILES = 8
AGENTS = 256
GROUP_HEADS = HEADS // TILES
GROUP = GROUP_HEADS * HEAD_DIM
K_ROW = GROUP
V_ROW = 2 * GROUP
SENT = 3 * GROUP
PLANE_AGENTS = TILES * AGENT_DEV
EDGE = TILES * COLUMNS
STATS = 16
GRANT = 6 * 1024 * 1024
ALL = 60 * 1024 * 1024
INV_ROOT = HEAD_DIM ** (-0.5)
F32 = jnp.float32
BF16 = jnp.bfloat16


VMEM = pl.BlockSpec(memory_space=pltpu.VMEM)

SMEM = pl.BlockSpec(memory_space=pltpu.SMEM)
HBM = pl.BlockSpec(memory_space=pltpu.HBM)


def call(kernel, out_shape, us, *args, scalars=(), scratch=(), far=False):
    cost = pl.CostEstimate(flops=int(us * 3.0e8), bytes_accessed=int(us * 2.0e6), transcendentals=0)
    many = isinstance(out_shape, tuple)
    return pl.pallas_call(
        kernel,
        out_shape=out_shape,
        in_specs=[SMEM] * len(scalars) + [HBM if far else VMEM] * len(args),
        out_specs=(VMEM,) * len(out_shape) if many else HBM if far else VMEM,
        scratch_shapes=list(scratch),
        cost_estimate=cost,
        compiler_params=pltpu.CompilerParams(vmem_limit_bytes=ALL if far else GRANT),
    )(*scalars, *args)


def exchange(x, axes):
    return lax.all_to_all(x, axes, 0, 0)


def shift(x, axis, step):
    count = lax.axis_size(axis)
    pairs = [(i, i + step) for i in range(count) if 0 <= i + step < count]
    return lax.ppermute(x, axis, pairs)


def pool_kernel(q_ref, out_ref):
    shape = (8, TOKENS)
    token = lax.broadcasted_iota(jnp.int32, shape, 1)
    agent = lax.broadcasted_iota(jnp.int32, shape, 0)
    width = COLUMNS // AGENT_DEV
    pick = ((token % COLUMNS) // width == agent).astype(F32).astype(BF16)
    sums = jnp.dot(pick, q_ref[...], preferred_element_type=F32)
    pooled = (sums[:AGENT_DEV] * (1.0 / (FRAMES * width))).astype(BF16)
    for tile in range(TILES):
        out_ref[tile] = pooled[:, tile * GROUP : (tile + 1) * GROUP]


def pack_kernel(q_ref, k_ref, v_ref, out_ref, came, turned, in_sems, out_sems):
    refs = (q_ref, k_ref, v_ref)
    loads = [pltpu.make_async_copy(ref, came.at[n], in_sems.at[n]) for n, ref in enumerate(refs)]
    for load in loads:
        load.start()
    stores = []
    for n, load in enumerate(loads):
        load.wait()
        flipped = came[n].T
        for tile in range(TILES):
            turned[n, tile] = flipped[tile * GROUP : (tile + 1) * GROUP]
        rows = pl.ds(n * GROUP, GROUP)
        store = pltpu.make_async_copy(turned.at[n], out_ref.at[:, rows, :], out_sems.at[n])
        store.start()
        stores.append(store)
    for store in stores:
        store.wait()


def rows_of(x_ref, start, size):
    return jnp.concatenate([x_ref[s, start : start + size, :] for s in range(TILES)], axis=1)


def agent_kernel(z_ref, *refs):
    came, (x_ref, out_ref, a_ref) = refs[:PLANES], refs[PLANES:]
    for hop, ref in enumerate(came):
        z = lax.rem(z_ref[0] + PLANES - hop, PLANES)
        a_ref[pl.ds(pl.multiple_of(z * PLANE_AGENTS, PLANE_AGENTS), PLANE_AGENTS), :] = ref[...]
    columns = []
    lane = lax.broadcasted_iota(jnp.int32, (AGENTS, HEAD_DIM), 1)
    stats = jnp.zeros((AGENTS, HEAD_DIM), F32)
    for h in range(GROUP_HEADS):
        keys = rows_of(x_ref, K_ROW + h * HEAD_DIM, HEAD_DIM)
        values = rows_of(x_ref, V_ROW + h * HEAD_DIM, HEAD_DIM)
        agents = a_ref[:, h * HEAD_DIM : (h + 1) * HEAD_DIM]
        scores = jnp.dot(agents, keys, preferred_element_type=F32) * INV_ROOT
        peak = jnp.max(scores, axis=1, keepdims=True)
        weights = jnp.exp(scores - peak)
        total = jnp.sum(weights, axis=1, keepdims=True)
        acc = lax.dot_general(
            weights.astype(BF16), values, (((1,), (1,)), ((), ())), preferred_element_type=F32
        )
        columns.append(acc / total)
        left = peak + jnp.log(total)
        for piece in range(3):
            short = left.astype(BF16).astype(F32)
            left = left - short
            stats = jnp.where(lane == piece * GROUP_HEADS + h, short, stats)
    flipped = jnp.concatenate(columns + [stats], axis=1).T
    part = flipped[: GROUP + STATS].astype(BF16)
    for z in range(PLANES):
        out_ref[z] = part


def query_kernel(a_ref, x_ref, one_ref, rest_ref, total_ref):
    for h in range(GROUP_HEADS):
        queries = rows_of(x_ref, h * HEAD_DIM, HEAD_DIM)
        agents = a_ref[:, h * HEAD_DIM : (h + 1) * HEAD_DIM]
        scores = jnp.dot(agents, queries, preferred_element_type=F32) * INV_ROOT
        weights = jnp.exp(scores - jnp.max(scores, axis=0, keepdims=True))
        total_ref[h : h + 1, :] = jnp.sum(weights, axis=0, keepdims=True)
        if h == 0:
            one_ref[...] = weights.astype(BF16)
        else:
            rest_ref[h - 1] = weights.astype(BF16)


def edge_kernel(x_ref, last_ref, first_ref):
    spot = lax.broadcasted_iota(jnp.int32, (GROUP, TOKENS), 1) // COLUMNS
    for block in range(EDGE // TOKENS):
        last = first = jnp.zeros((GROUP, TOKENS), F32)
        for j in range(FRAMES):
            cells = x_ref[block * FRAMES + j, V_ROW:, :].astype(F32)
            late = cells if j == FRAMES - 1 else pltpu.roll(cells, (j + 1) * COLUMNS, 1)
            early = cells if j == 0 else pltpu.roll(cells, j * COLUMNS, 1)
            last = jnp.where(spot == j, late, last)
            first = jnp.where(spot == j, early, first)
        lanes = slice(block * TOKENS, (block + 1) * TOKENS)
        last_ref[:, lanes] = last.astype(BF16)
        first_ref[:, lanes] = first.astype(BF16)


TALL = 16


def turned(cells, by):
    by %= TOKENS
    return cells if by == 0 else pltpu.roll(cells, by, 1)


def frames_of(r, at, x_ref, before_ref, after_ref):
    lane = lax.broadcasted_iota(jnp.int32, (TALL, TOKENS), 1)
    cells = x_ref[r, pl.ds(V_ROW + at, TALL), :].astype(F32)
    block, j = divmod(r, FRAMES)
    lanes = slice(block * TOKENS, (block + 1) * TOKENS)
    before = turned(before_ref[pl.ds(at, TALL), lanes].astype(F32), -j * COLUMNS)
    after = turned(after_ref[pl.ds(at, TALL), lanes].astype(F32), (FRAMES - 1 - j) * COLUMNS)
    return (
        jnp.where(lane < COLUMNS, before, turned(cells, COLUMNS)),
        cells,
        jnp.where(lane >= TOKENS - COLUMNS, after, turned(cells, -COLUMNS)),
    )


def taps_of(w_ref, at, rows=range(3)):
    w = w_ref[pl.ds(at, TALL), :]
    return {
        (i, j, k): jnp.broadcast_to(w[:, n : n + 1], (TALL, TOKENS))
        for i in range(3)
        for j in rows
        for k in range(3)
        for n in (i * 9 + j * 3 + k,)
    }


def stencil(rows, taps):
    column = lax.broadcasted_iota(jnp.int32, (TALL, TOKENS), 1) % COLUMNS
    sums = []
    for k in range(3):
        total = None
        for j, frames in rows.items():
            for i in range(3):
                term = frames[i] * taps[i, j, k]
                total = term if total is None else total + term
        sums.append(total)
    left = jnp.where(column == 0, 0.0, pltpu.roll(sums[0], 1, 1))
    right = jnp.where(column == COLUMNS - 1, 0.0, pltpu.roll(sums[2], TOKENS - 1, 1))
    return left + sums[1] + right


def rim_kernel(x_ref, before_ref, after_ref, w_ref, up_ref, down_ref):
    def step(n, carry):
        at = pl.multiple_of(n * TALL, TALL)
        for r, j, ref in ((TILES - 1, 0, up_ref), (0, 2, down_ref)):
            frames = frames_of(r, at, x_ref, before_ref, after_ref)
            ref[pl.ds(at, TALL), :] = stencil({j: frames}, taps_of(w_ref, at, (j,))).astype(BF16)
        return carry

    lax.fori_loop(0, GROUP // TALL, step, 0)


def conv_kernel(x_ref, before_ref, after_ref, w_ref, out_ref):
    def step(n, carry):
        at = pl.multiple_of(n * TALL, TALL)
        taps = taps_of(w_ref, at)
        rows = {0: frames_of(0, at, x_ref, before_ref, after_ref)}
        for r in range(TILES):
            if r + 1 < TILES:
                rows[r + 1] = frames_of(r + 1, at, x_ref, before_ref, after_ref)
            near = {j: rows[r + j - 1] for j in range(3) if r + j - 1 in rows}
            out_ref[r, pl.ds(at, TALL), :] = stencil(near, taps)
            rows.pop(r - 1, None)
        return carry

    lax.fori_loop(0, GROUP // TALL, step, 0)


def mix_kernel(parts_ref, one_ref, rest_ref, total_ref, local_ref, up_ref, down_ref, out_ref):
    logs = []
    for z in range(PLANES):
        pieces = parts_ref[z, GROUP : GROUP + STATS, :].astype(F32)
        n = GROUP_HEADS
        logs.append(pieces[:n] + pieces[n : 2 * n] + pieces[2 * n : 3 * n])
    peak = logs[0]
    for log in logs[1:]:
        peak = jnp.maximum(peak, log)
    shares = [jnp.exp(log - peak) for log in logs]
    whole = sum(shares[1:], shares[0])
    shares = [share / whole for share in shares]
    for h in range(GROUP_HEADS):
        rows = slice(h * HEAD_DIM, (h + 1) * HEAD_DIM)
        values = None
        for z in range(PLANES):
            term = parts_ref[z, rows, :].astype(F32) * shares[z][h : h + 1]
            values = term if values is None else values + term
        weights = one_ref[...] if h == 0 else rest_ref[h - 1]
        mixed = jnp.dot(values.astype(BF16), weights, preferred_element_type=F32)
        mixed = mixed / total_ref[h : h + 1, :]
        for s in range(TILES):
            cells = mixed[:, s * TOKENS : (s + 1) * TOKENS] + local_ref[s, rows, :]
            if s == 0:
                cells += up_ref[rows, :].astype(F32)
            if s == TILES - 1:
                cells += down_ref[rows, :].astype(F32)
            out_ref[s, rows, :] = cells.astype(BF16)


def unpack_kernel(x_ref, out_ref):
    out_ref[...] = x_ref[...].reshape(D, TOKENS).T


def turn(x, axis, step):
    count = lax.axis_size(axis)
    return lax.ppermute(x, axis, [(i, (i + step) % count) for i in range(count)])


def body(queries, key_states, value_states, conv_weight):
    q = queries.reshape(TOKENS, D)
    k = key_states.reshape(TOKENS, D)
    v = value_states.reshape(TOKENS, D)
    shape = jax.ShapeDtypeStruct
    pooled = call(pool_kernel, shape((TILES, AGENT_DEV, GROUP), BF16), 1.0, q)
    packed = call(
        pack_kernel,
        shape((TILES, SENT, TOKENS), BF16),
        3.0,
        q,
        k,
        v,
        scratch=(
            pltpu.VMEM((3, TOKENS, D), BF16),
            pltpu.VMEM((3, TILES, GROUP, TOKENS), BF16),
            pltpu.SemaphoreType.DMA((3,)),
            pltpu.SemaphoreType.DMA((3,)),
        ),
        far=True,
    )
    own = exchange(pooled, "xy").reshape(PLANE_AGENTS, GROUP)
    x = exchange(packed, "xy")
    came = [own] + [turn(own, "z", n) for n in range(1, PLANES)]

    part, agents = call(
        agent_kernel,
        (shape((PLANES, GROUP + STATS, AGENTS), BF16), shape((AGENTS, GROUP), BF16)),
        4.0,
        *came,
        x,
        scalars=(lax.axis_index("z").astype(jnp.int32).reshape(1),),
    )
    parts = exchange(part, "z")

    edges = shape((GROUP, EDGE), BF16)
    last, first = call(edge_kernel, (edges, edges), 1.0, x)
    before = shift(last, "tm", 1)
    after = shift(first, "tm", -1)
    cells = TILES * TOKENS
    one, rest, totals = call(
        query_kernel,
        (
            shape((AGENTS, cells), BF16),
            shape((GROUP_HEADS - 1, AGENTS, cells), BF16),
            shape((8, cells), F32),
        ),
        2.0,
        agents,
        x,
    )
    taps = lax.dynamic_index_in_dim(
        conv_weight.reshape(27, TILES, GROUP), lax.axis_index("xy"), 1, keepdims=False
    ).T
    row = shape((GROUP, TOKENS), BF16)
    to_next, to_last = call(rim_kernel, (row, row), 1.0, x, before, after, taps)
    up = shift(to_next, "z", 1)
    down = shift(to_last, "z", -1)
    local = call(conv_kernel, shape((TILES, GROUP, TOKENS), F32), 5.0, x, before, after, taps)
    mixed = call(
        mix_kernel,
        shape((TILES, GROUP, TOKENS), BF16),
        1.0,
        parts,
        one,
        rest,
        totals,
        local,
        up,
        down,
    )
    mine = exchange(mixed, "xy")
    out = call(unpack_kernel, shape((TOKENS, D), BF16), 1.0, mine)
    return out.reshape(value_states.shape)


def solution(mesh):
    devices = mesh.devices
    fine = Mesh(devices.reshape(devices.shape[0], PLANES, TILES), ("tm", "z", "xy"))
    spec = P("tm", None, ("z", "xy"), None, None)
    return jax.shard_map(
        body,
        mesh=fine,
        in_specs=(spec, spec, spec, P()),
        out_specs=spec,
        check_vma=False,
    )
```

```python
import jax
import jax.numpy as jnp
from jax import lax
from jax.experimental import pallas as pl
from jax.experimental.pallas import tpu as pltpu
from jax.sharding import Mesh
from jax.sharding import PartitionSpec as P


HEADS = 24
HEAD_DIM = 64
D = 1536
FRAMES = 4
COLUMNS = 32
TOKENS = FRAMES * COLUMNS
AGENT_DEV = 4
PAIRS = 4
PLANES = 2 * PAIRS
TILES = 8
AGENTS = 256
GROUP_HEADS = HEADS // TILES
GROUP = GROUP_HEADS * HEAD_DIM
K_ROW = GROUP
V_ROW = 2 * GROUP
SENT = 3 * GROUP
PAIR_AGENTS = 2 * TILES * AGENT_DEV
EDGE = TILES * COLUMNS
STATS = 16
GRANT = 6 * 1024 * 1024
ALL = 60 * 1024 * 1024
INV_ROOT = HEAD_DIM ** (-0.5)
F32 = jnp.float32
BF16 = jnp.bfloat16


VMEM = pl.BlockSpec(memory_space=pltpu.VMEM)

SMEM = pl.BlockSpec(memory_space=pltpu.SMEM)
HBM = pl.BlockSpec(memory_space=pltpu.HBM)


def call(kernel, out_shape, us, *args, scalars=(), scratch=(), far=False):
    cost = pl.CostEstimate(flops=int(us * 3.0e8), bytes_accessed=int(us * 2.0e6), transcendentals=0)
    many = isinstance(out_shape, tuple)
    return pl.pallas_call(
        kernel,
        out_shape=out_shape,
        in_specs=[SMEM] * len(scalars) + [HBM if far else VMEM] * len(args),
        out_specs=(VMEM,) * len(out_shape) if many else HBM if far else VMEM,
        scratch_shapes=list(scratch),
        cost_estimate=cost,
        compiler_params=pltpu.CompilerParams(vmem_limit_bytes=ALL if far else GRANT),
    )(*scalars, *args)


def exchange(x, axes):
    return lax.all_to_all(x, axes, 0, 0)


def shift(x, axis, step):
    count = PLANES
    pairs = [(i, i + step) for i in range(count) if 0 <= i + step < count]
    return lax.ppermute(x, axis, pairs)


def pool_kernel(q_ref, out_ref):
    shape = (8, TOKENS)
    token = lax.broadcasted_iota(jnp.int32, shape, 1)
    agent = lax.broadcasted_iota(jnp.int32, shape, 0)
    width = COLUMNS // AGENT_DEV
    pick = ((token % COLUMNS) // width == agent).astype(F32).astype(BF16)
    sums = jnp.dot(pick, q_ref[...], preferred_element_type=F32)
    pooled = (sums[:AGENT_DEV] * (1.0 / (FRAMES * width))).astype(BF16)
    for tile in range(TILES):
        part = pooled[:, tile * GROUP : (tile + 1) * GROUP]
        out_ref[tile] = part
        out_ref[TILES + tile] = part


def pack_kernel(q_ref, k_ref, v_ref, out_ref, came, turned, in_sems, out_sems):
    refs = (q_ref, k_ref, v_ref)
    loads = [pltpu.make_async_copy(ref, came.at[n], in_sems.at[n]) for n, ref in enumerate(refs)]
    for load in loads:
        load.start()
    stores = []
    for n, load in enumerate(loads):
        load.wait()
        flipped = came[n].T
        for tile in range(TILES):
            turned[n, tile] = flipped[tile * GROUP : (tile + 1) * GROUP]
        rows = pl.ds(n * GROUP, GROUP)
        store = pltpu.make_async_copy(turned.at[n], out_ref.at[:, rows, :], out_sems.at[n])
        store.start()
        stores.append(store)
    for store in stores:
        store.wait()


def rows_of(x_ref, start, size):
    return jnp.concatenate([x_ref[s, start : start + size, :] for s in range(TILES)], axis=1)


def agent_kernel(z_ref, *refs):
    came, (x_ref, out_ref, a_ref) = refs[:PAIRS], refs[PAIRS:]
    for hop, ref in enumerate(came):
        z = lax.rem(z_ref[0] + PAIRS - hop, PAIRS)
        a_ref[pl.ds(pl.multiple_of(z * PAIR_AGENTS, PAIR_AGENTS), PAIR_AGENTS), :] = ref[...]
    columns = []
    lane = lax.broadcasted_iota(jnp.int32, (AGENTS, HEAD_DIM), 1)
    stats = jnp.zeros((AGENTS, HEAD_DIM), F32)
    for h in range(GROUP_HEADS):
        keys = rows_of(x_ref, K_ROW + h * HEAD_DIM, HEAD_DIM)
        values = rows_of(x_ref, V_ROW + h * HEAD_DIM, HEAD_DIM)
        agents = a_ref[:, h * HEAD_DIM : (h + 1) * HEAD_DIM]
        scores = jnp.dot(agents, keys, preferred_element_type=F32) * INV_ROOT
        peak = jnp.max(scores, axis=1, keepdims=True)
        weights = jnp.exp(scores - peak)
        total = jnp.sum(weights, axis=1, keepdims=True)
        acc = lax.dot_general(
            weights.astype(BF16), values, (((1,), (1,)), ((), ())), preferred_element_type=F32
        )
        columns.append(acc / total)
        left = peak + jnp.log(total)
        for piece in range(3):
            short = left.astype(BF16).astype(F32)
            left = left - short
            stats = jnp.where(lane == piece * GROUP_HEADS + h, short, stats)
    flipped = jnp.concatenate(columns + [stats], axis=1).T
    part = flipped[: GROUP + STATS].astype(BF16)
    for z in range(PLANES):
        out_ref[z] = part


def query_kernel(a_ref, x_ref, one_ref, rest_ref, total_ref):
    for h in range(GROUP_HEADS):
        queries = rows_of(x_ref, h * HEAD_DIM, HEAD_DIM)
        agents = a_ref[:, h * HEAD_DIM : (h + 1) * HEAD_DIM]
        scores = jnp.dot(agents, queries, preferred_element_type=F32) * INV_ROOT
        weights = jnp.exp(scores - jnp.max(scores, axis=0, keepdims=True))
        total_ref[h : h + 1, :] = jnp.sum(weights, axis=0, keepdims=True)
        if h == 0:
            one_ref[...] = weights.astype(BF16)
        else:
            rest_ref[h - 1] = weights.astype(BF16)


def taps_kernel(tile_ref, w_ref, out_ref):
    for tile in range(TILES):

        @pl.when(tile_ref[0] == tile)
        def _(tile=tile):
            lanes = slice(tile * GROUP, (tile + 1) * GROUP)
            rows = [w_ref[i, j, :, lanes] for i in range(3) for j in range(3)]
            rows.append(jnp.zeros((5, GROUP), F32))
            out_ref[...] = jnp.concatenate(rows, axis=0).T


def edge_kernel(even_ref, x_ref, near_ref, far_ref):
    spot = lax.broadcasted_iota(jnp.int32, (GROUP, TOKENS), 1) // COLUMNS
    for block in range(EDGE // TOKENS):
        last = first = jnp.zeros((GROUP, TOKENS), F32)
        for j in range(FRAMES):
            cells = x_ref[block * FRAMES + j, V_ROW:, :].astype(F32)
            late = cells if j == FRAMES - 1 else pltpu.roll(cells, (j + 1) * COLUMNS, 1)
            early = cells if j == 0 else pltpu.roll(cells, j * COLUMNS, 1)
            last = jnp.where(spot == j, late, last)
            first = jnp.where(spot == j, early, first)
        lanes = slice(block * TOKENS, (block + 1) * TOKENS)
        last, first = last.astype(BF16), first.astype(BF16)

        @pl.when(even_ref[0] == 1)
        def _(last=last, first=first, lanes=lanes):
            near_ref[:, lanes] = last
            far_ref[:, lanes] = first

        @pl.when(even_ref[0] != 1)
        def _(last=last, first=first, lanes=lanes):
            near_ref[:, lanes] = first
            far_ref[:, lanes] = last


TALL = 16


def turned(cells, by):
    by %= TOKENS
    return cells if by == 0 else pltpu.roll(cells, by, 1)


def frames_of(r, at, even, x_ref, near_ref, far_ref):
    lane = lax.broadcasted_iota(jnp.int32, (TALL, TOKENS), 1)
    cells = x_ref[r, pl.ds(V_ROW + at, TALL), :].astype(F32)
    block, j = divmod(r, FRAMES)
    lanes = slice(block * TOKENS, (block + 1) * TOKENS)
    near = near_ref[pl.ds(at, TALL), lanes].astype(F32)
    far = far_ref[pl.ds(at, TALL), lanes].astype(F32)
    before = turned(jnp.where(even, far, near), -j * COLUMNS)
    after = turned(jnp.where(even, near, far), (FRAMES - 1 - j) * COLUMNS)
    return (
        jnp.where(lane < COLUMNS, before, turned(cells, COLUMNS)),
        cells,
        jnp.where(lane >= TOKENS - COLUMNS, after, turned(cells, -COLUMNS)),
    )


def taps_of(w_ref, at, rows=range(3)):
    w = w_ref[pl.ds(at, TALL), :]
    return {
        (i, j, k): jnp.broadcast_to(w[:, n : n + 1], (TALL, TOKENS))
        for i in range(3)
        for j in rows
        for k in range(3)
        for n in (i * 9 + j * 3 + k,)
    }


def stencil(rows, taps):
    column = lax.broadcasted_iota(jnp.int32, (TALL, TOKENS), 1) % COLUMNS
    sums = []
    for k in range(3):
        total = None
        for j, frames in rows.items():
            for i in range(3):
                term = frames[i] * taps[i, j, k]
                total = term if total is None else total + term
        sums.append(total)
    left = jnp.where(column == 0, 0.0, pltpu.roll(sums[0], 1, 1))
    right = jnp.where(column == COLUMNS - 1, 0.0, pltpu.roll(sums[2], TOKENS - 1, 1))
    return left + sums[1] + right


def rim_kernel(even_ref, x_ref, near_ref, far_ref, w_ref, up_ref, down_ref):
    even = even_ref[0] == 1
    for at in range(0, GROUP, TALL):
        for r, j, ref in ((TILES - 1, 0, up_ref), (0, 2, down_ref)):
            frames = frames_of(r, at, even, x_ref, near_ref, far_ref)
            ref[pl.ds(at, TALL), :] = stencil({j: frames}, taps_of(w_ref, at, (j,))).astype(BF16)


def conv_kernel(even_ref, x_ref, near_ref, far_ref, w_ref, out_ref):
    even = even_ref[0] == 1

    def step(n, carry):
        at = pl.multiple_of(n * TALL, TALL)
        taps = taps_of(w_ref, at)
        rows = {0: frames_of(0, at, even, x_ref, near_ref, far_ref)}
        for r in range(TILES):
            if r + 1 < TILES:
                rows[r + 1] = frames_of(r + 1, at, even, x_ref, near_ref, far_ref)
            near = {j: rows[r + j - 1] for j in range(3) if r + j - 1 in rows}
            out_ref[r, pl.ds(at, TALL), :] = stencil(near, taps)
            rows.pop(r - 1, None)
        return carry

    lax.fori_loop(0, GROUP // TALL, step, 0)


def mix_kernel(parts_ref, one_ref, rest_ref, total_ref, local_ref, up_ref, down_ref, out_ref):
    logs = []
    for z in range(PLANES):
        pieces = parts_ref[z, GROUP : GROUP + STATS, :].astype(F32)
        n = GROUP_HEADS
        logs.append(pieces[:n] + pieces[n : 2 * n] + pieces[2 * n : 3 * n])
    peak = logs[0]
    for log in logs[1:]:
        peak = jnp.maximum(peak, log)
    shares = [jnp.exp(log - peak) for log in logs]
    whole = sum(shares[1:], shares[0])
    shares = [share / whole for share in shares]
    for h in range(GROUP_HEADS):
        rows = slice(h * HEAD_DIM, (h + 1) * HEAD_DIM)
        values = None
        for z in range(PLANES):
            term = parts_ref[z, rows, :].astype(F32) * shares[z][h : h + 1]
            values = term if values is None else values + term
        weights = one_ref[...] if h == 0 else rest_ref[h - 1]
        mixed = jnp.dot(values.astype(BF16), weights, preferred_element_type=F32)
        mixed = mixed / total_ref[h : h + 1, :]
        for s in range(TILES):
            cells = mixed[:, s * TOKENS : (s + 1) * TOKENS] + local_ref[s, rows, :]
            if s == 0:
                cells += up_ref[rows, :].astype(F32)
            if s == TILES - 1:
                cells += down_ref[rows, :].astype(F32)
            out_ref[s, rows, :] = cells.astype(BF16)


def unpack_kernel(x_ref, out_ref):
    out_ref[...] = x_ref[...].reshape(D, TOKENS).T


def scalar(x):
    return x.astype(jnp.int32).reshape(1)


def body(queries, key_states, value_states, conv_weight):
    q = queries.reshape(TOKENS, D)
    k = key_states.reshape(TOKENS, D)
    v = value_states.reshape(TOKENS, D)
    shape = jax.ShapeDtypeStruct
    pooled = call(pool_kernel, shape((2 * TILES, AGENT_DEV, GROUP), BF16), 1.0, q)
    packed = call(
        pack_kernel,
        shape((TILES, SENT, TOKENS), BF16),
        3.0,
        q,
        k,
        v,
        scratch=(
            pltpu.VMEM((3, TOKENS, D), BF16),
            pltpu.VMEM((3, TILES, GROUP, TOKENS), BF16),
            pltpu.SemaphoreType.DMA((3,)),
            pltpu.SemaphoreType.DMA((3,)),
        ),
        far=True,
    )
    own = exchange(pooled, ("zl", "xy")).reshape(PAIR_AGENTS, GROUP)
    x = exchange(packed, "xy")
    came = [own]
    for n in range(1, PAIRS):
        came.append(lax.ppermute(own, "zh", [(i, (i + n) % PAIRS) for i in range(PAIRS)]))
    tile = scalar(lax.axis_index("xy"))
    taps = call(taps_kernel, shape((GROUP, 32), F32), 1.0, conv_weight, scalars=(tile,))

    part, agents = call(
        agent_kernel,
        (shape((PLANES, GROUP + STATS, AGENTS), BF16), shape((AGENTS, GROUP), BF16)),
        4.0,
        *came,
        x,
        scalars=(scalar(lax.axis_index("zh")),),
    )
    parts = exchange(part, ("zh", "zl"))

    edges = shape((GROUP, EDGE), BF16)
    even = scalar(1 - lax.axis_index("tm") % 2)
    near, far = call(edge_kernel, (edges, edges), 1.0, x, scalars=(even,))
    groups = lax.axis_size("tm")
    pairs = [(i, i + 1) for i in range(0, groups - 1, 2)]
    near = lax.ppermute(near, "tm", pairs + [(b, a) for a, b in pairs])
    pairs = [(i, i + 1) for i in range(1, groups - 1, 2)]
    far = lax.ppermute(far, "tm", pairs + [(b, a) for a, b in pairs])
    cells = TILES * TOKENS
    one, rest, totals = call(
        query_kernel,
        (
            shape((AGENTS, cells), BF16),
            shape((GROUP_HEADS - 1, AGENTS, cells), BF16),
            shape((8, cells), F32),
        ),
        2.0,
        agents,
        x,
    )
    row = shape((GROUP, TOKENS), BF16)
    to_next, to_last = call(rim_kernel, (row, row), 1.0, x, near, far, taps, scalars=(even,))
    up = shift(to_next, ("zh", "zl"), 1)
    down = shift(to_last, ("zh", "zl"), -1)
    local = call(
        conv_kernel, shape((TILES, GROUP, TOKENS), F32), 5.0, x, near, far, taps, scalars=(even,)
    )
    mixed = call(
        mix_kernel,
        shape((TILES, GROUP, TOKENS), BF16),
        1.0,
        parts,
        one,
        rest,
        totals,
        local,
        up,
        down,
    )
    mine = exchange(mixed, "xy")
    out = call(unpack_kernel, shape((TOKENS, D), BF16), 1.0, mine)
    return out.reshape(value_states.shape)


def solution(mesh):
    devices = mesh.devices
    fine = Mesh(devices.reshape(devices.shape[0], PAIRS, 2, TILES), ("tm", "zh", "zl", "xy"))
    spec = P("tm", None, ("zh", "zl", "xy"), None, None)
    return jax.shard_map(
        body,
        mesh=fine,
        in_specs=(spec, spec, spec, P()),
        out_specs=spec,
        check_vma=False,
    )
```

```python
import jax
import jax.numpy as jnp
from jax import lax
from jax.experimental import pallas as pl
from jax.experimental.pallas import tpu as pltpu
from jax.sharding import Mesh
from jax.sharding import PartitionSpec as P


HEADS = 24
HEAD_DIM = 64
D = 1536
FRAMES = 4
COLUMNS = 32
TOKENS = FRAMES * COLUMNS
AGENT_DEV = 4
PLANES = 8
TILES = 8
AGENTS = 256
OWNED = AGENTS // PLANES
SLOT = 8
GROUP_HEADS = HEADS // TILES
GROUP = GROUP_HEADS * HEAD_DIM
K_ROW = GROUP
V_ROW = 2 * GROUP
SENT = 3 * GROUP
EDGE_ROWS = TILES + 2
EDGE = 3 * TOKENS
PART = 256
GRANT = 6 * 1024 * 1024
ALL = 60 * 1024 * 1024
INV_ROOT = HEAD_DIM ** (-0.5)
F32 = jnp.float32
BF16 = jnp.bfloat16


VMEM = pl.BlockSpec(memory_space=pltpu.VMEM)

SMEM = pl.BlockSpec(memory_space=pltpu.SMEM)
HBM = pl.BlockSpec(memory_space=pltpu.HBM)


def call(kernel, out_shape, us, *args, scalars=(), scratch=(), far=None):
    cost = pl.CostEstimate(flops=int(us * 3.0e8), bytes_accessed=int(us * 2.0e6), transcendentals=0)
    outs = out_shape if isinstance(out_shape, tuple) else (out_shape,)
    out_specs = tuple(HBM if n == far else VMEM for n in range(len(outs)))
    return pl.pallas_call(
        kernel,
        out_shape=out_shape,
        in_specs=[SMEM] * len(scalars) + [VMEM if far is None else HBM] * len(args),
        out_specs=out_specs if isinstance(out_shape, tuple) else out_specs[0],
        scratch_shapes=list(scratch),
        cost_estimate=cost,
        compiler_params=pltpu.CompilerParams(vmem_limit_bytes=GRANT if far is None else ALL),
    )(*scalars, *args)


def exchange(x, axes):
    return lax.all_to_all(x, axes, 0, 0)


def shift(x, axis, step):
    count = PLANES
    pairs = [(i, i + step) for i in range(count) if 0 <= i + step < count]
    return lax.ppermute(x, axis, pairs)


def pack_kernel(q_ref, k_ref, v_ref, out_ref, pooled_ref, came, turned, in_sems, out_sems):
    refs = (q_ref, k_ref, v_ref)
    loads = [pltpu.make_async_copy(ref, came.at[n], in_sems.at[n]) for n, ref in enumerate(refs)]
    for load in loads:
        load.start()
    stores = []
    for n, load in enumerate(loads):
        load.wait()
        flipped = came[n].T
        for tile in range(TILES):
            turned[n, tile] = flipped[tile * GROUP : (tile + 1) * GROUP]
        rows = pl.ds(n * GROUP, GROUP)
        store = pltpu.make_async_copy(turned.at[n], out_ref.at[:, rows, :], out_sems.at[n])
        store.start()
        stores.append(store)
    shape = (SLOT, TOKENS)
    token = lax.broadcasted_iota(jnp.int32, shape, 1)
    agent = lax.broadcasted_iota(jnp.int32, shape, 0)
    width = COLUMNS // AGENT_DEV
    pick = ((token % COLUMNS) // width == agent).astype(F32).astype(BF16)
    sums = jnp.dot(pick, came[0], preferred_element_type=F32)
    pooled_ref[...] = (sums * (1.0 / (FRAMES * width))).astype(BF16)
    for store in stores:
        store.wait()


def route_kernel(z_ref, *refs):
    came, out_ref = refs[:PLANES], refs[PLANES]
    rows = jnp.concatenate([ref[...].astype(F32) for ref in came], axis=0).astype(BF16)
    shape = (OWNED, PLANES * SLOT)
    to = lax.broadcasted_iota(jnp.int32, shape, 0)
    at = lax.broadcasted_iota(jnp.int32, shape, 1)
    hop = (z_ref[0] + PLANES - to // AGENT_DEV) % PLANES
    pick = (at == hop * SLOT + to % AGENT_DEV).astype(F32).astype(BF16)
    agents = jnp.dot(pick, rows, preferred_element_type=F32).astype(BF16)
    for tile in range(TILES):
        out_ref[tile] = agents[:, tile * GROUP : (tile + 1) * GROUP]


def rows_of(x_ref, start, size):
    return jnp.concatenate([x_ref[s, start : start + size, :] for s in range(TILES)], axis=1)


def agent_kernel(a_ref, x_ref, out_ref):
    agents = a_ref[...].reshape(AGENTS, GROUP)
    columns = []
    lane = lax.broadcasted_iota(jnp.int32, (AGENTS, HEAD_DIM), 1)
    stats = jnp.zeros((AGENTS, HEAD_DIM), F32)
    for h in range(GROUP_HEADS):
        keys = rows_of(x_ref, K_ROW + h * HEAD_DIM, HEAD_DIM)
        values = rows_of(x_ref, V_ROW + h * HEAD_DIM, HEAD_DIM)
        head = agents[:, h * HEAD_DIM : (h + 1) * HEAD_DIM]
        scores = jnp.dot(head, keys, preferred_element_type=F32) * INV_ROOT
        peak = jnp.max(scores, axis=1, keepdims=True)
        weights = jnp.exp(scores - peak)
        total = jnp.sum(weights, axis=1, keepdims=True)
        acc = lax.dot_general(
            weights.astype(BF16), values, (((1,), (1,)), ((), ())), preferred_element_type=F32
        )
        columns.append(acc / total)
        left = peak + jnp.log(total)
        for piece in range(3):
            short = left.astype(BF16).astype(F32)
            left = left - short
            stats = jnp.where(lane == piece * GROUP_HEADS + h, short, stats)
    part = jnp.concatenate(columns + [stats], axis=1).astype(BF16)
    out_ref[...] = part.reshape(PLANES, OWNED, PART)


def comb_kernel(parts_ref, out_ref):
    logs = []
    for z in range(PLANES):
        pieces = parts_ref[z, :, PART - TOKENS :].astype(F32)
        n = GROUP_HEADS
        logs.append(pieces + turned(pieces, -n) + turned(pieces, -2 * n))
    peak = logs[0]
    for log in logs[1:]:
        peak = jnp.maximum(peak, log)
    shares = [jnp.exp(log - peak) for log in logs]
    whole = sum(shares[1:], shares[0])
    shares = [share / whole for share in shares]
    columns = []
    for h in range(GROUP_HEADS):
        lanes = slice(h * HEAD_DIM, (h + 1) * HEAD_DIM)
        at = GROUP + h - (PART - TOKENS)
        values = None
        for z in range(PLANES):
            term = parts_ref[z, :, lanes].astype(F32) * shares[z][:, at : at + 1]
            values = term if values is None else values + term
        columns.append(values)
    owned = jnp.concatenate(columns, axis=1).astype(BF16)
    for z in range(PLANES):
        out_ref[z] = owned


def taps_kernel(tile_ref, w_ref, out_ref):
    for tile in range(TILES):

        @pl.when(tile_ref[0] == tile)
        def _(tile=tile):
            lanes = slice(tile * GROUP, (tile + 1) * GROUP)
            rows = [w_ref[i, j, :, lanes] for i in range(3) for j in range(3)]
            rows.append(jnp.zeros((5, GROUP), F32))
            out_ref[...] = jnp.concatenate(rows, axis=0).T


def edge_kernel(even_ref, x_ref, above_ref, below_ref, near_ref, far_ref):
    even = even_ref[0] == 1
    spot = lax.broadcasted_iota(jnp.int32, (GROUP, TOKENS), 1) // COLUMNS
    for block in range(EDGE // TOKENS):
        last = first = jnp.zeros((GROUP, TOKENS), F32)
        for j in range(FRAMES):
            row = block * FRAMES + j
            if row >= EDGE_ROWS:
                break
            if row == 0:
                cells = above_ref[...]
            elif row == EDGE_ROWS - 1:
                cells = below_ref[...]
            else:
                cells = x_ref[row - 1, V_ROW:, :]
            cells = cells.astype(F32)
            last = jnp.where(spot == j, turned(cells, (j + 1) * COLUMNS), last)
            first = jnp.where(spot == j, turned(cells, j * COLUMNS), first)
        lanes = slice(block * TOKENS, (block + 1) * TOKENS)
        near_ref[:, lanes] = jnp.where(even, last, first).astype(BF16)
        far_ref[:, lanes] = jnp.where(even, first, last).astype(BF16)


TALL = 16


def turned(cells, by):
    by %= TOKENS
    return cells if by == 0 else pltpu.roll(cells, by, 1)


def frames_of(r, at, even, x_ref, above_ref, below_ref, near_ref, far_ref):
    lane = lax.broadcasted_iota(jnp.int32, (TALL, TOKENS), 1)
    if r < 0:
        cells = above_ref[pl.ds(at, TALL), :]
    elif r == TILES:
        cells = below_ref[pl.ds(at, TALL), :]
    else:
        cells = x_ref[r, pl.ds(V_ROW + at, TALL), :]
    cells = cells.astype(F32)
    block, j = divmod(r + 1, FRAMES)
    lanes = slice(block * TOKENS, (block + 1) * TOKENS)
    near = near_ref[pl.ds(at, TALL), lanes].astype(F32)
    far = far_ref[pl.ds(at, TALL), lanes].astype(F32)
    before = turned(jnp.where(even, far, near), -j * COLUMNS)
    after = turned(jnp.where(even, near, far), (FRAMES - 1 - j) * COLUMNS)
    return (
        jnp.where(lane < COLUMNS, before, turned(cells, COLUMNS)),
        cells,
        jnp.where(lane >= TOKENS - COLUMNS, after, turned(cells, -COLUMNS)),
    )


def taps_of(w_ref, at, rows=range(3)):
    w = w_ref[pl.ds(at, TALL), :]
    return {
        (i, j, k): jnp.broadcast_to(w[:, n : n + 1], (TALL, TOKENS))
        for i in range(3)
        for j in rows
        for k in range(3)
        for n in (i * 9 + j * 3 + k,)
    }


def stencil(rows, taps):
    column = lax.broadcasted_iota(jnp.int32, (TALL, TOKENS), 1) % COLUMNS
    sums = []
    for k in range(3):
        total = None
        for j, frames in rows.items():
            for i in range(3):
                term = frames[i] * taps[i, j, k]
                total = term if total is None else total + term
        sums.append(total)
    left = jnp.where(column == 0, 0.0, pltpu.roll(sums[0], 1, 1))
    right = jnp.where(column == COLUMNS - 1, 0.0, pltpu.roll(sums[2], TOKENS - 1, 1))
    return left + sums[1] + right


def conv_kernel(even_ref, x_ref, above_ref, below_ref, near_ref, far_ref, w_ref, out_ref):
    even = even_ref[0] == 1
    refs = (x_ref, above_ref, below_ref, near_ref, far_ref)

    def step(n, carry):
        at = pl.multiple_of(n * TALL, TALL)
        taps = taps_of(w_ref, at)
        rows = {r: frames_of(r, at, even, *refs) for r in range(-1, 1)}
        for r in range(TILES):
            rows[r + 1] = frames_of(r + 1, at, even, *refs)
            out_ref[r, pl.ds(at, TALL), :] = stencil({j: rows[r + j - 1] for j in range(3)}, taps)
            rows.pop(r - 1)
        return carry

    lax.fori_loop(0, GROUP // TALL, step, 0)


def mix_kernel(a_ref, values_ref, x_ref, local_ref, out_ref):
    agents = a_ref[...].reshape(AGENTS, GROUP)
    values = values_ref[...].reshape(AGENTS, GROUP).T
    for h in range(GROUP_HEADS):
        rows = slice(h * HEAD_DIM, (h + 1) * HEAD_DIM)
        queries = rows_of(x_ref, h * HEAD_DIM, HEAD_DIM)
        scores = jnp.dot(agents[:, rows], queries, preferred_element_type=F32) * INV_ROOT
        weights = jnp.exp(scores - jnp.max(scores, axis=0, keepdims=True))
        total = jnp.sum(weights, axis=0, keepdims=True)
        mixed = jnp.dot(values[rows], weights.astype(BF16), preferred_element_type=F32) / total
        for s in range(TILES):
            cells = mixed[:, s * TOKENS : (s + 1) * TOKENS] + local_ref[s, rows, :]
            out_ref[s, rows, :] = cells.astype(BF16)


def unpack_kernel(x_ref, out_ref):
    out_ref[...] = x_ref[...].reshape(D, TOKENS).T


def scalar(x):
    return x.astype(jnp.int32).reshape(1)


def body(queries, key_states, value_states, conv_weight):
    q = queries.reshape(TOKENS, D)
    k = key_states.reshape(TOKENS, D)
    v = value_states.reshape(TOKENS, D)
    shape = jax.ShapeDtypeStruct
    packed, pooled = call(
        pack_kernel,
        (shape((TILES, SENT, TOKENS), BF16), shape((SLOT, D), BF16)),
        3.0,
        q,
        k,
        v,
        scratch=(
            pltpu.VMEM((3, TOKENS, D), BF16),
            pltpu.VMEM((3, TILES, GROUP, TOKENS), BF16),
            pltpu.SemaphoreType.DMA((3,)),
            pltpu.SemaphoreType.DMA((3,)),
        ),
        far=0,
    )
    x = exchange(packed, "xy")
    came = [pooled]
    for n in range(1, PLANES):
        came.append(lax.ppermute(pooled, "z", [(i, (i + n) % PLANES) for i in range(PLANES)]))
    tile = scalar(lax.axis_index("xy"))
    taps = call(taps_kernel, shape((GROUP, 32), F32), 1.0, conv_weight, scalars=(tile,))
    z = scalar(lax.axis_index("z"))
    by_tile = shape((TILES, OWNED, GROUP), BF16)
    agents = exchange(call(route_kernel, by_tile, 1.0, *came, scalars=(z,)), "xy")
    above = shift(x[TILES - 1, V_ROW:], "z", 1)
    below = shift(x[0, V_ROW:], "z", -1)

    part = call(agent_kernel, shape((PLANES, OWNED, PART), BF16), 3.0, agents, x)
    parts = exchange(part, "z")
    edges = shape((GROUP, EDGE), BF16)
    even = scalar(1 - lax.axis_index("tm") % 2)
    near, far = call(edge_kernel, (edges, edges), 1.0, x, above, below, scalars=(even,))
    groups = lax.axis_size("tm")
    pairs = [(i, i + 1) for i in range(0, groups - 1, 2)]
    near = lax.ppermute(near, "tm", pairs + [(b, a) for a, b in pairs])
    pairs = [(i, i + 1) for i in range(1, groups - 1, 2)]
    far = lax.ppermute(far, "tm", pairs + [(b, a) for a, b in pairs])

    owned = call(comb_kernel, shape((PLANES, OWNED, GROUP), BF16), 1.0, parts)
    values = exchange(owned, "z")
    local = call(
        conv_kernel,
        shape((TILES, GROUP, TOKENS), F32),
        5.0,
        x,
        above,
        below,
        near,
        far,
        taps,
        scalars=(even,),
    )
    mixed = call(mix_kernel, shape((TILES, GROUP, TOKENS), BF16), 2.0, agents, values, x, local)
    mine = exchange(mixed, "xy")
    out = call(unpack_kernel, shape((TOKENS, D), BF16), 1.0, mine)
    return out.reshape(value_states.shape)


def solution(mesh):
    devices = mesh.devices
    fine = Mesh(devices.reshape(devices.shape[0], PLANES, TILES), ("tm", "z", "xy"))
    spec = P("tm", None, ("z", "xy"), None, None)
    return jax.shard_map(
        body,
        mesh=fine,
        in_specs=(spec, spec, spec, P()),
        out_specs=spec,
        check_vma=False,
    )
```

```python
import jax
import jax.numpy as jnp
from jax import lax
from jax.experimental import pallas as pl
from jax.experimental.pallas import tpu as pltpu
from jax.sharding import Mesh
from jax.sharding import PartitionSpec as P


HEADS = 24
HEAD_DIM = 64
D = 1536
FRAMES = 4
COLUMNS = 32
TOKENS = FRAMES * COLUMNS
AGENT_DEV = 4
PAIRS = 4
PLANES = 2 * PAIRS
TILES = 8
AGENTS = 256
GROUP_HEADS = HEADS // TILES
GROUP = GROUP_HEADS * HEAD_DIM
K_ROW = GROUP
V_ROW = 2 * GROUP
SENT = 3 * GROUP
PAIR_AGENTS = 2 * TILES * AGENT_DEV
EDGE = TILES * COLUMNS
STATS = 16
GRANT = 6 * 1024 * 1024
ALL = 60 * 1024 * 1024
INV_ROOT = HEAD_DIM ** (-0.5)
F32 = jnp.float32
BF16 = jnp.bfloat16


VMEM = pl.BlockSpec(memory_space=pltpu.VMEM)

SMEM = pl.BlockSpec(memory_space=pltpu.SMEM)
HBM = pl.BlockSpec(memory_space=pltpu.HBM)


def call(kernel, out_shape, us, *args, scalars=(), scratch=(), far=False, far_out=False):
    cost = pl.CostEstimate(flops=int(us * 3.0e8), bytes_accessed=int(us * 2.0e6), transcendentals=0)
    out = HBM if far_out else VMEM
    return pl.pallas_call(
        kernel,
        out_shape=out_shape,
        in_specs=[SMEM] * len(scalars) + [HBM if far else VMEM] * len(args),
        out_specs=(out,) * len(out_shape) if isinstance(out_shape, tuple) else out,
        scratch_shapes=list(scratch),
        cost_estimate=cost,
        compiler_params=pltpu.CompilerParams(vmem_limit_bytes=ALL if far else GRANT),
    )(*scalars, *args)


def exchange(x, axes):
    return lax.all_to_all(x, axes, 0, 0)


def shift(x, axis, step):
    count = PLANES
    pairs = [(i, i + step) for i in range(count) if 0 <= i + step < count]
    return lax.ppermute(x, axis, pairs)


def pool_kernel(q_ref, out_ref, came, sems):
    half = D // 2
    loads = [
        pltpu.make_async_copy(
            q_ref.at[:, pl.ds(n * half, half)], came.at[:, pl.ds(n * half, half)], sems.at[n]
        )
        for n in range(2)
    ]
    for load in loads:
        load.start()
    shape = (8, TOKENS)
    token = lax.broadcasted_iota(jnp.int32, shape, 1)
    agent = lax.broadcasted_iota(jnp.int32, shape, 0)
    width = COLUMNS // AGENT_DEV
    pick = ((token % COLUMNS) // width == agent).astype(F32).astype(BF16)
    for n, load in enumerate(loads):
        load.wait()
        sums = jnp.dot(pick, came[:, n * half : (n + 1) * half], preferred_element_type=F32)
        pooled = (sums[:AGENT_DEV] * (1.0 / (FRAMES * width))).astype(BF16)
        for k in range(TILES // 2):
            tile = n * (TILES // 2) + k
            part = pooled[:, k * GROUP : (k + 1) * GROUP]
            out_ref[tile] = part
            out_ref[TILES + tile] = part


def pack_kernel(q_ref, k_ref, v_ref, out_ref, came, turned, in_sems, out_sems):
    refs = (q_ref, k_ref, v_ref)
    loads = [pltpu.make_async_copy(ref, came.at[n], in_sems.at[n]) for n, ref in enumerate(refs)]
    for load in loads:
        load.start()
    stores = []
    for n, load in enumerate(loads):
        load.wait()
        flipped = came[n].T
        for tile in range(TILES):
            turned[n, tile] = flipped[tile * GROUP : (tile + 1) * GROUP]
        rows = pl.ds(n * GROUP, GROUP)
        store = pltpu.make_async_copy(turned.at[n], out_ref.at[:, rows, :], out_sems.at[n])
        store.start()
        stores.append(store)
    for store in stores:
        store.wait()


def rows_of(x_ref, start, size):
    return jnp.concatenate([x_ref[s, start : start + size, :] for s in range(TILES)], axis=1)


def agent_kernel(z_ref, *refs):
    came, (x_ref, out_ref, a_ref, q_ref) = refs[:PAIRS], refs[PAIRS:]
    for hop, ref in enumerate(came):
        z = lax.rem(z_ref[0] + PAIRS - hop, PAIRS)
        a_ref[pl.ds(pl.multiple_of(z * PAIR_AGENTS, PAIR_AGENTS), PAIR_AGENTS), :] = ref[...]
    columns = []
    lane = lax.broadcasted_iota(jnp.int32, (AGENTS, HEAD_DIM), 1)
    stats = jnp.zeros((AGENTS, HEAD_DIM), F32)
    for h in range(GROUP_HEADS):
        keys = rows_of(x_ref, K_ROW + h * HEAD_DIM, HEAD_DIM)
        values = rows_of(x_ref, V_ROW + h * HEAD_DIM, HEAD_DIM)
        agents = a_ref[:, h * HEAD_DIM : (h + 1) * HEAD_DIM]
        scores = jnp.dot(agents, keys, preferred_element_type=F32) * INV_ROOT
        peak = jnp.max(scores, axis=1, keepdims=True)
        weights = jnp.exp(scores - peak)
        total = jnp.sum(weights, axis=1, keepdims=True)
        acc = lax.dot_general(
            weights.astype(BF16), values, (((1,), (1,)), ((), ())), preferred_element_type=F32
        )
        columns.append(acc / total)
        left = peak + jnp.log(total)
        for piece in range(3):
            short = left.astype(BF16).astype(F32)
            left = left - short
            stats = jnp.where(lane == piece * GROUP_HEADS + h, short, stats)
    flipped = jnp.concatenate(columns + [stats], axis=1).T
    part = flipped[: GROUP + STATS].astype(BF16)
    for z in range(PLANES):
        out_ref[z] = part
    q_ref[...] = rows_of(x_ref, 0, GROUP)


def taps_kernel(tile_ref, w_ref, out_ref):
    for tile in range(TILES):

        @pl.when(tile_ref[0] == tile)
        def _(tile=tile):
            lanes = slice(tile * GROUP, (tile + 1) * GROUP)
            rows = [w_ref[i, j, :, lanes] for i in range(3) for j in range(3)]
            rows.append(jnp.zeros((5, GROUP), F32))
            out_ref[...] = jnp.concatenate(rows, axis=0).T


def edge_kernel(even_ref, x_ref, near_ref, far_ref):
    spot = lax.broadcasted_iota(jnp.int32, (GROUP, TOKENS), 1) // COLUMNS
    for block in range(EDGE // TOKENS):
        last = first = jnp.zeros((GROUP, TOKENS), F32)
        for j in range(FRAMES):
            cells = x_ref[block * FRAMES + j, V_ROW:, :].astype(F32)
            late = cells if j == FRAMES - 1 else pltpu.roll(cells, (j + 1) * COLUMNS, 1)
            early = cells if j == 0 else pltpu.roll(cells, j * COLUMNS, 1)
            last = jnp.where(spot == j, late, last)
            first = jnp.where(spot == j, early, first)
        lanes = slice(block * TOKENS, (block + 1) * TOKENS)
        last, first = last.astype(BF16), first.astype(BF16)

        @pl.when(even_ref[0] == 1)
        def _(last=last, first=first, lanes=lanes):
            near_ref[:, lanes] = last
            far_ref[:, lanes] = first

        @pl.when(even_ref[0] != 1)
        def _(last=last, first=first, lanes=lanes):
            near_ref[:, lanes] = first
            far_ref[:, lanes] = last


TALL = 16


def turned(cells, by):
    by %= TOKENS
    return cells if by == 0 else pltpu.roll(cells, by, 1)


def frames_of(r, at, even, x_ref, near_ref, far_ref, tall=TALL):
    lane = lax.broadcasted_iota(jnp.int32, (tall, TOKENS), 1)
    cells = x_ref[r, pl.ds(V_ROW + at, tall), :].astype(F32)
    block, j = divmod(r, FRAMES)
    lanes = slice(block * TOKENS, (block + 1) * TOKENS)
    near = near_ref[pl.ds(at, tall), lanes].astype(F32)
    far = far_ref[pl.ds(at, tall), lanes].astype(F32)
    before = turned(jnp.where(even, far, near), -j * COLUMNS)
    after = turned(jnp.where(even, near, far), (FRAMES - 1 - j) * COLUMNS)
    return (
        jnp.where(lane < COLUMNS, before, turned(cells, COLUMNS)),
        cells,
        jnp.where(lane >= TOKENS - COLUMNS, after, turned(cells, -COLUMNS)),
    )


def taps_of(w_ref, at, rows=range(3), tall=TALL):
    w = w_ref[pl.ds(at, tall), :]
    return {
        (i, j, k): jnp.broadcast_to(w[:, n : n + 1], (tall, TOKENS))
        for i in range(3)
        for j in rows
        for k in range(3)
        for n in (i * 9 + j * 3 + k,)
    }


def stencil(rows, taps):
    shape = next(iter(rows.values()))[1].shape
    column = lax.broadcasted_iota(jnp.int32, shape, 1) % COLUMNS
    sums = []
    for k in range(3):
        total = None
        for j, frames in rows.items():
            for i in range(3):
                term = frames[i] * taps[i, j, k]
                total = term if total is None else total + term
        sums.append(total)
    left = jnp.where(column == 0, 0.0, pltpu.roll(sums[0], 1, 1))
    right = jnp.where(column == COLUMNS - 1, 0.0, pltpu.roll(sums[2], TOKENS - 1, 1))
    return left + sums[1] + right


def rim_kernel(even_ref, x_ref, near_ref, far_ref, w_ref, up_ref, down_ref):
    even = even_ref[0] == 1
    tall = GROUP // 2
    for at in range(0, GROUP, tall):
        for r, j, ref in ((TILES - 1, 0, up_ref), (0, 2, down_ref)):
            frames = frames_of(r, at, even, x_ref, near_ref, far_ref, tall)
            taps = taps_of(w_ref, at, (j,), tall)
            ref[pl.ds(at, tall), :] = stencil({j: frames}, taps).astype(BF16)


def conv_kernel(even_ref, x_ref, near_ref, far_ref, w_ref, out_ref):
    even = even_ref[0] == 1

    def step(n, carry):
        at = pl.multiple_of(n * TALL, TALL)
        taps = taps_of(w_ref, at)
        rows = {0: frames_of(0, at, even, x_ref, near_ref, far_ref)}
        for r in range(TILES):
            if r + 1 < TILES:
                rows[r + 1] = frames_of(r + 1, at, even, x_ref, near_ref, far_ref)
            near = {j: rows[r + j - 1] for j in range(3) if r + j - 1 in rows}
            out_ref[r, pl.ds(at, TALL), :] = stencil(near, taps)
            rows.pop(r - 1, None)
        return carry

    lax.fori_loop(0, GROUP // TALL, step, 0)


def mix_kernel(parts_ref, a_ref, q_ref, local_ref, up_ref, down_ref, out_ref):
    logs = []
    for z in range(PLANES):
        pieces = parts_ref[z, GROUP : GROUP + STATS, :].astype(F32)
        n = GROUP_HEADS
        logs.append(pieces[:n] + pieces[n : 2 * n] + pieces[2 * n : 3 * n])
    peak = logs[0]
    for log in logs[1:]:
        peak = jnp.maximum(peak, log)
    shares = [jnp.exp(log - peak) for log in logs]
    whole = sum(shares[1:], shares[0])
    shares = [share / whole for share in shares]
    for h in range(GROUP_HEADS):
        rows = slice(h * HEAD_DIM, (h + 1) * HEAD_DIM)
        values = None
        for z in range(PLANES):
            term = parts_ref[z, rows, :].astype(F32) * shares[z][h : h + 1]
            values = term if values is None else values + term
        scores = jnp.dot(a_ref[:, rows], q_ref[rows, :], preferred_element_type=F32) * INV_ROOT
        weights = jnp.exp(scores - jnp.max(scores, axis=0, keepdims=True))
        total = jnp.sum(weights, axis=0, keepdims=True)
        mixed = jnp.dot(values.astype(BF16), weights.astype(BF16), preferred_element_type=F32) / total
        for s in range(TILES):
            cells = mixed[:, s * TOKENS : (s + 1) * TOKENS] + local_ref[s, rows, :]
            if s == 0:
                cells += up_ref[rows, :].astype(F32)
            if s == TILES - 1:
                cells += down_ref[rows, :].astype(F32)
            out_ref[s, rows, :] = cells.astype(BF16)


def unpack_kernel(x_ref, out_ref, back, sems):
    pieces, stores = TILES // 2, []
    wide = D // pieces
    for n in range(pieces):
        back[n] = x_ref[2 * n : 2 * n + 2].reshape(wide, TOKENS).T
        store = pltpu.make_async_copy(back.at[n], out_ref.at[:, pl.ds(n * wide, wide)], sems.at[n])
        store.start()
        stores.append(store)
    for store in stores:
        store.wait()


def scalar(x):
    return x.astype(jnp.int32).reshape(1)


def body(queries, key_states, value_states, conv_weight):
    q = queries.reshape(TOKENS, D)
    k = key_states.reshape(TOKENS, D)
    v = value_states.reshape(TOKENS, D)
    shape = jax.ShapeDtypeStruct
    pooled = call(
        pool_kernel,
        shape((2 * TILES, AGENT_DEV, GROUP), BF16),
        1.0,
        q,
        scratch=(pltpu.VMEM((TOKENS, D), BF16), pltpu.SemaphoreType.DMA((2,))),
        far=True,
    )
    packed = call(
        pack_kernel,
        shape((TILES, SENT, TOKENS), BF16),
        3.0,
        q,
        k,
        v,
        scratch=(
            pltpu.VMEM((3, TOKENS, D), BF16),
            pltpu.VMEM((3, TILES, GROUP, TOKENS), BF16),
            pltpu.SemaphoreType.DMA((3,)),
            pltpu.SemaphoreType.DMA((3,)),
        ),
        far=True,
        far_out=True,
    )
    own = exchange(pooled, ("zl", "xy")).reshape(PAIR_AGENTS, GROUP)
    x = exchange(packed, "xy")
    came = [own]
    for n in range(1, PAIRS):
        came.append(lax.ppermute(own, "zh", [(i, (i + n) % PAIRS) for i in range(PAIRS)]))
    tile = scalar(lax.axis_index("xy"))
    taps = call(taps_kernel, shape((GROUP, 32), F32), 1.0, conv_weight, scalars=(tile,))

    part, agents, turned_q = call(
        agent_kernel,
        (
            shape((PLANES, GROUP + STATS, AGENTS), BF16),
            shape((AGENTS, GROUP), BF16),
            shape((GROUP, TILES * TOKENS), BF16),
        ),
        4.0,
        *came,
        x,
        scalars=(scalar(lax.axis_index("zh")),),
    )
    parts = exchange(part, ("zh", "zl"))

    edges = shape((GROUP, EDGE), BF16)
    even = scalar(1 - lax.axis_index("tm") % 2)
    near, far = call(edge_kernel, (edges, edges), 1.0, x, scalars=(even,))
    groups = lax.axis_size("tm")
    pairs = [(i, i + 1) for i in range(0, groups - 1, 2)]
    near = lax.ppermute(near, "tm", pairs + [(b, a) for a, b in pairs])
    pairs = [(i, i + 1) for i in range(1, groups - 1, 2)]
    far = lax.ppermute(far, "tm", pairs + [(b, a) for a, b in pairs])
    row = shape((GROUP, TOKENS), BF16)
    to_next, to_last = call(rim_kernel, (row, row), 1.0, x, near, far, taps, scalars=(even,))
    up = shift(to_next, ("zh", "zl"), 1)
    down = shift(to_last, ("zh", "zl"), -1)
    local = call(
        conv_kernel, shape((TILES, GROUP, TOKENS), F32), 5.0, x, near, far, taps, scalars=(even,)
    )
    mixed = call(
        mix_kernel,
        shape((TILES, GROUP, TOKENS), BF16),
        1.0,
        parts,
        agents,
        turned_q,
        local,
        up,
        down,
    )
    mine = exchange(mixed, "xy")
    pieces = TILES // 2
    out = call(
        unpack_kernel,
        shape((TOKENS, D), BF16),
        1.0,
        mine,
        scratch=(
            pltpu.VMEM((pieces, TOKENS, D // pieces), BF16),
            pltpu.SemaphoreType.DMA((pieces,)),
        ),
        far_out=True,
    )
    return out.reshape(value_states.shape)


def solution(mesh):
    devices = mesh.devices
    fine = Mesh(devices.reshape(devices.shape[0], PAIRS, 2, TILES), ("tm", "zh", "zl", "xy"))
    spec = P("tm", None, ("zh", "zl", "xy"), None, None)
    return jax.shard_map(
        body,
        mesh=fine,
        in_specs=(spec, spec, spec, P()),
        out_specs=spec,
        check_vma=False,
    )
```

```python
import jax
import jax.numpy as jnp
from jax import lax
from jax.experimental import pallas as pl
from jax.experimental.pallas import tpu as pltpu
from jax.sharding import Mesh
from jax.sharding import PartitionSpec as P


HEADS = 24
HEAD_DIM = 64
D = 1536
FRAMES = 4
COLUMNS = 32
TOKENS = FRAMES * COLUMNS
AGENT_DEV = 4
PAIRS = 4
PLANES = 2 * PAIRS
TILES = 8
AGENTS = 256
HALF = AGENTS // 2
GROUP_HEADS = HEADS // TILES
GROUP = GROUP_HEADS * HEAD_DIM
K_ROW = GROUP
V_ROW = 2 * GROUP
SENT = 3 * GROUP
PAIR_AGENTS = 2 * TILES * AGENT_DEV
EDGE = TILES * COLUMNS
STATS = 16
GRANT = 6 * 1024 * 1024
ALL = 60 * 1024 * 1024
INV_ROOT = HEAD_DIM ** (-0.5)
F32 = jnp.float32
BF16 = jnp.bfloat16


VMEM = pl.BlockSpec(memory_space=pltpu.VMEM)

SMEM = pl.BlockSpec(memory_space=pltpu.SMEM)
HBM = pl.BlockSpec(memory_space=pltpu.HBM)


def call(kernel, out_shape, us, *args, scalars=(), scratch=(), far=False, far_out=False):
    cost = pl.CostEstimate(flops=int(us * 3.0e8), bytes_accessed=int(us * 2.0e6), transcendentals=0)
    out = HBM if far_out else VMEM
    return pl.pallas_call(
        kernel,
        out_shape=out_shape,
        in_specs=[SMEM] * len(scalars) + [HBM if far else VMEM] * len(args),
        out_specs=(out,) * len(out_shape) if isinstance(out_shape, tuple) else out,
        scratch_shapes=list(scratch),
        cost_estimate=cost,
        compiler_params=pltpu.CompilerParams(vmem_limit_bytes=ALL if far else GRANT),
    )(*scalars, *args)


def exchange(x, axes):
    return lax.all_to_all(x, axes, 0, 0)


def shift(x, axis, step):
    count = PLANES
    pairs = [(i, i + step) for i in range(count) if 0 <= i + step < count]
    return lax.ppermute(x, axis, pairs)


def pool_kernel(q_ref, out_ref, came, sems):
    half = D // 2
    loads = [
        pltpu.make_async_copy(
            q_ref.at[:, pl.ds(n * half, half)], came.at[:, pl.ds(n * half, half)], sems.at[n]
        )
        for n in range(2)
    ]
    for load in loads:
        load.start()
    shape = (8, TOKENS)
    token = lax.broadcasted_iota(jnp.int32, shape, 1)
    agent = lax.broadcasted_iota(jnp.int32, shape, 0)
    width = COLUMNS // AGENT_DEV
    pick = ((token % COLUMNS) // width == agent).astype(F32).astype(BF16)
    for n, load in enumerate(loads):
        load.wait()
        sums = jnp.dot(pick, came[:, n * half : (n + 1) * half], preferred_element_type=F32)
        pooled = (sums[:AGENT_DEV] * (1.0 / (FRAMES * width))).astype(BF16)
        for k in range(TILES // 2):
            tile = n * (TILES // 2) + k
            part = pooled[:, k * GROUP : (k + 1) * GROUP]
            out_ref[tile] = part
            out_ref[TILES + tile] = part


def pack_kernel(q_ref, k_ref, v_ref, out_ref, came, turned, in_sems, out_sems):
    refs = (q_ref, k_ref, v_ref)
    loads = [pltpu.make_async_copy(ref, came.at[n], in_sems.at[n]) for n, ref in enumerate(refs)]
    for load in loads:
        load.start()
    stores = []
    for n, load in enumerate(loads):
        load.wait()
        flipped = came[n].T
        for tile in range(TILES):
            turned[n, tile] = flipped[tile * GROUP : (tile + 1) * GROUP]
        rows = pl.ds(n * GROUP, GROUP)
        store = pltpu.make_async_copy(turned.at[n], out_ref.at[:, rows, :], out_sems.at[n])
        store.start()
        stores.append(store)
    for store in stores:
        store.wait()


def rows_of(x_ref, start, size):
    return jnp.concatenate([x_ref[s, start : start + size, :] for s in range(TILES)], axis=1)


def agent_kernel(z_ref, *refs):
    came, (x_ref, keep_ref, send_ref, a_ref, q_ref) = refs[:PAIRS], refs[PAIRS:]
    low = z_ref[1] == 0
    for hop, ref in enumerate(came):
        z = lax.rem(z_ref[0] + PAIRS - hop, PAIRS)
        a_ref[pl.ds(pl.multiple_of(z * PAIR_AGENTS, PAIR_AGENTS), PAIR_AGENTS), :] = ref[...]
    columns = []
    logs = []
    for h in range(GROUP_HEADS):
        keys = rows_of(x_ref, K_ROW + h * HEAD_DIM, HEAD_DIM)
        values = rows_of(x_ref, V_ROW + h * HEAD_DIM, HEAD_DIM)
        agents = a_ref[:, h * HEAD_DIM : (h + 1) * HEAD_DIM]
        scores = jnp.dot(agents, keys, preferred_element_type=F32) * INV_ROOT
        peak = jnp.max(scores, axis=1, keepdims=True)
        weights = jnp.exp(scores - peak)
        total = jnp.sum(weights, axis=1, keepdims=True)
        acc = lax.dot_general(
            weights.astype(BF16), values, (((1,), (1,)), ((), ())), preferred_element_type=F32
        )
        columns.append(acc / total)
        logs.append(peak + jnp.log(total))
    lane = lax.broadcasted_iota(jnp.int32, (AGENTS, HEAD_DIM), 1)
    stats = jnp.zeros((AGENTS, HEAD_DIM), F32)
    for h, log in enumerate(logs):
        stats = jnp.where(lane == h, log, stats)
    part = jnp.concatenate(columns + [stats], axis=1).T
    near, far = part[:, :HALF], part[:, HALF:]
    keep_ref[...] = jnp.where(low, near, far)[: GROUP + 8]
    away = jnp.where(low, far, near)
    send_ref[:GROUP] = away[:GROUP].astype(BF16)
    send_ref[GROUP:] = pieces_of(away[GROUP : GROUP + GROUP_HEADS])
    q_ref[...] = rows_of(x_ref, 0, GROUP)


def pieces_of(logs):
    pieces = []
    for _ in range(3):
        short = logs.astype(BF16).astype(F32)
        logs = logs - short
        pieces.append(short)
    pieces.append(jnp.zeros((STATS - 3 * GROUP_HEADS, HALF), F32))
    return jnp.concatenate(pieces, axis=0).astype(BF16)


def logs_of(pieces):
    n = GROUP_HEADS
    pieces = pieces.astype(F32)
    return pieces[:n] + pieces[n : 2 * n] + pieces[2 * n : 3 * n]


def blend_kernel(keep_ref, came_ref, out_ref):
    ours, theirs = keep_ref[GROUP : GROUP + GROUP_HEADS, :], logs_of(came_ref[GROUP:, :])
    peak = jnp.maximum(ours, theirs)
    left, right = jnp.exp(ours - peak), jnp.exp(theirs - peak)
    whole = left + right
    left, right = left / whole, right / whole
    stats = pieces_of(peak + jnp.log(whole))
    for h in range(GROUP_HEADS):
        rows = slice(h * HEAD_DIM, (h + 1) * HEAD_DIM)
        part = keep_ref[rows, :] * left[h : h + 1] + came_ref[rows, :].astype(F32) * right[h : h + 1]
        part = part.astype(BF16)
        for z in range(PLANES):
            out_ref[z, rows, :] = part
    for z in range(PLANES):
        out_ref[z, GROUP:, :] = stats


def taps_kernel(tile_ref, w_ref, out_ref):
    for tile in range(TILES):

        @pl.when(tile_ref[0] == tile)
        def _(tile=tile):
            lanes = slice(tile * GROUP, (tile + 1) * GROUP)
            rows = [w_ref[i, j, :, lanes] for i in range(3) for j in range(3)]
            rows.append(jnp.zeros((5, GROUP), F32))
            out_ref[...] = jnp.concatenate(rows, axis=0).T


def edge_kernel(even_ref, x_ref, near_ref, far_ref):
    spot = lax.broadcasted_iota(jnp.int32, (GROUP, TOKENS), 1) // COLUMNS
    for block in range(EDGE // TOKENS):
        last = first = jnp.zeros((GROUP, TOKENS), F32)
        for j in range(FRAMES):
            cells = x_ref[block * FRAMES + j, V_ROW:, :].astype(F32)
            late = cells if j == FRAMES - 1 else pltpu.roll(cells, (j + 1) * COLUMNS, 1)
            early = cells if j == 0 else pltpu.roll(cells, j * COLUMNS, 1)
            last = jnp.where(spot == j, late, last)
            first = jnp.where(spot == j, early, first)
        lanes = slice(block * TOKENS, (block + 1) * TOKENS)
        last, first = last.astype(BF16), first.astype(BF16)

        @pl.when(even_ref[0] == 1)
        def _(last=last, first=first, lanes=lanes):
            near_ref[:, lanes] = last
            far_ref[:, lanes] = first

        @pl.when(even_ref[0] != 1)
        def _(last=last, first=first, lanes=lanes):
            near_ref[:, lanes] = first
            far_ref[:, lanes] = last


TALL = 16


def turned(cells, by):
    by %= TOKENS
    return cells if by == 0 else pltpu.roll(cells, by, 1)


def frames_of(r, at, even, x_ref, near_ref, far_ref, tall=TALL):
    lane = lax.broadcasted_iota(jnp.int32, (tall, TOKENS), 1)
    cells = x_ref[r, pl.ds(V_ROW + at, tall), :].astype(F32)
    block, j = divmod(r, FRAMES)
    lanes = slice(block * TOKENS, (block + 1) * TOKENS)
    near = near_ref[pl.ds(at, tall), lanes].astype(F32)
    far = far_ref[pl.ds(at, tall), lanes].astype(F32)
    before = turned(jnp.where(even, far, near), -j * COLUMNS)
    after = turned(jnp.where(even, near, far), (FRAMES - 1 - j) * COLUMNS)
    return (
        jnp.where(lane < COLUMNS, before, turned(cells, COLUMNS)),
        cells,
        jnp.where(lane >= TOKENS - COLUMNS, after, turned(cells, -COLUMNS)),
    )


def taps_of(w_ref, at, rows=range(3), tall=TALL):
    w = w_ref[pl.ds(at, tall), :]
    return {
        (i, j, k): jnp.broadcast_to(w[:, n : n + 1], (tall, TOKENS))
        for i in range(3)
        for j in rows
        for k in range(3)
        for n in (i * 9 + j * 3 + k,)
    }


def stencil(rows, taps):
    shape = next(iter(rows.values()))[1].shape
    column = lax.broadcasted_iota(jnp.int32, shape, 1) % COLUMNS
    sums = []
    for k in range(3):
        total = None
        for j, frames in rows.items():
            for i in range(3):
                term = frames[i] * taps[i, j, k]
                total = term if total is None else total + term
        sums.append(total)
    left = jnp.where(column == 0, 0.0, pltpu.roll(sums[0], 1, 1))
    right = jnp.where(column == COLUMNS - 1, 0.0, pltpu.roll(sums[2], TOKENS - 1, 1))
    return left + sums[1] + right


def rim_kernel(even_ref, x_ref, near_ref, far_ref, w_ref, up_ref, down_ref):
    even = even_ref[0] == 1
    tall = GROUP // 2
    for at in range(0, GROUP, tall):
        for r, j, ref in ((TILES - 1, 0, up_ref), (0, 2, down_ref)):
            frames = frames_of(r, at, even, x_ref, near_ref, far_ref, tall)
            taps = taps_of(w_ref, at, (j,), tall)
            ref[pl.ds(at, tall), :] = stencil({j: frames}, taps).astype(BF16)


def conv_kernel(even_ref, x_ref, near_ref, far_ref, w_ref, out_ref):
    even = even_ref[0] == 1

    def step(n, carry):
        at = pl.multiple_of(n * TALL, TALL)
        taps = taps_of(w_ref, at)
        rows = {0: frames_of(0, at, even, x_ref, near_ref, far_ref)}
        for r in range(TILES):
            if r + 1 < TILES:
                rows[r + 1] = frames_of(r + 1, at, even, x_ref, near_ref, far_ref)
            near = {j: rows[r + j - 1] for j in range(3) if r + j - 1 in rows}
            out_ref[r, pl.ds(at, TALL), :] = stencil(near, taps)
            rows.pop(r - 1, None)
        return carry

    lax.fori_loop(0, GROUP // TALL, step, 0)


def mix_kernel(parts_ref, a_ref, q_ref, local_ref, up_ref, down_ref, out_ref):
    shares = []
    for half in range(2):
        logs = [logs_of(parts_ref[z, GROUP:, :]) for z in range(half, PLANES, 2)]
        peak = logs[0]
        for log in logs[1:]:
            peak = jnp.maximum(peak, log)
        some = [jnp.exp(log - peak) for log in logs]
        whole = sum(some[1:], some[0])
        shares.append([share / whole for share in some])
    for h in range(GROUP_HEADS):
        rows = slice(h * HEAD_DIM, (h + 1) * HEAD_DIM)
        halves = []
        for half in range(2):
            terms = [
                parts_ref[z, rows, :].astype(F32) * shares[half][z // 2][h : h + 1]
                for z in range(half, PLANES, 2)
            ]
            halves.append(sum(terms[1:], terms[0]))
        values = jnp.concatenate(halves, axis=1)
        scores = jnp.dot(a_ref[:, rows], q_ref[rows, :], preferred_element_type=F32) * INV_ROOT
        weights = jnp.exp(scores - jnp.max(scores, axis=0, keepdims=True))
        total = jnp.sum(weights, axis=0, keepdims=True)
        mixed = jnp.dot(values.astype(BF16), weights.astype(BF16), preferred_element_type=F32) / total
        for s in range(TILES):
            cells = mixed[:, s * TOKENS : (s + 1) * TOKENS] + local_ref[s, rows, :]
            if s == 0:
                cells += up_ref[rows, :].astype(F32)
            if s == TILES - 1:
                cells += down_ref[rows, :].astype(F32)
            out_ref[s, rows, :] = cells.astype(BF16)


def unpack_kernel(x_ref, out_ref, back, sems):
    pieces, stores = TILES // 2, []
    wide = D // pieces
    for n in range(pieces):
        back[n] = x_ref[2 * n : 2 * n + 2].reshape(wide, TOKENS).T
        store = pltpu.make_async_copy(back.at[n], out_ref.at[:, pl.ds(n * wide, wide)], sems.at[n])
        store.start()
        stores.append(store)
    for store in stores:
        store.wait()


def scalar(x):
    return x.astype(jnp.int32).reshape(1)


def body(queries, key_states, value_states, conv_weight):
    q = queries.reshape(TOKENS, D)
    k = key_states.reshape(TOKENS, D)
    v = value_states.reshape(TOKENS, D)
    shape = jax.ShapeDtypeStruct
    pooled = call(
        pool_kernel,
        shape((2 * TILES, AGENT_DEV, GROUP), BF16),
        1.0,
        q,
        scratch=(pltpu.VMEM((TOKENS, D), BF16), pltpu.SemaphoreType.DMA((2,))),
        far=True,
    )
    packed = call(
        pack_kernel,
        shape((TILES, SENT, TOKENS), BF16),
        3.0,
        q,
        k,
        v,
        scratch=(
            pltpu.VMEM((3, TOKENS, D), BF16),
            pltpu.VMEM((3, TILES, GROUP, TOKENS), BF16),
            pltpu.SemaphoreType.DMA((3,)),
            pltpu.SemaphoreType.DMA((3,)),
        ),
        far=True,
        far_out=True,
    )
    own = exchange(pooled, ("zl", "xy")).reshape(PAIR_AGENTS, GROUP)
    x = exchange(packed, "xy")
    came = [own]
    for n in range(1, PAIRS):
        came.append(lax.ppermute(own, "zh", [(i, (i + n) % PAIRS) for i in range(PAIRS)]))
    tile = scalar(lax.axis_index("xy"))
    taps = call(taps_kernel, shape((GROUP, 32), F32), 1.0, conv_weight, scalars=(tile,))

    keep, send, agents, turned_q = call(
        agent_kernel,
        (
            shape((GROUP + 8, HALF), F32),
            shape((GROUP + STATS, HALF), BF16),
            shape((AGENTS, GROUP), BF16),
            shape((GROUP, TILES * TOKENS), BF16),
        ),
        3.0,
        *came,
        x,
        scalars=(jnp.stack([lax.axis_index("zh"), lax.axis_index("zl")]).astype(jnp.int32),),
    )
    theirs = lax.ppermute(send, "zl", [(0, 1), (1, 0)])
    blended = call(blend_kernel, shape((PLANES, GROUP + STATS, HALF), BF16), 1.0, keep, theirs)
    parts = exchange(blended, ("zh", "zl"))

    edges = shape((GROUP, EDGE), BF16)
    even = scalar(1 - lax.axis_index("tm") % 2)
    near, far = call(edge_kernel, (edges, edges), 1.0, x, scalars=(even,))
    groups = lax.axis_size("tm")
    pairs = [(i, i + 1) for i in range(0, groups - 1, 2)]
    near = lax.ppermute(near, "tm", pairs + [(b, a) for a, b in pairs])
    pairs = [(i, i + 1) for i in range(1, groups - 1, 2)]
    far = lax.ppermute(far, "tm", pairs + [(b, a) for a, b in pairs])
    row = shape((GROUP, TOKENS), BF16)
    to_next, to_last = call(rim_kernel, (row, row), 1.0, x, near, far, taps, scalars=(even,))
    up = shift(to_next, ("zh", "zl"), 1)
    down = shift(to_last, ("zh", "zl"), -1)
    local = call(
        conv_kernel, shape((TILES, GROUP, TOKENS), F32), 5.0, x, near, far, taps, scalars=(even,)
    )
    mixed = call(
        mix_kernel,
        shape((TILES, GROUP, TOKENS), BF16),
        1.0,
        parts,
        agents,
        turned_q,
        local,
        up,
        down,
    )
    mine = exchange(mixed, "xy")
    pieces = TILES // 2
    out = call(
        unpack_kernel,
        shape((TOKENS, D), BF16),
        1.0,
        mine,
        scratch=(
            pltpu.VMEM((pieces, TOKENS, D // pieces), BF16),
            pltpu.SemaphoreType.DMA((pieces,)),
        ),
        far_out=True,
    )
    return out.reshape(value_states.shape)


def solution(mesh):
    devices = mesh.devices
    fine = Mesh(devices.reshape(devices.shape[0], PAIRS, 2, TILES), ("tm", "zh", "zl", "xy"))
    spec = P("tm", None, ("zh", "zl", "xy"), None, None)
    return jax.shard_map(
        body,
        mesh=fine,
        in_specs=(spec, spec, spec, P()),
        out_specs=spec,
        check_vma=False,
    )
```

```python
import jax
import jax.numpy as jnp
from jax import lax
from jax.experimental import pallas as pl
from jax.experimental.pallas import tpu as pltpu
from jax.sharding import Mesh
from jax.sharding import PartitionSpec as P


HEADS = 24
HEAD_DIM = 64
D = 1536
FRAMES = 4
COLUMNS = 32
TOKENS = FRAMES * COLUMNS
AGENT_DEV = 4
PAIRS = 4
PLANES = 2 * PAIRS
TILES = 8
AGENTS = 256
HALF = AGENTS // 2
GROUP_HEADS = HEADS // TILES
GROUP = GROUP_HEADS * HEAD_DIM
K_ROW = GROUP
V_ROW = 2 * GROUP
SENT = 3 * GROUP
PLANE_AGENTS = TILES * AGENT_DEV
EDGE = TILES * COLUMNS
STATS = 16
GRANT = 6 * 1024 * 1024
ALL = 60 * 1024 * 1024
INV_ROOT = HEAD_DIM ** (-0.5)
F32 = jnp.float32
BF16 = jnp.bfloat16


VMEM = pl.BlockSpec(memory_space=pltpu.VMEM)

SMEM = pl.BlockSpec(memory_space=pltpu.SMEM)
HBM = pl.BlockSpec(memory_space=pltpu.HBM)


def call(kernel, out_shape, us, *args, scalars=(), scratch=(), far=False, far_out=False):
    cost = pl.CostEstimate(flops=int(us * 3.0e8), bytes_accessed=int(us * 2.0e6), transcendentals=0)
    out = HBM if far_out else VMEM
    return pl.pallas_call(
        kernel,
        out_shape=out_shape,
        in_specs=[SMEM] * len(scalars) + [HBM if far else VMEM] * len(args),
        out_specs=(out,) * len(out_shape) if isinstance(out_shape, tuple) else out,
        scratch_shapes=list(scratch),
        cost_estimate=cost,
        compiler_params=pltpu.CompilerParams(vmem_limit_bytes=ALL if far else GRANT),
    )(*scalars, *args)


def exchange(x, axes):
    return lax.all_to_all(x, axes, 0, 0)


def shift(x, axis, step):
    count = PLANES
    pairs = [(i, i + step) for i in range(count) if 0 <= i + step < count]
    return lax.ppermute(x, axis, pairs)


def pack_kernel(q_ref, k_ref, v_ref, out_ref, came, turned, in_sems, out_sems):
    refs = (q_ref, k_ref, v_ref)
    loads = [pltpu.make_async_copy(ref, came.at[n], in_sems.at[n]) for n, ref in enumerate(refs)]
    for load in loads:
        load.start()
    stores = []
    for n, load in enumerate(loads):
        load.wait()
        flipped = came[n].T
        for tile in range(TILES):
            turned[n, tile] = flipped[tile * GROUP : (tile + 1) * GROUP]
        rows = pl.ds(n * GROUP, GROUP)
        store = pltpu.make_async_copy(turned.at[n], out_ref.at[:, rows, :], out_sems.at[n])
        store.start()
        stores.append(store)
    for store in stores:
        store.wait()


def rows_of(x_ref, start, size):
    return jnp.concatenate([x_ref[s, start : start + size, :] for s in range(TILES)], axis=1)


def pool_kernel(x_ref, out_ref):
    shape = (PLANE_AGENTS, TILES * TOKENS)
    cell = lax.broadcasted_iota(jnp.int32, shape, 1)
    agent = lax.broadcasted_iota(jnp.int32, shape, 0)
    width = COLUMNS // AGENT_DEV
    owner = cell // TOKENS * AGENT_DEV + cell % COLUMNS // width
    pick = (owner == agent).astype(F32).astype(BF16)
    sums = lax.dot_general(
        pick, rows_of(x_ref, 0, GROUP), (((1,), (1,)), ((), ())), preferred_element_type=F32
    )
    pooled = (sums * (1.0 / (FRAMES * width))).astype(BF16)
    for z in range(PLANES):
        out_ref[z] = pooled


def agent_kernel(low_ref, a_ref, x_ref, keep_ref, send_ref):
    low = low_ref[0] == 1
    everyone = a_ref[...].reshape(AGENTS, GROUP)
    columns = []
    logs = []
    for h in range(GROUP_HEADS):
        keys = rows_of(x_ref, K_ROW + h * HEAD_DIM, HEAD_DIM)
        values = rows_of(x_ref, V_ROW + h * HEAD_DIM, HEAD_DIM)
        agents = everyone[:, h * HEAD_DIM : (h + 1) * HEAD_DIM]
        scores = jnp.dot(agents, keys, preferred_element_type=F32) * INV_ROOT
        peak = jnp.max(scores, axis=1, keepdims=True)
        weights = jnp.exp(scores - peak)
        total = jnp.sum(weights, axis=1, keepdims=True)
        acc = lax.dot_general(
            weights.astype(BF16), values, (((1,), (1,)), ((), ())), preferred_element_type=F32
        )
        columns.append(acc / total)
        logs.append(peak + jnp.log(total))
    lane = lax.broadcasted_iota(jnp.int32, (AGENTS, HEAD_DIM), 1)
    stats = jnp.zeros((AGENTS, HEAD_DIM), F32)
    for h, log in enumerate(logs):
        stats = jnp.where(lane == h, log, stats)
    part = jnp.concatenate(columns + [stats], axis=1).T
    near, far = part[:, :HALF], part[:, HALF:]
    keep_ref[...] = jnp.where(low, near, far)[: GROUP + 8]
    away = jnp.where(low, far, near)
    send_ref[:GROUP] = away[:GROUP].astype(BF16)
    send_ref[GROUP:] = pieces_of(away[GROUP : GROUP + GROUP_HEADS])


def pieces_of(logs):
    pieces = []
    for _ in range(3):
        short = logs.astype(BF16).astype(F32)
        logs = logs - short
        pieces.append(short)
    pieces.append(jnp.zeros((STATS - 3 * GROUP_HEADS, HALF), F32))
    return jnp.concatenate(pieces, axis=0).astype(BF16)


def logs_of(pieces):
    n = GROUP_HEADS
    pieces = pieces.astype(F32)
    return pieces[:n] + pieces[n : 2 * n] + pieces[2 * n : 3 * n]


def blend_kernel(keep_ref, came_ref, out_ref):
    ours, theirs = keep_ref[GROUP : GROUP + GROUP_HEADS, :], logs_of(came_ref[GROUP:, :])
    peak = jnp.maximum(ours, theirs)
    left, right = jnp.exp(ours - peak), jnp.exp(theirs - peak)
    whole = left + right
    left, right = left / whole, right / whole
    stats = pieces_of(peak + jnp.log(whole))
    for h in range(GROUP_HEADS):
        rows = slice(h * HEAD_DIM, (h + 1) * HEAD_DIM)
        part = keep_ref[rows, :] * left[h : h + 1] + came_ref[rows, :].astype(F32) * right[h : h + 1]
        out_ref[rows, :] = part.astype(BF16)
    out_ref[GROUP:, :] = stats


def comb_kernel(*refs):
    parts, out_ref = refs[:-1], refs[-1]
    logs = [logs_of(part[GROUP:, :]) for part in parts]
    peak = logs[0]
    for log in logs[1:]:
        peak = jnp.maximum(peak, log)
    shares = [jnp.exp(log - peak) for log in logs]
    whole = sum(shares[1:], shares[0])
    shares = [share / whole for share in shares]
    for h in range(GROUP_HEADS):
        rows = slice(h * HEAD_DIM, (h + 1) * HEAD_DIM)
        terms = [
            part[rows, :].astype(F32) * share[h : h + 1]
            for part, share in zip(parts, shares, strict=True)
        ]
        out_ref[rows, :] = sum(terms[1:], terms[0]).astype(BF16)


def taps_kernel(tile_ref, w_ref, out_ref):
    for tile in range(TILES):

        @pl.when(tile_ref[0] == tile)
        def _(tile=tile):
            lanes = slice(tile * GROUP, (tile + 1) * GROUP)
            rows = [w_ref[i, j, :, lanes] for i in range(3) for j in range(3)]
            rows.append(jnp.zeros((5, GROUP), F32))
            out_ref[...] = jnp.concatenate(rows, axis=0).T


def edge_kernel(even_ref, x_ref, near_ref, far_ref, q_ref):
    q_ref[...] = rows_of(x_ref, 0, GROUP)
    spot = lax.broadcasted_iota(jnp.int32, (GROUP, TOKENS), 1) // COLUMNS
    for block in range(EDGE // TOKENS):
        last = first = jnp.zeros((GROUP, TOKENS), F32)
        for j in range(FRAMES):
            cells = x_ref[block * FRAMES + j, V_ROW:, :].astype(F32)
            late = cells if j == FRAMES - 1 else pltpu.roll(cells, (j + 1) * COLUMNS, 1)
            early = cells if j == 0 else pltpu.roll(cells, j * COLUMNS, 1)
            last = jnp.where(spot == j, late, last)
            first = jnp.where(spot == j, early, first)
        lanes = slice(block * TOKENS, (block + 1) * TOKENS)
        last, first = last.astype(BF16), first.astype(BF16)

        @pl.when(even_ref[0] == 1)
        def _(last=last, first=first, lanes=lanes):
            near_ref[:, lanes] = last
            far_ref[:, lanes] = first

        @pl.when(even_ref[0] != 1)
        def _(last=last, first=first, lanes=lanes):
            near_ref[:, lanes] = first
            far_ref[:, lanes] = last


TALL = 16


def turned(cells, by):
    by %= TOKENS
    return cells if by == 0 else pltpu.roll(cells, by, 1)


def frames_of(r, at, even, x_ref, near_ref, far_ref, tall=TALL):
    lane = lax.broadcasted_iota(jnp.int32, (tall, TOKENS), 1)
    cells = x_ref[r, pl.ds(V_ROW + at, tall), :].astype(F32)
    block, j = divmod(r, FRAMES)
    lanes = slice(block * TOKENS, (block + 1) * TOKENS)
    near = near_ref[pl.ds(at, tall), lanes].astype(F32)
    far = far_ref[pl.ds(at, tall), lanes].astype(F32)
    before = turned(jnp.where(even, far, near), -j * COLUMNS)
    after = turned(jnp.where(even, near, far), (FRAMES - 1 - j) * COLUMNS)
    return (
        jnp.where(lane < COLUMNS, before, turned(cells, COLUMNS)),
        cells,
        jnp.where(lane >= TOKENS - COLUMNS, after, turned(cells, -COLUMNS)),
    )


def taps_of(w_ref, at, rows=range(3), tall=TALL):
    w = w_ref[pl.ds(at, tall), :]
    return {
        (i, j, k): jnp.broadcast_to(w[:, n : n + 1], (tall, TOKENS))
        for i in range(3)
        for j in rows
        for k in range(3)
        for n in (i * 9 + j * 3 + k,)
    }


def stencil(rows, taps):
    shape = next(iter(rows.values()))[1].shape
    column = lax.broadcasted_iota(jnp.int32, shape, 1) % COLUMNS
    sums = []
    for k in range(3):
        total = None
        for j, frames in rows.items():
            for i in range(3):
                term = frames[i] * taps[i, j, k]
                total = term if total is None else total + term
        sums.append(total)
    left = jnp.where(column == 0, 0.0, pltpu.roll(sums[0], 1, 1))
    right = jnp.where(column == COLUMNS - 1, 0.0, pltpu.roll(sums[2], TOKENS - 1, 1))
    return left + sums[1] + right


def rim_kernel(even_ref, x_ref, near_ref, far_ref, w_ref, up_ref, down_ref):
    even = even_ref[0] == 1
    tall = GROUP // 2
    for at in range(0, GROUP, tall):
        for r, j, ref in ((TILES - 1, 0, up_ref), (0, 2, down_ref)):
            frames = frames_of(r, at, even, x_ref, near_ref, far_ref, tall)
            taps = taps_of(w_ref, at, (j,), tall)
            ref[pl.ds(at, tall), :] = stencil({j: frames}, taps).astype(BF16)


def conv_kernel(even_ref, x_ref, near_ref, far_ref, w_ref, out_ref):
    even = even_ref[0] == 1

    def step(n, carry):
        at = pl.multiple_of(n * TALL, TALL)
        taps = taps_of(w_ref, at)
        rows = {0: frames_of(0, at, even, x_ref, near_ref, far_ref)}
        for r in range(TILES):
            if r + 1 < TILES:
                rows[r + 1] = frames_of(r + 1, at, even, x_ref, near_ref, far_ref)
            near = {j: rows[r + j - 1] for j in range(3) if r + j - 1 in rows}
            out_ref[r, pl.ds(at, TALL), :] = stencil(near, taps)
            rows.pop(r - 1, None)
        return carry

    lax.fori_loop(0, GROUP // TALL, step, 0)


def mix_kernel(low_ref, a_ref, q_ref, ours_ref, theirs_ref, local_ref, up_ref, down_ref, out_ref):
    low = low_ref[0] == 1
    agents = a_ref[...].reshape(AGENTS, GROUP)
    ours, theirs = ours_ref[...], theirs_ref[...]
    values = jnp.concatenate(
        [jnp.where(low, ours, theirs), jnp.where(low, theirs, ours)], axis=1
    )
    for h in range(GROUP_HEADS):
        rows = slice(h * HEAD_DIM, (h + 1) * HEAD_DIM)
        scores = jnp.dot(agents[:, rows], q_ref[rows, :], preferred_element_type=F32) * INV_ROOT
        weights = jnp.exp(scores - jnp.max(scores, axis=0, keepdims=True))
        total = jnp.sum(weights, axis=0, keepdims=True)
        mixed = jnp.dot(values[rows], weights.astype(BF16), preferred_element_type=F32) / total
        for s in range(TILES):
            cells = mixed[:, s * TOKENS : (s + 1) * TOKENS] + local_ref[s, rows, :]
            if s == 0:
                cells += up_ref[rows, :].astype(F32)
            if s == TILES - 1:
                cells += down_ref[rows, :].astype(F32)
            out_ref[s, rows, :] = cells.astype(BF16)


def unpack_kernel(x_ref, out_ref, back, sems):
    pieces, stores = TILES // 2, []
    wide = D // pieces
    for n in range(pieces):
        back[n] = x_ref[2 * n : 2 * n + 2].reshape(wide, TOKENS).T
        store = pltpu.make_async_copy(back.at[n], out_ref.at[:, pl.ds(n * wide, wide)], sems.at[n])
        store.start()
        stores.append(store)
    for store in stores:
        store.wait()


def scalar(x):
    return x.astype(jnp.int32).reshape(1)


def body(queries, key_states, value_states, conv_weight):
    q = queries.reshape(TOKENS, D)
    k = key_states.reshape(TOKENS, D)
    v = value_states.reshape(TOKENS, D)
    shape = jax.ShapeDtypeStruct
    packed = call(
        pack_kernel,
        shape((TILES, SENT, TOKENS), BF16),
        3.0,
        q,
        k,
        v,
        scratch=(
            pltpu.VMEM((3, TOKENS, D), BF16),
            pltpu.VMEM((3, TILES, GROUP, TOKENS), BF16),
            pltpu.SemaphoreType.DMA((3,)),
            pltpu.SemaphoreType.DMA((3,)),
        ),
        far=True,
        far_out=True,
    )
    x = exchange(packed, "xy")
    tile = scalar(lax.axis_index("xy"))
    taps = call(taps_kernel, shape((GROUP, 32), F32), 1.0, conv_weight, scalars=(tile,))

    low = scalar(1 - lax.axis_index("zl"))
    even = scalar(1 - lax.axis_index("tm") % 2)
    pooled = call(pool_kernel, shape((PLANES, PLANE_AGENTS, GROUP), BF16), 1.0, x)
    agents = exchange(pooled, ("zh", "zl"))
    edges = shape((GROUP, EDGE), BF16)
    near, far, turned_q = call(
        edge_kernel, (edges, edges, shape((GROUP, TILES * TOKENS), BF16)), 1.0, x, scalars=(even,)
    )
    groups = lax.axis_size("tm")
    pairs = [(i, i + 1) for i in range(0, groups - 1, 2)]
    near = lax.ppermute(near, "tm", pairs + [(b, a) for a, b in pairs])
    pairs = [(i, i + 1) for i in range(1, groups - 1, 2)]
    far = lax.ppermute(far, "tm", pairs + [(b, a) for a, b in pairs])
    keep, send = call(
        agent_kernel,
        (shape((GROUP + 8, HALF), F32), shape((GROUP + STATS, HALF), BF16)),
        3.0,
        agents,
        x,
        scalars=(low,),
    )
    swap = [(0, 1), (1, 0)]
    theirs = lax.ppermute(send, "zl", swap)
    row = shape((GROUP, TOKENS), BF16)
    to_next, to_last = call(rim_kernel, (row, row), 1.0, x, near, far, taps, scalars=(even,))
    up = shift(to_next, ("zh", "zl"), 1)
    down = shift(to_last, ("zh", "zl"), -1)
    blended = call(blend_kernel, shape((GROUP + STATS, HALF), BF16), 1.0, keep, theirs)
    parts = [blended]
    for n in range(1, PAIRS):
        parts.append(lax.ppermute(blended, "zh", [(i, (i + n) % PAIRS) for i in range(PAIRS)]))
    local = call(
        conv_kernel, shape((TILES, GROUP, TOKENS), F32), 5.0, x, near, far, taps, scalars=(even,)
    )
    ours = call(comb_kernel, shape((GROUP, HALF), BF16), 1.0, *parts)
    theirs = lax.ppermute(ours, "zl", swap)
    mixed = call(
        mix_kernel,
        shape((TILES, GROUP, TOKENS), BF16),
        1.0,
        agents,
        turned_q,
        ours,
        theirs,
        local,
        up,
        down,
        scalars=(low,),
    )
    mine = exchange(mixed, "xy")
    pieces = TILES // 2
    out = call(
        unpack_kernel,
        shape((TOKENS, D), BF16),
        1.0,
        mine,
        scratch=(
            pltpu.VMEM((pieces, TOKENS, D // pieces), BF16),
            pltpu.SemaphoreType.DMA((pieces,)),
        ),
        far_out=True,
    )
    return out.reshape(value_states.shape)


def solution(mesh):
    devices = mesh.devices
    fine = Mesh(devices.reshape(devices.shape[0], PAIRS, 2, TILES), ("tm", "zh", "zl", "xy"))
    spec = P("tm", None, ("zh", "zl", "xy"), None, None)
    return jax.shard_map(
        body,
        mesh=fine,
        in_specs=(spec, spec, spec, P()),
        out_specs=spec,
        check_vma=False,
    )
```

```python
import jax
import jax.numpy as jnp
from jax import lax
from jax.experimental import pallas as pl
from jax.experimental.pallas import tpu as pltpu
from jax.sharding import Mesh
from jax.sharding import PartitionSpec as P


HEADS = 24
HEAD_DIM = 64
D = 1536
FRAMES = 4
COLUMNS = 32
TOKENS = FRAMES * COLUMNS
AGENT_DEV = 4
PAIRS = 4
PLANES = 2 * PAIRS
TILES = 8
AGENTS = 256
HALF = AGENTS // 2
GROUP_HEADS = HEADS // TILES
GROUP = GROUP_HEADS * HEAD_DIM
K_ROW = GROUP
V_ROW = 2 * GROUP
SENT = 3 * GROUP
PLANE_AGENTS = TILES * AGENT_DEV
EDGE = TILES * COLUMNS
STATS = 16
GRANT = 6 * 1024 * 1024
ALL = 60 * 1024 * 1024
INV_ROOT = HEAD_DIM ** (-0.5)
F32 = jnp.float32
BF16 = jnp.bfloat16


VMEM = pl.BlockSpec(memory_space=pltpu.VMEM)

SMEM = pl.BlockSpec(memory_space=pltpu.SMEM)
HBM = pl.BlockSpec(memory_space=pltpu.HBM)


def call(kernel, out_shape, us, *args, scalars=(), scratch=(), far=False, far_out=False):
    cost = pl.CostEstimate(flops=int(us * 3.0e8), bytes_accessed=int(us * 2.0e6), transcendentals=0)
    out = HBM if far_out else VMEM
    return pl.pallas_call(
        kernel,
        out_shape=out_shape,
        in_specs=[SMEM] * len(scalars) + [HBM if far else VMEM] * len(args),
        out_specs=(out,) * len(out_shape) if isinstance(out_shape, tuple) else out,
        scratch_shapes=list(scratch),
        cost_estimate=cost,
        compiler_params=pltpu.CompilerParams(vmem_limit_bytes=ALL if far else GRANT),
    )(*scalars, *args)


def exchange(x, axes):
    return lax.all_to_all(x, axes, 0, 0)


def pack_kernel(q_ref, k_ref, v_ref, out_ref, came, turned, in_sems, out_sems):
    refs = (q_ref, k_ref, v_ref)
    loads = [pltpu.make_async_copy(ref, came.at[n], in_sems.at[n]) for n, ref in enumerate(refs)]
    for load in loads:
        load.start()
    stores = []
    for n, load in enumerate(loads):
        load.wait()
        flipped = came[n].T
        for tile in range(TILES):
            turned[n, tile] = flipped[tile * GROUP : (tile + 1) * GROUP]
        rows = pl.ds(n * GROUP, GROUP)
        store = pltpu.make_async_copy(turned.at[n], out_ref.at[:, rows, :], out_sems.at[n])
        store.start()
        stores.append(store)
    for store in stores:
        store.wait()


def rows_of(x_ref, start, size):
    return jnp.concatenate([x_ref[s, start : start + size, :] for s in range(TILES)], axis=1)


def pool_kernel(x_ref, out_ref):
    shape = (PLANE_AGENTS, TILES * TOKENS)
    cell = lax.broadcasted_iota(jnp.int32, shape, 1)
    agent = lax.broadcasted_iota(jnp.int32, shape, 0)
    width = COLUMNS // AGENT_DEV
    owner = cell // TOKENS * AGENT_DEV + cell % COLUMNS // width
    pick = (owner == agent).astype(F32).astype(BF16)
    sums = lax.dot_general(
        pick, rows_of(x_ref, 0, GROUP), (((1,), (1,)), ((), ())), preferred_element_type=F32
    )
    pooled = (sums * (1.0 / (FRAMES * width))).astype(BF16)
    for z in range(PLANES):
        out_ref[z] = pooled


def agent_kernel(flags_ref, a_ref, x_ref, keep_ref, send_ref):
    low = flags_ref[1] == 1
    everyone = a_ref[...].reshape(AGENTS, GROUP)
    columns = []
    logs = []
    for h in range(GROUP_HEADS):
        keys = rows_of(x_ref, K_ROW + h * HEAD_DIM, HEAD_DIM)
        values = rows_of(x_ref, V_ROW + h * HEAD_DIM, HEAD_DIM)
        agents = everyone[:, h * HEAD_DIM : (h + 1) * HEAD_DIM]
        scores = jnp.dot(agents, keys, preferred_element_type=F32) * INV_ROOT
        peak = jnp.max(scores, axis=1, keepdims=True)
        weights = jnp.exp(scores - peak)
        total = jnp.sum(weights, axis=1, keepdims=True)
        acc = lax.dot_general(
            weights.astype(BF16), values, (((1,), (1,)), ((), ())), preferred_element_type=F32
        )
        columns.append(acc / total)
        logs.append(peak + jnp.log(total))
    lane = lax.broadcasted_iota(jnp.int32, (AGENTS, HEAD_DIM), 1)
    stats = jnp.zeros((AGENTS, HEAD_DIM), F32)
    for h, log in enumerate(logs):
        stats = jnp.where(lane == h, log, stats)
    part = jnp.concatenate(columns + [stats], axis=1).T
    near, far = part[:, :HALF], part[:, HALF:]
    keep_ref[...] = jnp.where(low, near, far)[: GROUP + 8]
    away = jnp.where(low, far, near)
    send_ref[:GROUP] = away[:GROUP].astype(BF16)
    send_ref[GROUP:] = pieces_of(away[GROUP : GROUP + GROUP_HEADS])


def pieces_of(logs):
    pieces = []
    for _ in range(3):
        short = logs.astype(BF16).astype(F32)
        logs = logs - short
        pieces.append(short)
    pieces.append(jnp.zeros((STATS - 3 * GROUP_HEADS, HALF), F32))
    return jnp.concatenate(pieces, axis=0).astype(BF16)


def logs_of(pieces):
    n = GROUP_HEADS
    pieces = pieces.astype(F32)
    return pieces[:n] + pieces[n : 2 * n] + pieces[2 * n : 3 * n]


def blend_kernel(keep_ref, came_ref, cross_ref, out_ref, long_ref):
    ours, theirs = keep_ref[GROUP : GROUP + GROUP_HEADS, :], logs_of(came_ref[GROUP:, :])
    peak = jnp.maximum(ours, theirs)
    left, right = jnp.exp(ours - peak), jnp.exp(theirs - peak)
    whole = left + right
    left, right = left / whole, right / whole
    stats = pieces_of(peak + jnp.log(whole))
    for h in range(GROUP_HEADS):
        rows = slice(h * HEAD_DIM, (h + 1) * HEAD_DIM)
        part = keep_ref[rows, :] * left[h : h + 1] + came_ref[rows, :].astype(F32) * right[h : h + 1]
        part = part.astype(BF16)
        out_ref[rows, :] = part
        long_ref[rows, :] = part
    out_ref[GROUP:, :] = stats
    long_ref[GROUP : GROUP + STATS, :] = stats
    long_ref[GROUP + STATS :, :] = cross_ref[...]


def comb_kernel(*refs):
    parts, (kin_ref, out_ref) = refs[:PAIRS], refs[PAIRS:]
    out_ref[GROUP:, :] = kin_ref[...]
    logs = [logs_of(part[GROUP : GROUP + STATS, :]) for part in parts]
    peak = logs[0]
    for log in logs[1:]:
        peak = jnp.maximum(peak, log)
    shares = [jnp.exp(log - peak) for log in logs]
    whole = sum(shares[1:], shares[0])
    shares = [share / whole for share in shares]
    for h in range(GROUP_HEADS):
        rows = slice(h * HEAD_DIM, (h + 1) * HEAD_DIM)
        terms = [
            part[rows, :].astype(F32) * share[h : h + 1]
            for part, share in zip(parts, shares, strict=True)
        ]
        out_ref[rows, :] = sum(terms[1:], terms[0]).astype(BF16)


def taps_kernel(tile_ref, w_ref, out_ref):
    for tile in range(TILES):

        @pl.when(tile_ref[0] == tile)
        def _(tile=tile):
            lanes = slice(tile * GROUP, (tile + 1) * GROUP)
            rows = [w_ref[i, j, :, lanes] for i in range(3) for j in range(3)]
            rows.append(jnp.zeros((5, GROUP), F32))
            out_ref[...] = jnp.concatenate(rows, axis=0).T


def edge_kernel(flags_ref, x_ref, near_ref, far_ref, q_ref):
    q_ref[...] = rows_of(x_ref, 0, GROUP)
    spot = lax.broadcasted_iota(jnp.int32, (GROUP, TOKENS), 1) // COLUMNS
    for block in range(EDGE // TOKENS):
        last = first = jnp.zeros((GROUP, TOKENS), F32)
        for j in range(FRAMES):
            cells = x_ref[block * FRAMES + j, V_ROW:, :].astype(F32)
            late = cells if j == FRAMES - 1 else pltpu.roll(cells, (j + 1) * COLUMNS, 1)
            early = cells if j == 0 else pltpu.roll(cells, j * COLUMNS, 1)
            last = jnp.where(spot == j, late, last)
            first = jnp.where(spot == j, early, first)
        lanes = slice(block * TOKENS, (block + 1) * TOKENS)
        last, first = last.astype(BF16), first.astype(BF16)

        @pl.when(flags_ref[0] == 1)
        def _(last=last, first=first, lanes=lanes):
            near_ref[:, lanes] = last
            far_ref[:, lanes] = first

        @pl.when(flags_ref[0] != 1)
        def _(last=last, first=first, lanes=lanes):
            near_ref[:, lanes] = first
            far_ref[:, lanes] = last


TALL = 16


def turned(cells, by):
    by %= TOKENS
    return cells if by == 0 else pltpu.roll(cells, by, 1)


def frames_of(r, at, even, x_ref, near_ref, far_ref, tall=TALL):
    lane = lax.broadcasted_iota(jnp.int32, (tall, TOKENS), 1)
    cells = x_ref[r, pl.ds(V_ROW + at, tall), :].astype(F32)
    block, j = divmod(r, FRAMES)
    lanes = slice(block * TOKENS, (block + 1) * TOKENS)
    near = near_ref[pl.ds(at, tall), lanes].astype(F32)
    far = far_ref[pl.ds(at, tall), lanes].astype(F32)
    before = turned(jnp.where(even, far, near), -j * COLUMNS)
    after = turned(jnp.where(even, near, far), (FRAMES - 1 - j) * COLUMNS)
    return (
        jnp.where(lane < COLUMNS, before, turned(cells, COLUMNS)),
        cells,
        jnp.where(lane >= TOKENS - COLUMNS, after, turned(cells, -COLUMNS)),
    )


def taps_of(w_ref, at, rows=range(3), tall=TALL):
    w = w_ref[pl.ds(at, tall), :]
    return {
        (i, j, k): jnp.broadcast_to(w[:, n : n + 1], (tall, TOKENS))
        for i in range(3)
        for j in rows
        for k in range(3)
        for n in (i * 9 + j * 3 + k,)
    }


def stencil(rows, taps):
    shape = next(iter(rows.values()))[1].shape
    column = lax.broadcasted_iota(jnp.int32, shape, 1) % COLUMNS
    sums = []
    for k in range(3):
        total = None
        for j, frames in rows.items():
            for i in range(3):
                term = frames[i] * taps[i, j, k]
                total = term if total is None else total + term
        sums.append(total)
    left = jnp.where(column == 0, 0.0, pltpu.roll(sums[0], 1, 1))
    right = jnp.where(column == COLUMNS - 1, 0.0, pltpu.roll(sums[2], TOKENS - 1, 1))
    return left + sums[1] + right


def rim_kernel(flags_ref, x_ref, near_ref, far_ref, w_ref, cross_ref, kin_ref):
    even, second = flags_ref[0] == 1, flags_ref[2] == 1
    tall = GROUP // 2
    for at in range(0, GROUP, tall):
        sums = []
        for r, j in ((TILES - 1, 0), (0, 2)):
            frames = frames_of(r, at, even, x_ref, near_ref, far_ref, tall)
            sums.append(stencil({j: frames}, taps_of(w_ref, at, (j,), tall)).astype(BF16))
        cross_ref[pl.ds(at, tall), :] = jnp.where(second, sums[0], sums[1])
        kin_ref[pl.ds(at, tall), :] = jnp.where(second, sums[1], sums[0])


def conv_kernel(flags_ref, x_ref, near_ref, far_ref, w_ref, out_ref):
    even = flags_ref[0] == 1

    def step(n, carry):
        at = pl.multiple_of(n * TALL, TALL)
        taps = taps_of(w_ref, at)
        rows = {0: frames_of(0, at, even, x_ref, near_ref, far_ref)}
        for r in range(TILES):
            if r + 1 < TILES:
                rows[r + 1] = frames_of(r + 1, at, even, x_ref, near_ref, far_ref)
            near = {j: rows[r + j - 1] for j in range(3) if r + j - 1 in rows}
            out_ref[r, pl.ds(at, TALL), :] = stencil(near, taps)
            rows.pop(r - 1, None)
        return carry

    lax.fori_loop(0, GROUP // TALL, step, 0)


def query_kernel(a_ref, q_ref, e_ref, total_ref):
    agents = a_ref[...].reshape(AGENTS, GROUP)
    for h in range(GROUP_HEADS):
        rows = slice(h * HEAD_DIM, (h + 1) * HEAD_DIM)
        scores = jnp.dot(agents[:, rows], q_ref[rows, :], preferred_element_type=F32) * INV_ROOT
        weights = jnp.exp(scores - jnp.max(scores, axis=0, keepdims=True))
        total_ref[h : h + 1, :] = jnp.sum(weights, axis=0, keepdims=True)
        e_ref[h] = weights.astype(BF16)


def mix_kernel(flags_ref, e_ref, total_ref, ours_ref, theirs_ref, one_ref, three_ref, local_ref, out_ref):
    low, second = flags_ref[1] == 1, flags_ref[2] == 1
    first, last = flags_ref[3] == 1, flags_ref[4] == 1
    ours, theirs = ours_ref[:GROUP], theirs_ref[:GROUP]
    values = jnp.concatenate(
        [jnp.where(low, ours, theirs), jnp.where(low, theirs, ours)], axis=1
    )
    kin = theirs_ref[GROUP:].astype(F32)
    below = three_ref[GROUP + STATS :].astype(F32)
    above = one_ref[GROUP + STATS :].astype(F32)
    above = jnp.where(first, 0.0, jnp.where(second, kin, above))
    below = jnp.where(last, 0.0, jnp.where(second, below, kin))
    for h in range(GROUP_HEADS):
        rows = slice(h * HEAD_DIM, (h + 1) * HEAD_DIM)
        mixed = jnp.dot(values[rows], e_ref[h], preferred_element_type=F32)
        mixed = mixed / total_ref[h : h + 1, :]
        for s in range(TILES):
            cells = mixed[:, s * TOKENS : (s + 1) * TOKENS] + local_ref[s, rows, :]
            if s == 0:
                cells += above[rows]
            if s == TILES - 1:
                cells += below[rows]
            out_ref[s, rows, :] = cells.astype(BF16)


def unpack_kernel(x_ref, out_ref, back, sems):
    pieces, stores = TILES // 2, []
    wide = D // pieces
    for n in range(pieces):
        back[n] = x_ref[2 * n : 2 * n + 2].reshape(wide, TOKENS).T
        store = pltpu.make_async_copy(back.at[n], out_ref.at[:, pl.ds(n * wide, wide)], sems.at[n])
        store.start()
        stores.append(store)
    for store in stores:
        store.wait()


def scalar(x):
    return x.astype(jnp.int32).reshape(1)


def body(queries, key_states, value_states, conv_weight):
    q = queries.reshape(TOKENS, D)
    k = key_states.reshape(TOKENS, D)
    v = value_states.reshape(TOKENS, D)
    shape = jax.ShapeDtypeStruct
    packed = call(
        pack_kernel,
        shape((TILES, SENT, TOKENS), BF16),
        3.0,
        q,
        k,
        v,
        scratch=(
            pltpu.VMEM((3, TOKENS, D), BF16),
            pltpu.VMEM((3, TILES, GROUP, TOKENS), BF16),
            pltpu.SemaphoreType.DMA((3,)),
            pltpu.SemaphoreType.DMA((3,)),
        ),
        far=True,
        far_out=True,
    )
    x = exchange(packed, "xy")
    tile = scalar(lax.axis_index("xy"))
    taps = call(taps_kernel, shape((GROUP, 32), F32), 1.0, conv_weight, scalars=(tile,))

    high, second = lax.axis_index("zh"), lax.axis_index("zl")
    plane = 2 * high + second
    flags = jnp.stack(
        [
            1 - lax.axis_index("tm") % 2,
            1 - (high + second) % 2,
            second,
            plane == 0,
            plane == PLANES - 1,
        ]
    ).astype(jnp.int32)
    pooled = call(pool_kernel, shape((PLANES, PLANE_AGENTS, GROUP), BF16), 1.0, x)
    agents = exchange(pooled, ("zh", "zl"))
    edges = shape((GROUP, EDGE), BF16)
    near, far, turned_q = call(
        edge_kernel, (edges, edges, shape((GROUP, TILES * TOKENS), BF16)), 1.0, x, scalars=(flags,)
    )
    groups = lax.axis_size("tm")
    pairs = [(i, i + 1) for i in range(0, groups - 1, 2)]
    near = lax.ppermute(near, "tm", pairs + [(b, a) for a, b in pairs])
    pairs = [(i, i + 1) for i in range(1, groups - 1, 2)]
    far = lax.ppermute(far, "tm", pairs + [(b, a) for a, b in pairs])
    keep, send = call(
        agent_kernel,
        (shape((GROUP + 8, HALF), F32), shape((GROUP + STATS, HALF), BF16)),
        3.0,
        agents,
        x,
        scalars=(flags,),
    )
    swap = [(0, 1), (1, 0)]
    theirs = lax.ppermute(send, "zl", swap)
    row = shape((GROUP, TOKENS), BF16)
    cross, kin = call(rim_kernel, (row, row), 1.0, x, near, far, taps, scalars=(flags,))
    blended, longer = call(
        blend_kernel,
        (shape((GROUP + STATS, HALF), BF16), shape((2 * GROUP + STATS, HALF), BF16)),
        1.0,
        keep,
        theirs,
        cross,
    )
    parts = [blended]
    for n in range(1, PAIRS):
        to = [2 * ((i // 2 + n) % PAIRS) + (i + n) % 2 for i in range(PLANES)]
        moved = longer if n % 2 else blended
        parts.append(lax.ppermute(moved, ("zh", "zl"), list(enumerate(to))))
    local = call(
        conv_kernel, shape((TILES, GROUP, TOKENS), F32), 5.0, x, near, far, taps, scalars=(flags,)
    )
    ours = call(comb_kernel, shape((2 * GROUP, HALF), BF16), 1.0, *parts, kin)
    theirs = lax.ppermute(ours, "zl", swap)
    weights, totals = call(
        query_kernel,
        (shape((GROUP_HEADS, AGENTS, TILES * TOKENS), BF16), shape((8, TILES * TOKENS), F32)),
        2.0,
        agents,
        turned_q,
    )
    mixed = call(
        mix_kernel,
        shape((TILES, GROUP, TOKENS), BF16),
        1.0,
        weights,
        totals,
        ours,
        theirs,
        parts[1],
        parts[3],
        local,
        scalars=(flags,),
    )
    mine = exchange(mixed, "xy")
    pieces = TILES // 2
    out = call(
        unpack_kernel,
        shape((TOKENS, D), BF16),
        1.0,
        mine,
        scratch=(
            pltpu.VMEM((pieces, TOKENS, D // pieces), BF16),
            pltpu.SemaphoreType.DMA((pieces,)),
        ),
        far_out=True,
    )
    return out.reshape(value_states.shape)


def solution(mesh):
    devices = mesh.devices
    fine = Mesh(devices.reshape(devices.shape[0], PAIRS, 2, TILES), ("tm", "zh", "zl", "xy"))
    spec = P("tm", None, ("zh", "zl", "xy"), None, None)
    return jax.shard_map(
        body,
        mesh=fine,
        in_specs=(spec, spec, spec, P()),
        out_specs=spec,
        check_vma=False,
    )
```

```python
import jax
import jax.numpy as jnp
from jax import lax
from jax.experimental import pallas as pl
from jax.experimental.pallas import tpu as pltpu
from jax.sharding import Mesh
from jax.sharding import PartitionSpec as P


HEADS = 24
HEAD_DIM = 64
D = 1536
FRAMES = 4
COLUMNS = 32
TOKENS = FRAMES * COLUMNS
AGENT_DEV = 4
PAIRS = 4
PLANES = 2 * PAIRS
TILES = 8
AGENTS = 256
SLOT = 8
HALF = AGENTS // 2
GROUP_HEADS = HEADS // TILES
GROUP = GROUP_HEADS * HEAD_DIM
K_ROW = GROUP
V_ROW = 2 * GROUP
SENT = 3 * GROUP
EDGE = TILES * COLUMNS
STATS = 16
GRANT = 6 * 1024 * 1024
ALL = 60 * 1024 * 1024
INV_ROOT = HEAD_DIM ** (-0.5)
F32 = jnp.float32
BF16 = jnp.bfloat16


VMEM = pl.BlockSpec(memory_space=pltpu.VMEM)

SMEM = pl.BlockSpec(memory_space=pltpu.SMEM)
HBM = pl.BlockSpec(memory_space=pltpu.HBM)


def call(kernel, out_shape, us, *args, scalars=(), scratch=(), far=False, far_out=False):
    cost = pl.CostEstimate(flops=int(us * 3.0e8), bytes_accessed=int(us * 2.0e6), transcendentals=0)
    first = HBM if far_out else VMEM
    several = isinstance(out_shape, tuple)
    return pl.pallas_call(
        kernel,
        out_shape=out_shape,
        in_specs=[SMEM] * len(scalars) + [HBM if far else VMEM] * len(args),
        out_specs=(first,) + (VMEM,) * (len(out_shape) - 1) if several else first,
        scratch_shapes=list(scratch),
        cost_estimate=cost,
        compiler_params=pltpu.CompilerParams(vmem_limit_bytes=ALL if far else GRANT),
    )(*scalars, *args)


def exchange(x, axes):
    return lax.all_to_all(x, axes, 0, 0)


def pack_kernel(q_ref, k_ref, v_ref, out_ref, pooled_ref, came, turned, in_sems, out_sems):
    refs = (q_ref, k_ref, v_ref)
    loads = [pltpu.make_async_copy(ref, came.at[n], in_sems.at[n]) for n, ref in enumerate(refs)]
    for load in loads:
        load.start()
    stores = []
    for n, load in enumerate(loads):
        load.wait()
        flipped = came[n].T
        for tile in range(TILES):
            turned[n, tile] = flipped[tile * GROUP : (tile + 1) * GROUP]
        rows = pl.ds(n * GROUP, GROUP)
        store = pltpu.make_async_copy(turned.at[n], out_ref.at[:, rows, :], out_sems.at[n])
        store.start()
        stores.append(store)
    shape = (SLOT, TOKENS)
    token = lax.broadcasted_iota(jnp.int32, shape, 1)
    agent = lax.broadcasted_iota(jnp.int32, shape, 0)
    width = COLUMNS // AGENT_DEV
    pick = ((token % COLUMNS) // width == agent).astype(F32).astype(BF16)
    sums = jnp.dot(pick, came[0], preferred_element_type=F32)
    pooled_ref[...] = (sums * (1.0 / (FRAMES * width))).astype(BF16)
    for store in stores:
        store.wait()


def rows_of(x_ref, start, size):
    return jnp.concatenate([x_ref[s, start : start + size, :] for s in range(TILES)], axis=1)


def couple_kernel(z_ref, ours_ref, theirs_ref, out_ref):
    ours, theirs = ours_ref[...].astype(F32), theirs_ref[...].astype(F32)
    second = lax.rem(z_ref[0], 2) == 1
    low, high = jnp.where(second, theirs, ours), jnp.where(second, ours, theirs)
    out_ref[...] = (low + pltpu.roll(high, AGENT_DEV, 0)).astype(BF16)


def route_kernel(z_ref, *refs):
    came, out_ref = refs[:PAIRS], refs[PAIRS]
    rows = jnp.concatenate([ref[...].astype(F32) for ref in came], axis=0).astype(BF16)
    shape = (PAIRS * SLOT, PAIRS * SLOT)
    to = lax.broadcasted_iota(jnp.int32, shape, 0)
    at = lax.broadcasted_iota(jnp.int32, shape, 1)
    hop = (z_ref[0] // 2 + PAIRS - to // SLOT) % PAIRS
    pick = (at == hop * SLOT + to % SLOT).astype(F32).astype(BF16)
    agents = jnp.dot(pick, rows, preferred_element_type=F32).astype(BF16)
    for tile in range(TILES):
        out_ref[tile] = agents[:, tile * GROUP : (tile + 1) * GROUP]


def agent_kernel(tm_ref, z_ref, a_ref, x_ref, keep_ref, send_ref):
    low = lax.rem(z_ref[0] // 2 + z_ref[0], 2) == 0
    everyone = a_ref[...].reshape(AGENTS, GROUP)
    columns = []
    logs = []
    for h in range(GROUP_HEADS):
        keys = rows_of(x_ref, K_ROW + h * HEAD_DIM, HEAD_DIM)
        values = rows_of(x_ref, V_ROW + h * HEAD_DIM, HEAD_DIM)
        agents = everyone[:, h * HEAD_DIM : (h + 1) * HEAD_DIM]
        scores = jnp.dot(agents, keys, preferred_element_type=F32) * INV_ROOT
        peak = jnp.max(scores, axis=1, keepdims=True)
        weights = jnp.exp(scores - peak)
        total = jnp.sum(weights, axis=1, keepdims=True)
        acc = lax.dot_general(
            weights.astype(BF16), values, (((1,), (1,)), ((), ())), preferred_element_type=F32
        )
        columns.append(acc / total)
        logs.append(peak + jnp.log(total))
    lane = lax.broadcasted_iota(jnp.int32, (AGENTS, HEAD_DIM), 1)
    stats = jnp.zeros((AGENTS, HEAD_DIM), F32)
    for h, log in enumerate(logs):
        stats = jnp.where(lane == h, log, stats)
    part = jnp.concatenate(columns + [stats], axis=1).T
    near, far = part[:, :HALF], part[:, HALF:]
    keep_ref[...] = jnp.where(low, near, far)[: GROUP + 8]
    away = jnp.where(low, far, near)
    send_ref[:GROUP] = away[:GROUP].astype(BF16)
    send_ref[GROUP:] = pieces_of(away[GROUP : GROUP + GROUP_HEADS])


def pieces_of(logs):
    pieces = []
    for _ in range(3):
        short = logs.astype(BF16).astype(F32)
        logs = logs - short
        pieces.append(short)
    pieces.append(jnp.zeros((STATS - 3 * GROUP_HEADS, HALF), F32))
    return jnp.concatenate(pieces, axis=0).astype(BF16)


def logs_of(pieces):
    n = GROUP_HEADS
    pieces = pieces.astype(F32)
    return pieces[:n] + pieces[n : 2 * n] + pieces[2 * n : 3 * n]


def blend_kernel(keep_ref, came_ref, cross_ref, out_ref, long_ref):
    ours, theirs = keep_ref[GROUP : GROUP + GROUP_HEADS, :], logs_of(came_ref[GROUP:, :])
    peak = jnp.maximum(ours, theirs)
    left, right = jnp.exp(ours - peak), jnp.exp(theirs - peak)
    whole = left + right
    left, right = left / whole, right / whole
    stats = pieces_of(peak + jnp.log(whole))
    for h in range(GROUP_HEADS):
        rows = slice(h * HEAD_DIM, (h + 1) * HEAD_DIM)
        part = keep_ref[rows, :] * left[h : h + 1] + came_ref[rows, :].astype(F32) * right[h : h + 1]
        part = part.astype(BF16)
        out_ref[rows, :] = part
        long_ref[rows, :] = part
    out_ref[GROUP:, :] = stats
    long_ref[GROUP : GROUP + STATS, :] = stats
    long_ref[GROUP + STATS :, :] = cross_ref[...]


def comb_kernel(*refs):
    parts, (kin_ref, out_ref) = refs[:PAIRS], refs[PAIRS:]
    out_ref[GROUP:, :] = kin_ref[...]
    logs = [logs_of(part[GROUP : GROUP + STATS, :]) for part in parts]
    peak = logs[0]
    for log in logs[1:]:
        peak = jnp.maximum(peak, log)
    shares = [jnp.exp(log - peak) for log in logs]
    whole = sum(shares[1:], shares[0])
    shares = [share / whole for share in shares]
    for h in range(GROUP_HEADS):
        rows = slice(h * HEAD_DIM, (h + 1) * HEAD_DIM)
        terms = [
            part[rows, :].astype(F32) * share[h : h + 1]
            for part, share in zip(parts, shares, strict=True)
        ]
        out_ref[rows, :] = sum(terms[1:], terms[0]).astype(BF16)


def taps_kernel(tile_ref, w_ref, out_ref):
    for tile in range(TILES):

        @pl.when(tile_ref[0] == tile)
        def _(tile=tile):
            lanes = slice(tile * GROUP, (tile + 1) * GROUP)
            rows = [w_ref[i, j, :, lanes] for i in range(3) for j in range(3)]
            rows.append(jnp.zeros((5, GROUP), F32))
            out_ref[...] = jnp.concatenate(rows, axis=0).T


def edge_kernel(tm_ref, z_ref, x_ref, near_ref, far_ref, q_ref):
    q_ref[...] = rows_of(x_ref, 0, GROUP)
    spot = lax.broadcasted_iota(jnp.int32, (GROUP, TOKENS), 1) // COLUMNS
    for block in range(EDGE // TOKENS):
        last = first = jnp.zeros((GROUP, TOKENS), F32)
        for j in range(FRAMES):
            cells = x_ref[block * FRAMES + j, V_ROW:, :].astype(F32)
            late = cells if j == FRAMES - 1 else pltpu.roll(cells, (j + 1) * COLUMNS, 1)
            early = cells if j == 0 else pltpu.roll(cells, j * COLUMNS, 1)
            last = jnp.where(spot == j, late, last)
            first = jnp.where(spot == j, early, first)
        lanes = slice(block * TOKENS, (block + 1) * TOKENS)
        last, first = last.astype(BF16), first.astype(BF16)

        @pl.when(lax.rem(tm_ref[0], 2) == 0)
        def _(last=last, first=first, lanes=lanes):
            near_ref[:, lanes] = last
            far_ref[:, lanes] = first

        @pl.when(lax.rem(tm_ref[0], 2) != 0)
        def _(last=last, first=first, lanes=lanes):
            near_ref[:, lanes] = first
            far_ref[:, lanes] = last


TALL = 16


def turned(cells, by):
    by %= TOKENS
    return cells if by == 0 else pltpu.roll(cells, by, 1)


def frames_of(r, at, even, x_ref, near_ref, far_ref, tall=TALL):
    lane = lax.broadcasted_iota(jnp.int32, (tall, TOKENS), 1)
    cells = x_ref[r, pl.ds(V_ROW + at, tall), :].astype(F32)
    block, j = divmod(r, FRAMES)
    lanes = slice(block * TOKENS, (block + 1) * TOKENS)
    near = near_ref[pl.ds(at, tall), lanes].astype(F32)
    far = far_ref[pl.ds(at, tall), lanes].astype(F32)
    before = turned(jnp.where(even, far, near), -j * COLUMNS)
    after = turned(jnp.where(even, near, far), (FRAMES - 1 - j) * COLUMNS)
    return (
        jnp.where(lane < COLUMNS, before, turned(cells, COLUMNS)),
        cells,
        jnp.where(lane >= TOKENS - COLUMNS, after, turned(cells, -COLUMNS)),
    )


def taps_of(w_ref, at, rows=range(3), tall=TALL):
    w = w_ref[pl.ds(at, tall), :]
    return {
        (i, j, k): jnp.broadcast_to(w[:, n : n + 1], (tall, TOKENS))
        for i in range(3)
        for j in rows
        for k in range(3)
        for n in (i * 9 + j * 3 + k,)
    }


def stencil(rows, taps):
    shape = next(iter(rows.values()))[1].shape
    column = lax.broadcasted_iota(jnp.int32, shape, 1) % COLUMNS
    sums = []
    for k in range(3):
        total = None
        for j, frames in rows.items():
            for i in range(3):
                term = frames[i] * taps[i, j, k]
                total = term if total is None else total + term
        sums.append(total)
    left = jnp.where(column == 0, 0.0, pltpu.roll(sums[0], 1, 1))
    right = jnp.where(column == COLUMNS - 1, 0.0, pltpu.roll(sums[2], TOKENS - 1, 1))
    return left + sums[1] + right


def rim_kernel(tm_ref, z_ref, x_ref, near_ref, far_ref, w_ref, cross_ref, kin_ref):
    even, second = lax.rem(tm_ref[0], 2) == 0, lax.rem(z_ref[0], 2) == 1
    tall = GROUP // 2
    for at in range(0, GROUP, tall):
        sums = []
        for r, j in ((TILES - 1, 0), (0, 2)):
            frames = frames_of(r, at, even, x_ref, near_ref, far_ref, tall)
            sums.append(stencil({j: frames}, taps_of(w_ref, at, (j,), tall)).astype(BF16))
        cross_ref[pl.ds(at, tall), :] = jnp.where(second, sums[0], sums[1])
        kin_ref[pl.ds(at, tall), :] = jnp.where(second, sums[1], sums[0])


def conv_kernel(tm_ref, z_ref, x_ref, near_ref, far_ref, w_ref, out_ref):
    even = lax.rem(tm_ref[0], 2) == 0

    def step(n, carry):
        at = pl.multiple_of(n * TALL, TALL)
        taps = taps_of(w_ref, at)
        rows = {0: frames_of(0, at, even, x_ref, near_ref, far_ref)}
        for r in range(TILES):
            if r + 1 < TILES:
                rows[r + 1] = frames_of(r + 1, at, even, x_ref, near_ref, far_ref)
            near = {j: rows[r + j - 1] for j in range(3) if r + j - 1 in rows}
            out_ref[r, pl.ds(at, TALL), :] = stencil(near, taps)
            rows.pop(r - 1, None)
        return carry

    lax.fori_loop(0, GROUP // TALL, step, 0)


def query_kernel(a_ref, q_ref, e_ref, total_ref):
    agents = a_ref[...].reshape(AGENTS, GROUP)
    for h in range(GROUP_HEADS):
        rows = slice(h * HEAD_DIM, (h + 1) * HEAD_DIM)
        scores = jnp.dot(agents[:, rows], q_ref[rows, :], preferred_element_type=F32) * INV_ROOT
        weights = jnp.exp(scores - jnp.max(scores, axis=0, keepdims=True))
        total_ref[h : h + 1, :] = jnp.sum(weights, axis=0, keepdims=True)
        e_ref[h] = weights.astype(BF16)


def mix_kernel(tm_ref, z_ref, e_ref, total_ref, ours_ref, theirs_ref, one_ref, three_ref, local_ref, out_ref):
    low, second = lax.rem(z_ref[0] // 2 + z_ref[0], 2) == 0, lax.rem(z_ref[0], 2) == 1
    first, last = z_ref[0] == 0, z_ref[0] == PLANES - 1
    ours, theirs = ours_ref[:GROUP], theirs_ref[:GROUP]
    values = jnp.concatenate(
        [jnp.where(low, ours, theirs), jnp.where(low, theirs, ours)], axis=1
    )
    kin = theirs_ref[GROUP:].astype(F32)
    below = three_ref[GROUP + STATS :].astype(F32)
    above = one_ref[GROUP + STATS :].astype(F32)
    above = jnp.where(first, 0.0, jnp.where(second, kin, above))
    below = jnp.where(last, 0.0, jnp.where(second, below, kin))
    for h in range(GROUP_HEADS):
        rows = slice(h * HEAD_DIM, (h + 1) * HEAD_DIM)
        mixed = jnp.dot(values[rows], e_ref[h], preferred_element_type=F32)
        mixed = mixed / total_ref[h : h + 1, :]
        for s in range(TILES):
            cells = mixed[:, s * TOKENS : (s + 1) * TOKENS] + local_ref[s, rows, :]
            if s == 0:
                cells += above[rows]
            if s == TILES - 1:
                cells += below[rows]
            out_ref[s, rows, :] = cells.astype(BF16)


def unpack_kernel(x_ref, out_ref, back, sems):
    pieces, stores = TILES // 2, []
    wide = D // pieces
    for n in range(pieces):
        back[n] = x_ref[2 * n : 2 * n + 2].reshape(wide, TOKENS).T
        store = pltpu.make_async_copy(back.at[n], out_ref.at[:, pl.ds(n * wide, wide)], sems.at[n])
        store.start()
        stores.append(store)
    for store in stores:
        store.wait()


def scalar(x):
    return x.astype(jnp.int32).reshape(1)


def body(queries, key_states, value_states, conv_weight):
    q = queries.reshape(TOKENS, D)
    k = key_states.reshape(TOKENS, D)
    v = value_states.reshape(TOKENS, D)
    shape = jax.ShapeDtypeStruct
    packed, pooled = call(
        pack_kernel,
        (shape((TILES, SENT, TOKENS), BF16), shape((SLOT, D), BF16)),
        3.0,
        q,
        k,
        v,
        scratch=(
            pltpu.VMEM((3, TOKENS, D), BF16),
            pltpu.VMEM((3, TILES, GROUP, TOKENS), BF16),
            pltpu.SemaphoreType.DMA((3,)),
            pltpu.SemaphoreType.DMA((3,)),
        ),
        far=True,
        far_out=True,
    )
    x = exchange(packed, "xy")
    tile = scalar(lax.axis_index("xy"))
    taps = call(taps_kernel, shape((GROUP, 32), F32), 1.0, conv_weight, scalars=(tile,))

    where = (
        scalar(lax.axis_index("tm")),
        scalar(2 * lax.axis_index("zh") + lax.axis_index("zl")),
    )
    swap = [(0, 1), (1, 0)]
    met = lax.ppermute(pooled, "zl", swap)
    couple = call(couple_kernel, shape((SLOT, D), BF16), 1.0, pooled, met, scalars=where[1:])
    came = [couple]
    for n in range(1, PAIRS):
        came.append(lax.ppermute(couple, "zh", [(i, (i + n) % PAIRS) for i in range(PAIRS)]))
    by_tile = shape((TILES, PAIRS * SLOT, GROUP), BF16)
    routed = call(route_kernel, by_tile, 1.0, *came, scalars=where[1:])
    agents = exchange(routed, "xy")
    edges = shape((GROUP, EDGE), BF16)
    near, far, turned_q = call(edge_kernel, (edges, edges, shape((GROUP, TILES * TOKENS), BF16)), 1.0, x, scalars=where)
    groups = lax.axis_size("tm")
    pairs = [(i, i + 1) for i in range(0, groups - 1, 2)]
    near = lax.ppermute(near, "tm", pairs + [(b, a) for a, b in pairs])
    pairs = [(i, i + 1) for i in range(1, groups - 1, 2)]
    far = lax.ppermute(far, "tm", pairs + [(b, a) for a, b in pairs])
    keep, send = call(
        agent_kernel, (shape((GROUP + 8, HALF), F32), shape((GROUP + STATS, HALF), BF16)), 3.0, agents, x, scalars=where
    )
    theirs = lax.ppermute(send, "zl", swap)
    row = shape((GROUP, TOKENS), BF16)
    cross, kin = call(rim_kernel, (row, row), 1.0, x, near, far, taps, scalars=where)
    blended, longer = call(
        blend_kernel,
        (shape((GROUP + STATS, HALF), BF16), shape((2 * GROUP + STATS, HALF), BF16)),
        1.0,
        keep,
        theirs,
        cross,
    )
    parts = [blended]
    for n in range(1, PAIRS):
        to = [2 * ((i // 2 + n) % PAIRS) + (i + n) % 2 for i in range(PLANES)]
        moved = longer if n % 2 else blended
        parts.append(lax.ppermute(moved, ("zh", "zl"), list(enumerate(to))))
    local = call(conv_kernel, shape((TILES, GROUP, TOKENS), F32), 5.0, x, near, far, taps, scalars=where)
    ours = call(comb_kernel, shape((2 * GROUP, HALF), BF16), 1.0, *parts, kin)
    theirs = lax.ppermute(ours, "zl", swap)
    weights, totals = call(
        query_kernel,
        (shape((GROUP_HEADS, AGENTS, TILES * TOKENS), BF16), shape((8, TILES * TOKENS), F32)),
        2.0,
        agents,
        turned_q,
    )
    mixed = call(
        mix_kernel,
        shape((TILES, GROUP, TOKENS), BF16),
        1.0,
        weights,
        totals,
        ours,
        theirs,
        parts[1],
        parts[3],
        local,
        scalars=where,
    )
    mine = exchange(mixed, "xy")
    pieces = TILES // 2
    out = call(
        unpack_kernel,
        shape((TOKENS, D), BF16),
        1.0,
        mine,
        scratch=(
            pltpu.VMEM((pieces, TOKENS, D // pieces), BF16),
            pltpu.SemaphoreType.DMA((pieces,)),
        ),
        far_out=True,
    )
    return out.reshape(value_states.shape)


def solution(mesh):
    devices = mesh.devices
    fine = Mesh(devices.reshape(devices.shape[0], PAIRS, 2, TILES), ("tm", "zh", "zl", "xy"))
    spec = P("tm", None, ("zh", "zl", "xy"), None, None)
    return jax.shard_map(
        body,
        mesh=fine,
        in_specs=(spec, spec, spec, P()),
        out_specs=spec,
        check_vma=False,
    )
```

```python
import jax
import jax.numpy as jnp
from jax import lax
from jax.experimental import pallas as pl
from jax.experimental.pallas import tpu as pltpu
from jax.sharding import Mesh
from jax.sharding import PartitionSpec as P


HEADS = 24
HEAD_DIM = 64
D = 1536
FRAMES = 4
COLUMNS = 32
TOKENS = FRAMES * COLUMNS
AGENT_DEV = 4
PAIRS = 4
PLANES = 2 * PAIRS
TILES = 8
AGENTS = 256
SLOT = 8
HALF = AGENTS // 2
GROUP_HEADS = HEADS // TILES
GROUP = GROUP_HEADS * HEAD_DIM
K_ROW = GROUP
V_ROW = 2 * GROUP
SENT = 3 * GROUP
EDGE = TILES * COLUMNS
STATS = 16
GRANT = 6 * 1024 * 1024
ALL = 60 * 1024 * 1024
INV_ROOT = HEAD_DIM ** (-0.5)
F32 = jnp.float32
BF16 = jnp.bfloat16


VMEM = pl.BlockSpec(memory_space=pltpu.VMEM)

SMEM = pl.BlockSpec(memory_space=pltpu.SMEM)
HBM = pl.BlockSpec(memory_space=pltpu.HBM)


def call(kernel, out_shape, us, *args, scalars=(), scratch=(), far=False, far_out=False):
    cost = pl.CostEstimate(flops=int(us * 3.0e8), bytes_accessed=int(us * 2.0e6), transcendentals=0)
    first = HBM if far_out else VMEM
    several = isinstance(out_shape, tuple)
    return pl.pallas_call(
        kernel,
        out_shape=out_shape,
        in_specs=[SMEM] * len(scalars) + [HBM if far else VMEM] * len(args),
        out_specs=(first,) + (VMEM,) * (len(out_shape) - 1) if several else first,
        scratch_shapes=list(scratch),
        cost_estimate=cost,
        compiler_params=pltpu.CompilerParams(vmem_limit_bytes=ALL if far else GRANT),
    )(*scalars, *args)


def exchange(x, axes):
    return lax.all_to_all(x, axes, 0, 0)


def pack_kernel(q_ref, k_ref, v_ref, out_ref, pooled_ref, came, turned, in_sems, out_sems):
    refs = (q_ref, k_ref, v_ref)
    loads = [pltpu.make_async_copy(ref, came.at[n], in_sems.at[n]) for n, ref in enumerate(refs)]
    for load in loads:
        load.start()
    stores = []
    for n, load in enumerate(loads):
        load.wait()
        flipped = came[n].T
        for tile in range(TILES):
            turned[n, tile] = flipped[tile * GROUP : (tile + 1) * GROUP]
        rows = pl.ds(n * GROUP, GROUP)
        store = pltpu.make_async_copy(turned.at[n], out_ref.at[:, rows, :], out_sems.at[n])
        store.start()
        stores.append(store)
    shape = (SLOT, TOKENS)
    token = lax.broadcasted_iota(jnp.int32, shape, 1)
    agent = lax.broadcasted_iota(jnp.int32, shape, 0)
    width = COLUMNS // AGENT_DEV
    pick = ((token % COLUMNS) // width == agent).astype(F32).astype(BF16)
    sums = jnp.dot(pick, came[0], preferred_element_type=F32)
    pooled_ref[...] = (sums * (1.0 / (FRAMES * width))).astype(BF16)
    for store in stores:
        store.wait()


def rows_of(x_ref, start, size):
    return jnp.concatenate([x_ref[s, start : start + size, :] for s in range(TILES)], axis=1)


def couple_kernel(z_ref, ours_ref, theirs_ref, out_ref):
    ours, theirs = ours_ref[...].astype(F32), theirs_ref[...].astype(F32)
    second = lax.rem(z_ref[0], 2) == 1
    low, high = jnp.where(second, theirs, ours), jnp.where(second, ours, theirs)
    out_ref[...] = (low + pltpu.roll(high, AGENT_DEV, 0)).astype(BF16)


def route_kernel(z_ref, *refs):
    came, out_ref = refs[:PAIRS], refs[PAIRS]
    rows = jnp.concatenate([ref[...].astype(F32) for ref in came], axis=0).astype(BF16)
    shape = (PAIRS * SLOT, PAIRS * SLOT)
    to = lax.broadcasted_iota(jnp.int32, shape, 0)
    at = lax.broadcasted_iota(jnp.int32, shape, 1)
    hop = (z_ref[0] // 2 + PAIRS - to // SLOT) % PAIRS
    pick = (at == hop * SLOT + to % SLOT).astype(F32).astype(BF16)
    agents = jnp.dot(pick, rows, preferred_element_type=F32).astype(BF16)
    for tile in range(TILES):
        out_ref[tile] = agents[:, tile * GROUP : (tile + 1) * GROUP]


def agent_kernel(tm_ref, z_ref, a_ref, x_ref, keep_ref, send_ref):
    low = lax.rem(z_ref[0] // 2 + z_ref[0], 2) == 0
    everyone = a_ref[...].reshape(AGENTS, GROUP)
    columns = []
    logs = []
    for h in range(GROUP_HEADS):
        keys = rows_of(x_ref, K_ROW + h * HEAD_DIM, HEAD_DIM)
        values = rows_of(x_ref, V_ROW + h * HEAD_DIM, HEAD_DIM)
        agents = everyone[:, h * HEAD_DIM : (h + 1) * HEAD_DIM]
        scores = jnp.dot(agents, keys, preferred_element_type=F32) * INV_ROOT
        peak = jnp.max(scores, axis=1, keepdims=True)
        weights = jnp.exp(scores - peak)
        total = jnp.sum(weights, axis=1, keepdims=True)
        acc = lax.dot_general(
            weights.astype(BF16), values, (((1,), (1,)), ((), ())), preferred_element_type=F32
        )
        columns.append(acc / total)
        logs.append(peak + jnp.log(total))
    lane = lax.broadcasted_iota(jnp.int32, (AGENTS, HEAD_DIM), 1)
    stats = jnp.zeros((AGENTS, HEAD_DIM), F32)
    for h, log in enumerate(logs):
        stats = jnp.where(lane == h, log, stats)
    part = jnp.concatenate(columns + [stats], axis=1).T
    near, far = part[:, :HALF], part[:, HALF:]
    keep_ref[...] = jnp.where(low, near, far)[: GROUP + 8]
    away = jnp.where(low, far, near)
    send_ref[:GROUP] = away[:GROUP].astype(BF16)
    send_ref[GROUP:] = pieces_of(away[GROUP : GROUP + GROUP_HEADS])


def pieces_of(logs):
    pieces = []
    for _ in range(3):
        short = logs.astype(BF16).astype(F32)
        logs = logs - short
        pieces.append(short)
    pieces.append(jnp.zeros((STATS - 3 * GROUP_HEADS, HALF), F32))
    return jnp.concatenate(pieces, axis=0).astype(BF16)


def logs_of(pieces):
    n = GROUP_HEADS
    pieces = pieces.astype(F32)
    return pieces[:n] + pieces[n : 2 * n] + pieces[2 * n : 3 * n]


def blend_kernel(keep_ref, came_ref, cross_ref, out_ref, long_ref):
    ours, theirs = keep_ref[GROUP : GROUP + GROUP_HEADS, :], logs_of(came_ref[GROUP:, :])
    peak = jnp.maximum(ours, theirs)
    left, right = jnp.exp(ours - peak), jnp.exp(theirs - peak)
    whole = left + right
    left, right = left / whole, right / whole
    stats = pieces_of(peak + jnp.log(whole))
    for h in range(GROUP_HEADS):
        rows = slice(h * HEAD_DIM, (h + 1) * HEAD_DIM)
        part = keep_ref[rows, :] * left[h : h + 1] + came_ref[rows, :].astype(F32) * right[h : h + 1]
        part = part.astype(BF16)
        out_ref[rows, :] = part
        long_ref[rows, :] = part
    out_ref[GROUP:, :] = stats
    long_ref[GROUP : GROUP + STATS, :] = stats
    long_ref[GROUP + STATS :, :] = cross_ref[...]


def comb_kernel(*refs):
    parts, (kin_ref, out_ref) = refs[:PAIRS], refs[PAIRS:]
    out_ref[GROUP:, :] = kin_ref[...]
    logs = [logs_of(part[GROUP : GROUP + STATS, :]) for part in parts]
    peak = logs[0]
    for log in logs[1:]:
        peak = jnp.maximum(peak, log)
    shares = [jnp.exp(log - peak) for log in logs]
    whole = sum(shares[1:], shares[0])
    shares = [share / whole for share in shares]
    for h in range(GROUP_HEADS):
        rows = slice(h * HEAD_DIM, (h + 1) * HEAD_DIM)
        terms = [
            part[rows, :].astype(F32) * share[h : h + 1]
            for part, share in zip(parts, shares, strict=True)
        ]
        out_ref[rows, :] = sum(terms[1:], terms[0]).astype(BF16)


def taps_kernel(tile_ref, w_ref, out_ref):
    for tile in range(TILES):

        @pl.when(tile_ref[0] == tile)
        def _(tile=tile):
            lanes = slice(tile * GROUP, (tile + 1) * GROUP)
            rows = [w_ref[i, j, :, lanes] for i in range(3) for j in range(3)]
            rows.append(jnp.zeros((5, GROUP), F32))
            out_ref[...] = jnp.concatenate(rows, axis=0).T


def edge_kernel(tm_ref, z_ref, x_ref, near_ref, far_ref, q_ref):
    q_ref[...] = rows_of(x_ref, 0, GROUP)
    spot = lax.broadcasted_iota(jnp.int32, (GROUP, TOKENS), 1) // COLUMNS
    for block in range(EDGE // TOKENS):
        last = first = jnp.zeros((GROUP, TOKENS), F32)
        for j in range(FRAMES):
            cells = x_ref[block * FRAMES + j, V_ROW:, :].astype(F32)
            late = cells if j == FRAMES - 1 else pltpu.roll(cells, (j + 1) * COLUMNS, 1)
            early = cells if j == 0 else pltpu.roll(cells, j * COLUMNS, 1)
            last = jnp.where(spot == j, late, last)
            first = jnp.where(spot == j, early, first)
        lanes = slice(block * TOKENS, (block + 1) * TOKENS)
        last, first = last.astype(BF16), first.astype(BF16)

        @pl.when(lax.rem(tm_ref[0], 2) == 0)
        def _(last=last, first=first, lanes=lanes):
            near_ref[:, lanes] = last
            far_ref[:, lanes] = first

        @pl.when(lax.rem(tm_ref[0], 2) != 0)
        def _(last=last, first=first, lanes=lanes):
            near_ref[:, lanes] = first
            far_ref[:, lanes] = last


TALL = 16


def turned(cells, by):
    by %= TOKENS
    return cells if by == 0 else pltpu.roll(cells, by, 1)


def frames_of(r, at, even, x_ref, near_ref, far_ref, tall=TALL):
    lane = lax.broadcasted_iota(jnp.int32, (tall, TOKENS), 1)
    cells = x_ref[r, pl.ds(V_ROW + at, tall), :].astype(F32)
    block, j = divmod(r, FRAMES)
    lanes = slice(block * TOKENS, (block + 1) * TOKENS)
    near = near_ref[pl.ds(at, tall), lanes].astype(F32)
    far = far_ref[pl.ds(at, tall), lanes].astype(F32)
    before = turned(jnp.where(even, far, near), -j * COLUMNS)
    after = turned(jnp.where(even, near, far), (FRAMES - 1 - j) * COLUMNS)
    return (
        jnp.where(lane < COLUMNS, before, turned(cells, COLUMNS)),
        cells,
        jnp.where(lane >= TOKENS - COLUMNS, after, turned(cells, -COLUMNS)),
    )


def taps_of(w_ref, at, rows=range(3), tall=TALL):
    w = w_ref[pl.ds(at, tall), :]
    return {
        (i, j, k): jnp.broadcast_to(w[:, n : n + 1], (tall, TOKENS))
        for i in range(3)
        for j in rows
        for k in range(3)
        for n in (i * 9 + j * 3 + k,)
    }


def stencil(rows, taps):
    shape = next(iter(rows.values()))[1].shape
    column = lax.broadcasted_iota(jnp.int32, shape, 1) % COLUMNS
    sums = []
    for k in range(3):
        total = None
        for j, frames in rows.items():
            for i in range(3):
                term = frames[i] * taps[i, j, k]
                total = term if total is None else total + term
        sums.append(total)
    left = jnp.where(column == 0, 0.0, pltpu.roll(sums[0], 1, 1))
    right = jnp.where(column == COLUMNS - 1, 0.0, pltpu.roll(sums[2], TOKENS - 1, 1))
    return left + sums[1] + right


def rim_kernel(tm_ref, z_ref, x_ref, near_ref, far_ref, w_ref, cross_ref, kin_ref):
    even, second = lax.rem(tm_ref[0], 2) == 0, lax.rem(z_ref[0], 2) == 1
    tall = GROUP // 2
    for at in range(0, GROUP, tall):
        sums = []
        for r, j in ((TILES - 1, 0), (0, 2)):
            frames = frames_of(r, at, even, x_ref, near_ref, far_ref, tall)
            sums.append(stencil({j: frames}, taps_of(w_ref, at, (j,), tall)).astype(BF16))
        cross_ref[pl.ds(at, tall), :] = jnp.where(second, sums[0], sums[1])
        kin_ref[pl.ds(at, tall), :] = jnp.where(second, sums[1], sums[0])


def conv_kernel(tm_ref, z_ref, x_ref, near_ref, far_ref, w_ref, out_ref):
    even = lax.rem(tm_ref[0], 2) == 0

    def step(n, carry):
        at = pl.multiple_of(n * TALL, TALL)
        taps = taps_of(w_ref, at)
        rows = {0: frames_of(0, at, even, x_ref, near_ref, far_ref)}
        for r in range(TILES):
            if r + 1 < TILES:
                rows[r + 1] = frames_of(r + 1, at, even, x_ref, near_ref, far_ref)
            near = {j: rows[r + j - 1] for j in range(3) if r + j - 1 in rows}
            out_ref[r, pl.ds(at, TALL), :] = stencil(near, taps)
            rows.pop(r - 1, None)
        return carry

    lax.fori_loop(0, GROUP // TALL, step, 0)


def query_kernel(a_ref, q_ref, e_ref, total_ref):
    agents = a_ref[...].reshape(AGENTS, GROUP)
    for h in range(GROUP_HEADS):
        rows = slice(h * HEAD_DIM, (h + 1) * HEAD_DIM)
        scores = jnp.dot(agents[:, rows], q_ref[rows, :], preferred_element_type=F32) * INV_ROOT
        weights = jnp.exp(scores - jnp.max(scores, axis=0, keepdims=True))
        total_ref[h : h + 1, :] = jnp.sum(weights, axis=0, keepdims=True)
        e_ref[h] = weights.astype(BF16)


def mix_kernel(tm_ref, z_ref, e_ref, total_ref, ours_ref, theirs_ref, one_ref, three_ref, local_ref, out_ref):
    low, second = lax.rem(z_ref[0] // 2 + z_ref[0], 2) == 0, lax.rem(z_ref[0], 2) == 1
    odd = lax.rem(tm_ref[0], 2)
    first, last = z_ref[0] == (PLANES - 1) * odd, z_ref[0] == PLANES - 1 - odd
    ours, theirs = ours_ref[:GROUP], theirs_ref[:GROUP]
    values = jnp.concatenate(
        [jnp.where(low, ours, theirs), jnp.where(low, theirs, ours)], axis=1
    )
    kin = theirs_ref[GROUP:].astype(F32)
    one, three = one_ref[GROUP + STATS :].astype(F32), three_ref[GROUP + STATS :].astype(F32)
    above, below = jnp.where(odd == 1, three, one), jnp.where(odd == 1, one, three)
    above = jnp.where(first, 0.0, jnp.where(second, kin, above))
    below = jnp.where(last, 0.0, jnp.where(second, below, kin))
    for h in range(GROUP_HEADS):
        rows = slice(h * HEAD_DIM, (h + 1) * HEAD_DIM)
        mixed = jnp.dot(values[rows], e_ref[h], preferred_element_type=F32)
        mixed = mixed / total_ref[h : h + 1, :]
        for s in range(TILES):
            cells = mixed[:, s * TOKENS : (s + 1) * TOKENS] + local_ref[s, rows, :]
            if s == 0:
                cells += above[rows]
            if s == TILES - 1:
                cells += below[rows]
            out_ref[s, rows, :] = cells.astype(BF16)


def unpack_kernel(x_ref, out_ref, back, sems):
    pieces, stores = TILES // 2, []
    wide = D // pieces
    for n in range(pieces):
        back[n] = x_ref[2 * n : 2 * n + 2].reshape(wide, TOKENS).T
        store = pltpu.make_async_copy(back.at[n], out_ref.at[:, pl.ds(n * wide, wide)], sems.at[n])
        store.start()
        stores.append(store)
    for store in stores:
        store.wait()


LINE = ("tm", "zh", "zl")


def along(step):
    pairs = []
    for group in range(lax.axis_size("tm")):
        odd = group % 2
        for z in range(PLANES):
            to = (step((z - odd) % PLANES, odd) + odd) % PLANES
            pairs.append((group * PLANES + z, group * PLANES + to))
    return pairs


def pair_plane(at, odd):
    return at ^ 1


def same_side(at, n):
    return 2 * ((at // 2 + n) % PAIRS) + at % 2


def other_side(at, n):
    return 2 * ((at // 2 + n) % PAIRS) + (at + n) % 2


def scalar(x):
    return x.astype(jnp.int32).reshape(1)


def body(queries, key_states, value_states, conv_weight):
    q = queries.reshape(TOKENS, D)
    k = key_states.reshape(TOKENS, D)
    v = value_states.reshape(TOKENS, D)
    shape = jax.ShapeDtypeStruct
    packed, pooled = call(
        pack_kernel,
        (shape((TILES, SENT, TOKENS), BF16), shape((SLOT, D), BF16)),
        3.0,
        q,
        k,
        v,
        scratch=(
            pltpu.VMEM((3, TOKENS, D), BF16),
            pltpu.VMEM((3, TILES, GROUP, TOKENS), BF16),
            pltpu.SemaphoreType.DMA((3,)),
            pltpu.SemaphoreType.DMA((3,)),
        ),
        far=True,
        far_out=True,
    )
    x = exchange(packed, "xy")
    tile = scalar(lax.axis_index("xy"))
    taps = call(taps_kernel, shape((GROUP, 32), F32), 1.0, conv_weight, scalars=(tile,))

    tm = lax.axis_index("tm")
    where = (
        scalar(tm),
        scalar((2 * lax.axis_index("zh") + lax.axis_index("zl") + 7 * (tm & 1)) & 7),
    )
    met = lax.ppermute(pooled, LINE, along(pair_plane))
    couple = call(couple_kernel, shape((SLOT, D), BF16), 1.0, pooled, met, scalars=where[1:])
    came = [couple]
    for n in range(1, PAIRS):
        came.append(lax.ppermute(couple, LINE, along(lambda at, odd: same_side(at, n))))
    by_tile = shape((TILES, PAIRS * SLOT, GROUP), BF16)
    routed = call(route_kernel, by_tile, 1.0, *came, scalars=where[1:])
    agents = exchange(routed, "xy")
    edges = shape((GROUP, EDGE), BF16)
    near, far, turned_q = call(
        edge_kernel, (edges, edges, shape((GROUP, TILES * TOKENS), BF16)), 1.0, x, scalars=where
    )
    groups = lax.axis_size("tm")
    pairs = [(i, i + 1) for i in range(0, groups - 1, 2)]
    near = lax.ppermute(near, "tm", pairs + [(b, a) for a, b in pairs])
    pairs = [(i, i + 1) for i in range(1, groups - 1, 2)]
    far = lax.ppermute(far, "tm", pairs + [(b, a) for a, b in pairs])
    keep, send = call(
        agent_kernel,
        (shape((GROUP + 8, HALF), F32), shape((GROUP + STATS, HALF), BF16)),
        3.0,
        agents,
        x,
        scalars=where,
    )
    theirs = lax.ppermute(send, LINE, along(pair_plane))
    row = shape((GROUP, TOKENS), BF16)
    cross, kin = call(rim_kernel, (row, row), 1.0, x, near, far, taps, scalars=where)
    blended, longer = call(
        blend_kernel,
        (shape((GROUP + STATS, HALF), BF16), shape((2 * GROUP + STATS, HALF), BF16)),
        1.0,
        keep,
        theirs,
        cross,
    )
    parts = [blended]
    for n in range(1, PAIRS):
        moved = longer if n % 2 else blended
        parts.append(
            lax.ppermute(moved, LINE, along(lambda at, odd: other_side(at, -n if odd else n)))
        )
    local = call(
        conv_kernel, shape((TILES, GROUP, TOKENS), F32), 5.0, x, near, far, taps, scalars=where
    )
    ours = call(comb_kernel, shape((2 * GROUP, HALF), BF16), 1.0, *parts, kin)
    theirs = lax.ppermute(ours, LINE, along(pair_plane))
    weights, totals = call(
        query_kernel,
        (shape((GROUP_HEADS, AGENTS, TILES * TOKENS), BF16), shape((8, TILES * TOKENS), F32)),
        2.0,
        agents,
        turned_q,
    )
    mixed = call(
        mix_kernel,
        shape((TILES, GROUP, TOKENS), BF16),
        1.0,
        weights,
        totals,
        ours,
        theirs,
        parts[1],
        parts[3],
        local,
        scalars=where,
    )
    mine = exchange(mixed, "xy")
    pieces = TILES // 2
    out = call(
        unpack_kernel,
        shape((TOKENS, D), BF16),
        1.0,
        mine,
        scratch=(
            pltpu.VMEM((pieces, TOKENS, D // pieces), BF16),
            pltpu.SemaphoreType.DMA((pieces,)),
        ),
        far_out=True,
    )
    return out.reshape(value_states.shape)


def solution(mesh):
    devices = mesh.devices
    fine = Mesh(devices.reshape(devices.shape[0], PAIRS, 2, TILES), ("tm", "zh", "zl", "xy"))
    spec = P("tm", None, ("zh", "zl", "xy"), None, None)
    return jax.shard_map(
        body,
        mesh=fine,
        in_specs=(spec, spec, spec, P()),
        out_specs=spec,
        check_vma=False,
    )
```

```python
import jax
import jax.numpy as jnp
from jax import lax
from jax.experimental import pallas as pl
from jax.experimental.pallas import tpu as pltpu
from jax.sharding import Mesh
from jax.sharding import PartitionSpec as P


HEADS = 24
HEAD_DIM = 64
D = 1536
FRAMES = 4
COLUMNS = 32
TOKENS = FRAMES * COLUMNS
AGENT_DEV = 4
PAIRS = 4
PLANES = 2 * PAIRS
TILES = 8
AGENTS = 256
SLOT = 8
HALF = AGENTS // 2
GROUP_HEADS = HEADS // TILES
GROUP = GROUP_HEADS * HEAD_DIM
K_ROW = GROUP
V_ROW = 2 * GROUP
SENT = 3 * GROUP
EDGE = TILES * COLUMNS
STATS = 16
GRANT = 6 * 1024 * 1024
ALL = 60 * 1024 * 1024
INV_ROOT = HEAD_DIM ** (-0.5)
F32 = jnp.float32
BF16 = jnp.bfloat16


VMEM = pl.BlockSpec(memory_space=pltpu.VMEM)

SMEM = pl.BlockSpec(memory_space=pltpu.SMEM)
HBM = pl.BlockSpec(memory_space=pltpu.HBM)


def call(kernel, out_shape, us, *args, scalars=(), scratch=(), far=False, far_out=False):
    cost = pl.CostEstimate(flops=int(us * 3.0e8), bytes_accessed=int(us * 2.0e6), transcendentals=0)
    first = HBM if far_out else VMEM
    several = isinstance(out_shape, tuple)
    return pl.pallas_call(
        kernel,
        out_shape=out_shape,
        in_specs=[SMEM] * len(scalars) + [HBM if far else VMEM] * len(args),
        out_specs=(first,) + (VMEM,) * (len(out_shape) - 1) if several else first,
        scratch_shapes=list(scratch),
        cost_estimate=cost,
        compiler_params=pltpu.CompilerParams(vmem_limit_bytes=ALL if far else GRANT),
    )(*scalars, *args)


def exchange(x, axes):
    return lax.all_to_all(x, axes, 0, 0)


def pack_kernel(q_ref, k_ref, v_ref, out_ref, pooled_ref, came, turned, in_sems, out_sems):
    refs = (q_ref, k_ref, v_ref)
    loads = [pltpu.make_async_copy(ref, came.at[n], in_sems.at[n]) for n, ref in enumerate(refs)]
    for load in loads:
        load.start()
    stores = []
    for n, load in enumerate(loads):
        load.wait()
        flipped = came[n].T
        for tile in range(TILES):
            turned[n, tile] = flipped[tile * GROUP : (tile + 1) * GROUP]
        rows = pl.ds(n * GROUP, GROUP)
        store = pltpu.make_async_copy(turned.at[n], out_ref.at[:, rows, :], out_sems.at[n])
        store.start()
        stores.append(store)
    width = COLUMNS // AGENT_DEV
    cells = came[0].astype(F32).reshape(FRAMES, AGENT_DEV, width, D)
    means = jnp.sum(jnp.sum(cells, axis=0), axis=1) * (1.0 / (FRAMES * width))
    pooled_ref[...] = jnp.concatenate([means, jnp.zeros_like(means)], axis=0).astype(BF16)
    for store in stores:
        store.wait()


def rows_of(x_ref, start, size):
    return jnp.concatenate([x_ref[s, start : start + size, :] for s in range(TILES)], axis=1)


def couple_kernel(z_ref, ours_ref, theirs_ref, out_ref):
    ours, theirs = ours_ref[...].astype(F32), theirs_ref[...].astype(F32)
    second = lax.rem(z_ref[0], 2) == 1
    low, high = jnp.where(second, theirs, ours), jnp.where(second, ours, theirs)
    out_ref[...] = (low + pltpu.roll(high, AGENT_DEV, 0)).astype(BF16)


def route_kernel(z_ref, *refs):
    came, out_ref = refs[:PAIRS], refs[PAIRS]
    slots = [ref[...].astype(F32) for ref in came]
    rows = []
    for pair in range(PAIRS):
        hop = (z_ref[0] // 2 + PAIRS - pair) % PAIRS
        row = slots[0]
        for n in range(1, PAIRS):
            row = jnp.where(hop == n, slots[n], row)
        rows.append(row)
    agents = jnp.concatenate(rows, axis=0).astype(BF16)
    for tile in range(TILES):
        out_ref[tile] = agents[:, tile * GROUP : (tile + 1) * GROUP]


def agent_kernel(tm_ref, z_ref, a_ref, x_ref, keep_ref, send_ref):
    low = lax.rem(z_ref[0] // 2 + z_ref[0], 2) == 0
    everyone = a_ref[...].reshape(AGENTS, GROUP)
    columns = []
    logs = []
    for h in range(GROUP_HEADS):
        keys = rows_of(x_ref, K_ROW + h * HEAD_DIM, HEAD_DIM)
        values = rows_of(x_ref, V_ROW + h * HEAD_DIM, HEAD_DIM)
        agents = everyone[:, h * HEAD_DIM : (h + 1) * HEAD_DIM]
        scores = jnp.dot(agents, keys, preferred_element_type=F32) * INV_ROOT
        peak = jnp.max(scores, axis=1, keepdims=True)
        weights = jnp.exp(scores - peak)
        total = jnp.sum(weights, axis=1, keepdims=True)
        acc = lax.dot_general(
            weights.astype(BF16), values, (((1,), (1,)), ((), ())), preferred_element_type=F32
        )
        columns.append(acc / total)
        logs.append(peak + jnp.log(total))
    lane = lax.broadcasted_iota(jnp.int32, (AGENTS, HEAD_DIM), 1)
    stats = jnp.zeros((AGENTS, HEAD_DIM), F32)
    for h, log in enumerate(logs):
        stats = jnp.where(lane == h, log, stats)
    part = jnp.concatenate(columns + [stats], axis=1).T
    near, far = part[:, :HALF], part[:, HALF:]
    keep_ref[...] = jnp.where(low, near, far)[: GROUP + 8]
    away = jnp.where(low, far, near)
    send_ref[:GROUP] = away[:GROUP].astype(BF16)
    send_ref[GROUP:] = pieces_of(away[GROUP : GROUP + GROUP_HEADS])


def pieces_of(logs):
    pieces = []
    for _ in range(3):
        short = logs.astype(BF16).astype(F32)
        logs = logs - short
        pieces.append(short)
    pieces.append(jnp.zeros((STATS - 3 * GROUP_HEADS, HALF), F32))
    return jnp.concatenate(pieces, axis=0).astype(BF16)


def logs_of(pieces):
    n = GROUP_HEADS
    pieces = pieces.astype(F32)
    return pieces[:n] + pieces[n : 2 * n] + pieces[2 * n : 3 * n]


def blend_kernel(keep_ref, came_ref, cross_ref, out_ref, long_ref):
    ours, theirs = keep_ref[GROUP : GROUP + GROUP_HEADS, :], logs_of(came_ref[GROUP:, :])
    peak = jnp.maximum(ours, theirs)
    left, right = jnp.exp(ours - peak), jnp.exp(theirs - peak)
    whole = left + right
    left, right = left / whole, right / whole
    stats = pieces_of(peak + jnp.log(whole))
    for h in range(GROUP_HEADS):
        rows = slice(h * HEAD_DIM, (h + 1) * HEAD_DIM)
        part = keep_ref[rows, :] * left[h : h + 1] + came_ref[rows, :].astype(F32) * right[h : h + 1]
        part = part.astype(BF16)
        out_ref[rows, :] = part
        long_ref[rows, :] = part
    out_ref[GROUP:, :] = stats
    long_ref[GROUP : GROUP + STATS, :] = stats
    long_ref[GROUP + STATS :, :] = cross_ref[...]


def comb_kernel(*refs):
    parts, (kin_ref, out_ref) = refs[:PAIRS], refs[PAIRS:]
    out_ref[GROUP:, :] = kin_ref[...]
    logs = [logs_of(part[GROUP : GROUP + STATS, :]) for part in parts]
    peak = logs[0]
    for log in logs[1:]:
        peak = jnp.maximum(peak, log)
    shares = [jnp.exp(log - peak) for log in logs]
    whole = sum(shares[1:], shares[0])
    shares = [share / whole for share in shares]
    for h in range(GROUP_HEADS):
        rows = slice(h * HEAD_DIM, (h + 1) * HEAD_DIM)
        terms = [
            part[rows, :].astype(F32) * share[h : h + 1]
            for part, share in zip(parts, shares, strict=True)
        ]
        out_ref[rows, :] = sum(terms[1:], terms[0]).astype(BF16)


def taps_kernel(tile_ref, w_ref, out_ref):
    for tile in range(TILES):

        @pl.when(tile_ref[0] == tile)
        def _(tile=tile):
            lanes = slice(tile * GROUP, (tile + 1) * GROUP)
            rows = [w_ref[i, j, :, lanes] for i in range(3) for j in range(3)]
            rows.append(jnp.zeros((5, GROUP), F32))
            out_ref[...] = jnp.concatenate(rows, axis=0).T


def edge_kernel(tm_ref, z_ref, x_ref, near_ref, far_ref, q_ref):
    q_ref[...] = rows_of(x_ref, 0, GROUP)
    spot = lax.broadcasted_iota(jnp.int32, (GROUP, TOKENS), 1) // COLUMNS
    for block in range(EDGE // TOKENS):
        last = first = jnp.zeros((GROUP, TOKENS), F32)
        for j in range(FRAMES):
            cells = x_ref[block * FRAMES + j, V_ROW:, :].astype(F32)
            late = cells if j == FRAMES - 1 else pltpu.roll(cells, (j + 1) * COLUMNS, 1)
            early = cells if j == 0 else pltpu.roll(cells, j * COLUMNS, 1)
            last = jnp.where(spot == j, late, last)
            first = jnp.where(spot == j, early, first)
        lanes = slice(block * TOKENS, (block + 1) * TOKENS)
        last, first = last.astype(BF16), first.astype(BF16)

        @pl.when(lax.rem(tm_ref[0], 2) == 0)
        def _(last=last, first=first, lanes=lanes):
            near_ref[:, lanes] = last
            far_ref[:, lanes] = first

        @pl.when(lax.rem(tm_ref[0], 2) != 0)
        def _(last=last, first=first, lanes=lanes):
            near_ref[:, lanes] = first
            far_ref[:, lanes] = last


TALL = 16


def turned(cells, by):
    by %= TOKENS
    return cells if by == 0 else pltpu.roll(cells, by, 1)


def frames_of(r, at, even, x_ref, near_ref, far_ref, tall=TALL):
    lane = lax.broadcasted_iota(jnp.int32, (tall, TOKENS), 1)
    cells = x_ref[r, pl.ds(V_ROW + at, tall), :].astype(F32)
    block, j = divmod(r, FRAMES)
    lanes = slice(block * TOKENS, (block + 1) * TOKENS)
    near = near_ref[pl.ds(at, tall), lanes].astype(F32)
    far = far_ref[pl.ds(at, tall), lanes].astype(F32)
    before = turned(jnp.where(even, far, near), -j * COLUMNS)
    after = turned(jnp.where(even, near, far), (FRAMES - 1 - j) * COLUMNS)
    return (
        jnp.where(lane < COLUMNS, before, turned(cells, COLUMNS)),
        cells,
        jnp.where(lane >= TOKENS - COLUMNS, after, turned(cells, -COLUMNS)),
    )


def taps_of(w_ref, at, rows=range(3), tall=TALL):
    w = w_ref[pl.ds(at, tall), :]
    return {
        (i, j, k): jnp.broadcast_to(w[:, n : n + 1], (tall, TOKENS))
        for i in range(3)
        for j in rows
        for k in range(3)
        for n in (i * 9 + j * 3 + k,)
    }


def stencil(rows, taps):
    shape = next(iter(rows.values()))[1].shape
    column = lax.broadcasted_iota(jnp.int32, shape, 1) % COLUMNS
    sums = []
    for k in range(3):
        total = None
        for j, frames in rows.items():
            for i in range(3):
                term = frames[i] * taps[i, j, k]
                total = term if total is None else total + term
        sums.append(total)
    left = jnp.where(column == 0, 0.0, pltpu.roll(sums[0], 1, 1))
    right = jnp.where(column == COLUMNS - 1, 0.0, pltpu.roll(sums[2], TOKENS - 1, 1))
    return left + sums[1] + right


def rim_kernel(tm_ref, z_ref, x_ref, near_ref, far_ref, w_ref, cross_ref, kin_ref):
    even, second = lax.rem(tm_ref[0], 2) == 0, lax.rem(z_ref[0], 2) == 1
    tall = GROUP // 2
    for at in range(0, GROUP, tall):
        sums = []
        for r, j in ((TILES - 1, 0), (0, 2)):
            frames = frames_of(r, at, even, x_ref, near_ref, far_ref, tall)
            sums.append(stencil({j: frames}, taps_of(w_ref, at, (j,), tall)).astype(BF16))
        cross_ref[pl.ds(at, tall), :] = jnp.where(second, sums[0], sums[1])
        kin_ref[pl.ds(at, tall), :] = jnp.where(second, sums[1], sums[0])


def conv_kernel(tm_ref, z_ref, x_ref, near_ref, far_ref, w_ref, out_ref):
    even = lax.rem(tm_ref[0], 2) == 0

    def step(n, carry):
        at = pl.multiple_of(n * TALL, TALL)
        taps = taps_of(w_ref, at)
        rows = {0: frames_of(0, at, even, x_ref, near_ref, far_ref)}
        for r in range(TILES):
            if r + 1 < TILES:
                rows[r + 1] = frames_of(r + 1, at, even, x_ref, near_ref, far_ref)
            near = {j: rows[r + j - 1] for j in range(3) if r + j - 1 in rows}
            out_ref[r, pl.ds(at, TALL), :] = stencil(near, taps)
            rows.pop(r - 1, None)
        return carry

    lax.fori_loop(0, GROUP // TALL, step, 0)


def query_kernel(a_ref, q_ref, e_ref, total_ref):
    agents = a_ref[...].reshape(AGENTS, GROUP)
    for h in range(GROUP_HEADS):
        rows = slice(h * HEAD_DIM, (h + 1) * HEAD_DIM)
        scores = jnp.dot(agents[:, rows], q_ref[rows, :], preferred_element_type=F32) * INV_ROOT
        weights = jnp.exp(scores - jnp.max(scores, axis=0, keepdims=True))
        total_ref[h : h + 1, :] = jnp.sum(weights, axis=0, keepdims=True)
        e_ref[h] = weights.astype(BF16)


def mix_kernel(tm_ref, z_ref, e_ref, total_ref, ours_ref, theirs_ref, one_ref, three_ref, local_ref, out_ref):
    low, second = lax.rem(z_ref[0] // 2 + z_ref[0], 2) == 0, lax.rem(z_ref[0], 2) == 1
    odd = lax.rem(tm_ref[0], 2)
    first, last = z_ref[0] == (PLANES - 1) * odd, z_ref[0] == PLANES - 1 - odd
    ours, theirs = ours_ref[:GROUP], theirs_ref[:GROUP]
    values = jnp.concatenate(
        [jnp.where(low, ours, theirs), jnp.where(low, theirs, ours)], axis=1
    )
    kin = theirs_ref[GROUP:].astype(F32)
    one, three = one_ref[GROUP + STATS :].astype(F32), three_ref[GROUP + STATS :].astype(F32)
    above, below = jnp.where(odd == 1, three, one), jnp.where(odd == 1, one, three)
    above = jnp.where(first, 0.0, jnp.where(second, kin, above))
    below = jnp.where(last, 0.0, jnp.where(second, below, kin))
    for h in range(GROUP_HEADS):
        rows = slice(h * HEAD_DIM, (h + 1) * HEAD_DIM)
        mixed = jnp.dot(values[rows], e_ref[h], preferred_element_type=F32)
        mixed = mixed / total_ref[h : h + 1, :]
        for s in range(TILES):
            cells = mixed[:, s * TOKENS : (s + 1) * TOKENS] + local_ref[s, rows, :]
            if s == 0:
                cells += above[rows]
            if s == TILES - 1:
                cells += below[rows]
            out_ref[s, rows, :] = cells.astype(BF16)


def unpack_kernel(x_ref, out_ref, back, sems):
    pieces, stores = TILES // 2, []
    wide = D // pieces
    for n in range(pieces):
        back[n] = x_ref[2 * n : 2 * n + 2].reshape(wide, TOKENS).T
        store = pltpu.make_async_copy(back.at[n], out_ref.at[:, pl.ds(n * wide, wide)], sems.at[n])
        store.start()
        stores.append(store)
    for store in stores:
        store.wait()


LINE = ("tm", "zh", "zl")


def along(step):
    pairs = []
    for group in range(lax.axis_size("tm")):
        odd = group % 2
        for z in range(PLANES):
            to = (step((z - odd) % PLANES, odd) + odd) % PLANES
            pairs.append((group * PLANES + z, group * PLANES + to))
    return pairs


def pair_plane(at, odd):
    return at ^ 1


def same_side(at, n):
    return 2 * ((at // 2 + n) % PAIRS) + at % 2


def other_side(at, n):
    return 2 * ((at // 2 + n) % PAIRS) + (at + n) % 2


def scalar(x):
    return x.astype(jnp.int32).reshape(1)


def body(queries, key_states, value_states, conv_weight):
    q = queries.reshape(TOKENS, D)
    k = key_states.reshape(TOKENS, D)
    v = value_states.reshape(TOKENS, D)
    shape = jax.ShapeDtypeStruct
    packed, pooled = call(
        pack_kernel,
        (shape((TILES, SENT, TOKENS), BF16), shape((SLOT, D), BF16)),
        3.0,
        q,
        k,
        v,
        scratch=(
            pltpu.VMEM((3, TOKENS, D), BF16),
            pltpu.VMEM((3, TILES, GROUP, TOKENS), BF16),
            pltpu.SemaphoreType.DMA((3,)),
            pltpu.SemaphoreType.DMA((3,)),
        ),
        far=True,
        far_out=True,
    )
    x = exchange(packed, "xy")
    tile = scalar(lax.axis_index("xy"))
    taps = call(taps_kernel, shape((GROUP, 32), F32), 1.0, conv_weight, scalars=(tile,))

    tm = lax.axis_index("tm")
    where = (
        scalar(tm),
        scalar((2 * lax.axis_index("zh") + lax.axis_index("zl") + 7 * (tm & 1)) & 7),
    )
    met = lax.ppermute(pooled, LINE, along(pair_plane))
    couple = call(couple_kernel, shape((SLOT, D), BF16), 1.0, pooled, met, scalars=where[1:])
    came = [couple]
    for n in range(1, PAIRS):
        came.append(lax.ppermute(couple, LINE, along(lambda at, odd: same_side(at, n))))
    by_tile = shape((TILES, PAIRS * SLOT, GROUP), BF16)
    routed = call(route_kernel, by_tile, 1.0, *came, scalars=where[1:])
    agents = exchange(routed, "xy")
    edges = shape((GROUP, EDGE), BF16)
    near, far, turned_q = call(
        edge_kernel, (edges, edges, shape((GROUP, TILES * TOKENS), BF16)), 1.0, x, scalars=where
    )
    groups = lax.axis_size("tm")
    pairs = [(i, i + 1) for i in range(0, groups - 1, 2)]
    near = lax.ppermute(near, "tm", pairs + [(b, a) for a, b in pairs])
    pairs = [(i, i + 1) for i in range(1, groups - 1, 2)]
    far = lax.ppermute(far, "tm", pairs + [(b, a) for a, b in pairs])
    keep, send = call(
        agent_kernel,
        (shape((GROUP + 8, HALF), F32), shape((GROUP + STATS, HALF), BF16)),
        3.0,
        agents,
        x,
        scalars=where,
    )
    theirs = lax.ppermute(send, LINE, along(pair_plane))
    row = shape((GROUP, TOKENS), BF16)
    cross, kin = call(rim_kernel, (row, row), 1.0, x, near, far, taps, scalars=where)
    blended, longer = call(
        blend_kernel,
        (shape((GROUP + STATS, HALF), BF16), shape((2 * GROUP + STATS, HALF), BF16)),
        1.0,
        keep,
        theirs,
        cross,
    )
    parts = [blended]
    for n in range(1, PAIRS):
        moved = longer if n % 2 else blended
        parts.append(
            lax.ppermute(moved, LINE, along(lambda at, odd: other_side(at, -n if odd else n)))
        )
    local = call(
        conv_kernel, shape((TILES, GROUP, TOKENS), F32), 5.0, x, near, far, taps, scalars=where
    )
    ours = call(comb_kernel, shape((2 * GROUP, HALF), BF16), 1.0, *parts, kin)
    theirs = lax.ppermute(ours, LINE, along(pair_plane))
    weights, totals = call(
        query_kernel,
        (shape((GROUP_HEADS, AGENTS, TILES * TOKENS), BF16), shape((8, TILES * TOKENS), F32)),
        2.0,
        agents,
        turned_q,
    )
    mixed = call(
        mix_kernel,
        shape((TILES, GROUP, TOKENS), BF16),
        1.0,
        weights,
        totals,
        ours,
        theirs,
        parts[1],
        parts[3],
        local,
        scalars=where,
    )
    mine = exchange(mixed, "xy")
    pieces = TILES // 2
    out = call(
        unpack_kernel,
        shape((TOKENS, D), BF16),
        1.0,
        mine,
        scratch=(
            pltpu.VMEM((pieces, TOKENS, D // pieces), BF16),
            pltpu.SemaphoreType.DMA((pieces,)),
        ),
        far_out=True,
    )
    return out.reshape(value_states.shape)


def solution(mesh):
    devices = mesh.devices
    fine = Mesh(devices.reshape(devices.shape[0], PAIRS, 2, TILES), ("tm", "zh", "zl", "xy"))
    spec = P("tm", None, ("zh", "zl", "xy"), None, None)
    return jax.shard_map(
        body,
        mesh=fine,
        in_specs=(spec, spec, spec, P()),
        out_specs=spec,
        check_vma=False,
    )
```

```python
import jax
import jax.numpy as jnp
from jax import lax
from jax.experimental import pallas as pl
from jax.experimental.pallas import tpu as pltpu
from jax.sharding import Mesh
from jax.sharding import PartitionSpec as P


HEADS = 24
HEAD_DIM = 64
D = 1536
FRAMES = 4
COLUMNS = 32
TOKENS = FRAMES * COLUMNS
AGENT_DEV = 4
PAIRS = 4
PLANES = 2 * PAIRS
TILES = 8
AGENTS = 256
SLOT = 8
HALF = AGENTS // 2
GROUP_HEADS = HEADS // TILES
GROUP = GROUP_HEADS * HEAD_DIM
K_ROW = GROUP
V_ROW = 2 * GROUP
SENT = 3 * GROUP
EDGE = TILES * COLUMNS
STATS = 16
GRANT = 6 * 1024 * 1024
ALL = 60 * 1024 * 1024
INV_ROOT = HEAD_DIM ** (-0.5)
F32 = jnp.float32
BF16 = jnp.bfloat16


VMEM = pl.BlockSpec(memory_space=pltpu.VMEM)

SMEM = pl.BlockSpec(memory_space=pltpu.SMEM)
HBM = pl.BlockSpec(memory_space=pltpu.HBM)


def call(kernel, out_shape, us, *args, scalars=(), scratch=(), far=False, far_out=False):
    cost = pl.CostEstimate(flops=int(us * 3.0e8), bytes_accessed=int(us * 2.0e6), transcendentals=0)
    first = HBM if far_out else VMEM
    several = isinstance(out_shape, tuple)
    return pl.pallas_call(
        kernel,
        out_shape=out_shape,
        in_specs=[SMEM] * len(scalars) + [HBM if far else VMEM] * len(args),
        out_specs=(first,) + (VMEM,) * (len(out_shape) - 1) if several else first,
        scratch_shapes=list(scratch),
        cost_estimate=cost,
        compiler_params=pltpu.CompilerParams(vmem_limit_bytes=ALL if far else GRANT),
    )(*scalars, *args)


def exchange(x, axes):
    return lax.all_to_all(x, axes, 0, 0)


def pack_kernel(q_ref, k_ref, v_ref, out_ref, pooled_ref, came, turned, in_sems, out_sems):
    refs = (q_ref, k_ref, v_ref)
    loads = [pltpu.make_async_copy(ref, came.at[n], in_sems.at[n]) for n, ref in enumerate(refs)]
    for load in loads:
        load.start()
    stores = []
    for n, load in enumerate(loads):
        load.wait()
        flipped = came[n].T
        for tile in range(TILES):
            turned[n, tile] = flipped[tile * GROUP : (tile + 1) * GROUP]
        rows = pl.ds(n * GROUP, GROUP)
        store = pltpu.make_async_copy(turned.at[n], out_ref.at[:, rows, :], out_sems.at[n])
        store.start()
        stores.append(store)
    width = COLUMNS // AGENT_DEV
    cells = came[0].astype(F32).reshape(FRAMES, AGENT_DEV, width, D)
    means = jnp.sum(jnp.sum(cells, axis=0), axis=1) * (1.0 / (FRAMES * width))
    pooled_ref[...] = jnp.concatenate([means, jnp.zeros_like(means)], axis=0).astype(BF16)
    for store in stores:
        store.wait()


def rows_of(x_ref, start, size):
    return jnp.concatenate([x_ref[s, start : start + size, :] for s in range(TILES)], axis=1)


def couple_kernel(z_ref, ours_ref, theirs_ref, out_ref):
    ours, theirs = ours_ref[...].astype(F32), theirs_ref[...].astype(F32)
    second = lax.rem(z_ref[0], 2) == 1
    low, high = jnp.where(second, theirs, ours), jnp.where(second, ours, theirs)
    out_ref[...] = (low + pltpu.roll(high, AGENT_DEV, 0)).astype(BF16)


def route_kernel(z_ref, *refs):
    came, out_ref = refs[:PAIRS], refs[PAIRS]
    slots = [ref[...].astype(F32) for ref in came]
    rows = []
    for pair in range(PAIRS):
        hop = (z_ref[0] // 2 + PAIRS - pair) % PAIRS
        row = slots[0]
        for n in range(1, PAIRS):
            row = jnp.where(hop == n, slots[n], row)
        rows.append(row)
    agents = jnp.concatenate(rows, axis=0).astype(BF16)
    for tile in range(TILES):
        out_ref[tile] = agents[:, tile * GROUP : (tile + 1) * GROUP]


def agent_kernel(tm_ref, z_ref, a_ref, x_ref, keep_ref, send_ref):
    low = lax.rem(z_ref[0] // 2 + z_ref[0], 2) == 0
    everyone = a_ref[...].reshape(AGENTS, GROUP)
    columns = []
    logs = []
    for h in range(GROUP_HEADS):
        keys = rows_of(x_ref, K_ROW + h * HEAD_DIM, HEAD_DIM)
        values = rows_of(x_ref, V_ROW + h * HEAD_DIM, HEAD_DIM)
        agents = everyone[:, h * HEAD_DIM : (h + 1) * HEAD_DIM]
        scores = jnp.dot(agents, keys, preferred_element_type=F32) * INV_ROOT
        peak = jnp.max(scores, axis=1, keepdims=True)
        weights = jnp.exp(scores - peak)
        total = jnp.sum(weights, axis=1, keepdims=True)
        acc = lax.dot_general(
            weights.astype(BF16), values, (((1,), (1,)), ((), ())), preferred_element_type=F32
        )
        columns.append(acc / total)
        logs.append(peak + jnp.log(total))
    lane = lax.broadcasted_iota(jnp.int32, (AGENTS, HEAD_DIM), 1)
    stats = jnp.zeros((AGENTS, HEAD_DIM), F32)
    for h, log in enumerate(logs):
        stats = jnp.where(lane == h, log, stats)
    part = jnp.concatenate(columns + [stats], axis=1).T
    near, far = part[:, :HALF], part[:, HALF:]
    keep_ref[...] = jnp.where(low, near, far)[: GROUP + 8]
    away = jnp.where(low, far, near)
    send_ref[:GROUP] = away[:GROUP].astype(BF16)
    send_ref[GROUP:] = pieces_of(away[GROUP : GROUP + GROUP_HEADS])


def pieces_of(logs):
    pieces = []
    for _ in range(3):
        short = logs.astype(BF16).astype(F32)
        logs = logs - short
        pieces.append(short)
    pieces.append(jnp.zeros((STATS - 3 * GROUP_HEADS, HALF), F32))
    return jnp.concatenate(pieces, axis=0).astype(BF16)


def logs_of(pieces):
    n = GROUP_HEADS
    pieces = pieces.astype(F32)
    return pieces[:n] + pieces[n : 2 * n] + pieces[2 * n : 3 * n]


def blend_kernel(keep_ref, came_ref, cross_ref, out_ref, long_ref):
    ours, theirs = keep_ref[GROUP : GROUP + GROUP_HEADS, :], logs_of(came_ref[GROUP:, :])
    peak = jnp.maximum(ours, theirs)
    left, right = jnp.exp(ours - peak), jnp.exp(theirs - peak)
    whole = left + right
    left, right = left / whole, right / whole
    stats = pieces_of(peak + jnp.log(whole))
    for h in range(GROUP_HEADS):
        rows = slice(h * HEAD_DIM, (h + 1) * HEAD_DIM)
        part = keep_ref[rows, :] * left[h : h + 1] + came_ref[rows, :].astype(F32) * right[h : h + 1]
        part = part.astype(BF16)
        out_ref[rows, :] = part
        long_ref[rows, :] = part
    out_ref[GROUP:, :] = stats
    long_ref[GROUP : GROUP + STATS, :] = stats
    long_ref[GROUP + STATS :, :] = cross_ref[...]


def comb_kernel(*refs):
    parts, out_ref = refs[:PAIRS], refs[PAIRS]
    logs = [logs_of(part[GROUP : GROUP + STATS, :]) for part in parts]
    peak = logs[0]
    for log in logs[1:]:
        peak = jnp.maximum(peak, log)
    shares = [jnp.exp(log - peak) for log in logs]
    whole = sum(shares[1:], shares[0])
    shares = [share / whole for share in shares]
    for h in range(GROUP_HEADS):
        rows = slice(h * HEAD_DIM, (h + 1) * HEAD_DIM)
        terms = [
            part[rows, :].astype(F32) * share[h : h + 1]
            for part, share in zip(parts, shares, strict=True)
        ]
        out_ref[rows, :] = sum(terms[1:], terms[0]).astype(BF16)


def taps_kernel(tile_ref, w_ref, out_ref):
    for tile in range(TILES):

        @pl.when(tile_ref[0] == tile)
        def _(tile=tile):
            lanes = slice(tile * GROUP, (tile + 1) * GROUP)
            rows = [w_ref[i, j, :, lanes] for i in range(3) for j in range(3)]
            rows.append(jnp.zeros((5, GROUP), F32))
            out_ref[...] = jnp.concatenate(rows, axis=0).T


def edge_kernel(tm_ref, z_ref, x_ref, near_ref, far_ref, q_ref):
    q_ref[...] = rows_of(x_ref, 0, GROUP)
    spot = lax.broadcasted_iota(jnp.int32, (GROUP, TOKENS), 1) // COLUMNS
    for block in range(EDGE // TOKENS):
        last = first = jnp.zeros((GROUP, TOKENS), F32)
        for j in range(FRAMES):
            cells = x_ref[block * FRAMES + j, V_ROW:, :].astype(F32)
            late = cells if j == FRAMES - 1 else pltpu.roll(cells, (j + 1) * COLUMNS, 1)
            early = cells if j == 0 else pltpu.roll(cells, j * COLUMNS, 1)
            last = jnp.where(spot == j, late, last)
            first = jnp.where(spot == j, early, first)
        lanes = slice(block * TOKENS, (block + 1) * TOKENS)
        last, first = last.astype(BF16), first.astype(BF16)

        @pl.when(lax.rem(tm_ref[0], 2) == 0)
        def _(last=last, first=first, lanes=lanes):
            near_ref[:, lanes] = last
            far_ref[:, lanes] = first

        @pl.when(lax.rem(tm_ref[0], 2) != 0)
        def _(last=last, first=first, lanes=lanes):
            near_ref[:, lanes] = first
            far_ref[:, lanes] = last


TALL = 16


def turned(cells, by):
    by %= TOKENS
    return cells if by == 0 else pltpu.roll(cells, by, 1)


def frames_of(r, at, even, x_ref, near_ref, far_ref, tall=TALL):
    lane = lax.broadcasted_iota(jnp.int32, (tall, TOKENS), 1)
    cells = x_ref[r, pl.ds(V_ROW + at, tall), :].astype(F32)
    block, j = divmod(r, FRAMES)
    lanes = slice(block * TOKENS, (block + 1) * TOKENS)
    near = near_ref[pl.ds(at, tall), lanes].astype(F32)
    far = far_ref[pl.ds(at, tall), lanes].astype(F32)
    before = turned(jnp.where(even, far, near), -j * COLUMNS)
    after = turned(jnp.where(even, near, far), (FRAMES - 1 - j) * COLUMNS)
    return (
        jnp.where(lane < COLUMNS, before, turned(cells, COLUMNS)),
        cells,
        jnp.where(lane >= TOKENS - COLUMNS, after, turned(cells, -COLUMNS)),
    )


def taps_of(w_ref, at, rows=range(3), tall=TALL):
    w = w_ref[pl.ds(at, tall), :]
    return {
        (i, j, k): jnp.broadcast_to(w[:, n : n + 1], (tall, TOKENS))
        for i in range(3)
        for j in rows
        for k in range(3)
        for n in (i * 9 + j * 3 + k,)
    }


def stencil(rows, taps):
    shape = next(iter(rows.values()))[1].shape
    column = lax.broadcasted_iota(jnp.int32, shape, 1) % COLUMNS
    sums = []
    for k in range(3):
        total = None
        for j, frames in rows.items():
            for i in range(3):
                term = frames[i] * taps[i, j, k]
                total = term if total is None else total + term
        sums.append(total)
    left = jnp.where(column == 0, 0.0, pltpu.roll(sums[0], 1, 1))
    right = jnp.where(column == COLUMNS - 1, 0.0, pltpu.roll(sums[2], TOKENS - 1, 1))
    return left + sums[1] + right


def rim_kernel(tm_ref, z_ref, x_ref, near_ref, far_ref, w_ref, cross_ref, kin_ref):
    even, second = lax.rem(tm_ref[0], 2) == 0, lax.rem(z_ref[0], 2) == 1
    tall = GROUP // 2
    for at in range(0, GROUP, tall):
        sums = []
        for r, j in ((TILES - 1, 0), (0, 2)):
            frames = frames_of(r, at, even, x_ref, near_ref, far_ref, tall)
            sums.append(stencil({j: frames}, taps_of(w_ref, at, (j,), tall)).astype(BF16))
        cross_ref[pl.ds(at, tall), :] = jnp.where(second, sums[0], sums[1])
        kin_ref[pl.ds(at, tall), :] = jnp.where(second, sums[1], sums[0])


def conv_kernel(tm_ref, z_ref, x_ref, near_ref, far_ref, w_ref, out_ref):
    even = lax.rem(tm_ref[0], 2) == 0

    def step(n, carry):
        at = pl.multiple_of(n * TALL, TALL)
        taps = taps_of(w_ref, at)
        rows = {0: frames_of(0, at, even, x_ref, near_ref, far_ref)}
        for r in range(TILES):
            if r + 1 < TILES:
                rows[r + 1] = frames_of(r + 1, at, even, x_ref, near_ref, far_ref)
            near = {j: rows[r + j - 1] for j in range(3) if r + j - 1 in rows}
            out_ref[r, pl.ds(at, TALL), :] = stencil(near, taps)
            rows.pop(r - 1, None)
        return carry

    lax.fori_loop(0, GROUP // TALL, step, 0)


def query_kernel(a_ref, q_ref, e_ref, total_ref):
    agents = a_ref[...].reshape(AGENTS, GROUP)
    for h in range(GROUP_HEADS):
        rows = slice(h * HEAD_DIM, (h + 1) * HEAD_DIM)
        scores = jnp.dot(agents[:, rows], q_ref[rows, :], preferred_element_type=F32) * INV_ROOT
        weights = jnp.exp(scores - jnp.max(scores, axis=0, keepdims=True))
        total_ref[h : h + 1, :] = jnp.sum(weights, axis=0, keepdims=True)
        e_ref[h] = weights.astype(BF16)


def mix_kernel(tm_ref, z_ref, e_ref, total_ref, ours_ref, theirs_ref, one_ref, three_ref, kin_ref, local_ref, out_ref):
    low, second = lax.rem(z_ref[0] // 2 + z_ref[0], 2) == 0, lax.rem(z_ref[0], 2) == 1
    odd = lax.rem(tm_ref[0], 2)
    first, last = z_ref[0] == (PLANES - 1) * odd, z_ref[0] == PLANES - 1 - odd
    ours, theirs = ours_ref[...], theirs_ref[...]
    values = jnp.concatenate(
        [jnp.where(low, ours, theirs), jnp.where(low, theirs, ours)], axis=1
    )
    kin = kin_ref[...].astype(F32)
    one, three = one_ref[GROUP + STATS :].astype(F32), three_ref[GROUP + STATS :].astype(F32)
    above, below = jnp.where(odd == 1, three, one), jnp.where(odd == 1, one, three)
    above = jnp.where(first, 0.0, jnp.where(second, kin, above))
    below = jnp.where(last, 0.0, jnp.where(second, below, kin))
    for h in range(GROUP_HEADS):
        rows = slice(h * HEAD_DIM, (h + 1) * HEAD_DIM)
        mixed = jnp.dot(values[rows], e_ref[h], preferred_element_type=F32)
        mixed = mixed / total_ref[h : h + 1, :]
        for s in range(TILES):
            cells = mixed[:, s * TOKENS : (s + 1) * TOKENS] + local_ref[s, rows, :]
            if s == 0:
                cells += above[rows]
            if s == TILES - 1:
                cells += below[rows]
            out_ref[s, rows, :] = cells.astype(BF16)


def unpack_kernel(x_ref, out_ref, back, sems):
    pieces, stores = TILES // 2, []
    wide = D // pieces
    for n in range(pieces):
        back[n] = x_ref[2 * n : 2 * n + 2].reshape(wide, TOKENS).T
        store = pltpu.make_async_copy(back.at[n], out_ref.at[:, pl.ds(n * wide, wide)], sems.at[n])
        store.start()
        stores.append(store)
    for store in stores:
        store.wait()


LINE = ("tm", "zh", "zl")


def along(step):
    pairs = []
    for group in range(lax.axis_size("tm")):
        odd = group % 2
        for z in range(PLANES):
            to = (step((z - odd) % PLANES, odd) + odd) % PLANES
            pairs.append((group * PLANES + z, group * PLANES + to))
    return pairs


def pair_plane(at, odd):
    return at ^ 1


def same_side(at, n):
    return 2 * ((at // 2 + n) % PAIRS) + at % 2


def other_side(at, n):
    return 2 * ((at // 2 + n) % PAIRS) + (at + n) % 2


def scalar(x):
    return x.astype(jnp.int32).reshape(1)


def body(queries, key_states, value_states, conv_weight):
    q = queries.reshape(TOKENS, D)
    k = key_states.reshape(TOKENS, D)
    v = value_states.reshape(TOKENS, D)
    shape = jax.ShapeDtypeStruct
    packed, pooled = call(
        pack_kernel,
        (shape((TILES, SENT, TOKENS), BF16), shape((SLOT, D), BF16)),
        3.0,
        q,
        k,
        v,
        scratch=(
            pltpu.VMEM((3, TOKENS, D), BF16),
            pltpu.VMEM((3, TILES, GROUP, TOKENS), BF16),
            pltpu.SemaphoreType.DMA((3,)),
            pltpu.SemaphoreType.DMA((3,)),
        ),
        far=True,
        far_out=True,
    )
    x = exchange(packed, "xy")
    tile = scalar(lax.axis_index("xy"))
    taps = call(taps_kernel, shape((GROUP, 32), F32), 1.0, conv_weight, scalars=(tile,))

    tm = lax.axis_index("tm")
    where = (
        scalar(tm),
        scalar((2 * lax.axis_index("zh") + lax.axis_index("zl") + 7 * (tm & 1)) & 7),
    )
    met = lax.ppermute(pooled, LINE, along(pair_plane))
    couple = call(couple_kernel, shape((SLOT, D), BF16), 1.0, pooled, met, scalars=where[1:])
    came = [couple]
    for n in range(1, PAIRS):
        came.append(lax.ppermute(couple, LINE, along(lambda at, odd: same_side(at, n))))
    by_tile = shape((TILES, PAIRS * SLOT, GROUP), BF16)
    routed = call(route_kernel, by_tile, 1.0, *came, scalars=where[1:])
    agents = exchange(routed, "xy")
    edges = shape((GROUP, EDGE), BF16)
    near, far, turned_q = call(
        edge_kernel, (edges, edges, shape((GROUP, TILES * TOKENS), BF16)), 1.0, x, scalars=where
    )
    groups = lax.axis_size("tm")
    pairs = [(i, i + 1) for i in range(0, groups - 1, 2)]
    near = lax.ppermute(near, "tm", pairs + [(b, a) for a, b in pairs])
    pairs = [(i, i + 1) for i in range(1, groups - 1, 2)]
    far = lax.ppermute(far, "tm", pairs + [(b, a) for a, b in pairs])
    keep, send = call(
        agent_kernel,
        (shape((GROUP + 8, HALF), F32), shape((GROUP + STATS, HALF), BF16)),
        3.0,
        agents,
        x,
        scalars=where,
    )
    theirs = lax.ppermute(send, LINE, along(pair_plane))
    row = shape((GROUP, TOKENS), BF16)
    cross, kin = call(rim_kernel, (row, row), 1.0, x, near, far, taps, scalars=where)
    blended, longer = call(
        blend_kernel,
        (shape((GROUP + STATS, HALF), BF16), shape((2 * GROUP + STATS, HALF), BF16)),
        1.0,
        keep,
        theirs,
        cross,
    )
    parts = [blended]
    for n in range(1, PAIRS):
        moved = longer if n % 2 else blended
        parts.append(
            lax.ppermute(moved, LINE, along(lambda at, odd: other_side(at, -n if odd else n)))
        )
    kin = lax.ppermute(kin, LINE, along(pair_plane))
    local = call(
        conv_kernel, shape((TILES, GROUP, TOKENS), F32), 5.0, x, near, far, taps, scalars=where
    )
    ours = call(comb_kernel, shape((GROUP, HALF), BF16), 1.0, *parts)
    theirs = lax.ppermute(ours, LINE, along(pair_plane))
    weights, totals = call(
        query_kernel,
        (shape((GROUP_HEADS, AGENTS, TILES * TOKENS), BF16), shape((8, TILES * TOKENS), F32)),
        2.0,
        agents,
        turned_q,
    )
    mixed = call(
        mix_kernel,
        shape((TILES, GROUP, TOKENS), BF16),
        1.0,
        weights,
        totals,
        ours,
        theirs,
        parts[1],
        parts[3],
        kin,
        local,
        scalars=where,
    )
    mine = exchange(mixed, "xy")
    pieces = TILES // 2
    out = call(
        unpack_kernel,
        shape((TOKENS, D), BF16),
        1.0,
        mine,
        scratch=(
            pltpu.VMEM((pieces, TOKENS, D // pieces), BF16),
            pltpu.SemaphoreType.DMA((pieces,)),
        ),
        far_out=True,
    )
    return out.reshape(value_states.shape)


def solution(mesh):
    devices = mesh.devices
    fine = Mesh(devices.reshape(devices.shape[0], PAIRS, 2, TILES), ("tm", "zh", "zl", "xy"))
    spec = P("tm", None, ("zh", "zl", "xy"), None, None)
    return jax.shard_map(
        body,
        mesh=fine,
        in_specs=(spec, spec, spec, P()),
        out_specs=spec,
        check_vma=False,
    )
```

```python
import jax
import jax.numpy as jnp
from jax import lax
from jax.experimental import pallas as pl
from jax.experimental.pallas import tpu as pltpu
from jax.sharding import Mesh
from jax.sharding import PartitionSpec as P


HEADS = 24
HEAD_DIM = 64
D = 1536
FRAMES = 4
COLUMNS = 32
TOKENS = FRAMES * COLUMNS
AGENT_DEV = 4
PAIRS = 4
PLANES = 2 * PAIRS
TILES = 8
AGENTS = 256
SLOT = 8
GROUP_HEADS = HEADS // TILES
GROUP = GROUP_HEADS * HEAD_DIM
K_ROW = GROUP
V_ROW = 2 * GROUP
SENT = 3 * GROUP
EDGE = TILES * COLUMNS
STATS = 16
GRANT = 6 * 1024 * 1024
ALL = 60 * 1024 * 1024
INV_ROOT = HEAD_DIM ** (-0.5)
F32 = jnp.float32
BF16 = jnp.bfloat16


VMEM = pl.BlockSpec(memory_space=pltpu.VMEM)

SMEM = pl.BlockSpec(memory_space=pltpu.SMEM)
HBM = pl.BlockSpec(memory_space=pltpu.HBM)


def call(kernel, out_shape, us, *args, scalars=(), scratch=(), far=False, far_out=False):
    cost = pl.CostEstimate(flops=int(us * 3.0e8), bytes_accessed=int(us * 2.0e6), transcendentals=0)
    first = HBM if far_out else VMEM
    several = isinstance(out_shape, tuple)
    return pl.pallas_call(
        kernel,
        out_shape=out_shape,
        in_specs=[SMEM] * len(scalars) + [HBM if far else VMEM] * len(args),
        out_specs=(first,) + (VMEM,) * (len(out_shape) - 1) if several else first,
        scratch_shapes=list(scratch),
        cost_estimate=cost,
        compiler_params=pltpu.CompilerParams(vmem_limit_bytes=ALL if far else GRANT),
    )(*scalars, *args)


def exchange(x, axes):
    return lax.all_to_all(x, axes, 0, 0)


def pack_kernel(q_ref, k_ref, v_ref, out_ref, pooled_ref, came, turned, in_sems, out_sems):
    refs = (q_ref, k_ref, v_ref)
    loads = [pltpu.make_async_copy(ref, came.at[n], in_sems.at[n]) for n, ref in enumerate(refs)]
    for load in loads:
        load.start()
    stores = []
    for n, load in enumerate(loads):
        load.wait()
        flipped = came[n].T
        for tile in range(TILES):
            turned[n, tile] = flipped[tile * GROUP : (tile + 1) * GROUP]
        rows = pl.ds(n * GROUP, GROUP)
        store = pltpu.make_async_copy(turned.at[n], out_ref.at[:, rows, :], out_sems.at[n])
        store.start()
        stores.append(store)
    width = COLUMNS // AGENT_DEV
    cells = came[0].astype(F32).reshape(FRAMES, AGENT_DEV, width, D)
    means = jnp.sum(jnp.sum(cells, axis=0), axis=1) * (1.0 / (FRAMES * width))
    pooled_ref[...] = jnp.concatenate([means, jnp.zeros_like(means)], axis=0).astype(BF16)
    for store in stores:
        store.wait()


def rows_of(x_ref, start, size):
    return jnp.concatenate([x_ref[s, start : start + size, :] for s in range(TILES)], axis=1)


def couple_kernel(z_ref, ours_ref, theirs_ref, out_ref):
    ours, theirs = ours_ref[...].astype(F32), theirs_ref[...].astype(F32)
    second = lax.rem(z_ref[0], 2) == 1
    low, high = jnp.where(second, theirs, ours), jnp.where(second, ours, theirs)
    out_ref[...] = (low + pltpu.roll(high, AGENT_DEV, 0)).astype(BF16)


def route_kernel(z_ref, *refs):
    came, out_ref = refs[:PAIRS], refs[PAIRS]
    slots = [ref[...].astype(F32) for ref in came]
    rows = []
    for pair in range(PAIRS):
        hop = (z_ref[0] // 2 + PAIRS - pair) % PAIRS
        row = slots[0]
        for n in range(1, PAIRS):
            row = jnp.where(hop == n, slots[n], row)
        rows.append(row)
    agents = jnp.concatenate(rows, axis=0).astype(BF16)
    for tile in range(TILES):
        out_ref[tile] = agents[:, tile * GROUP : (tile + 1) * GROUP]


def agent_kernel(a_ref, x_ref, keep_ref, send_ref):
    everyone = a_ref[...].reshape(AGENTS, GROUP)
    columns = []
    logs = []
    for h in range(GROUP_HEADS):
        keys = rows_of(x_ref, K_ROW + h * HEAD_DIM, HEAD_DIM)
        values = rows_of(x_ref, V_ROW + h * HEAD_DIM, HEAD_DIM)
        agents = everyone[:, h * HEAD_DIM : (h + 1) * HEAD_DIM]
        scores = jnp.dot(agents, keys, preferred_element_type=F32) * INV_ROOT
        peak = jnp.max(scores, axis=1, keepdims=True)
        weights = jnp.exp(scores - peak)
        total = jnp.sum(weights, axis=1, keepdims=True)
        acc = lax.dot_general(
            weights.astype(BF16), values, (((1,), (1,)), ((), ())), preferred_element_type=F32
        )
        columns.append(acc / total)
        logs.append(peak + jnp.log(total))
    lane = lax.broadcasted_iota(jnp.int32, (AGENTS, HEAD_DIM), 1)
    stats = jnp.zeros((AGENTS, HEAD_DIM), F32)
    for h, log in enumerate(logs):
        stats = jnp.where(lane == h, log, stats)
    part = jnp.concatenate(columns + [stats], axis=1).T
    keep_ref[...] = part[: GROUP + 8]
    send_ref[:GROUP] = part[:GROUP].astype(BF16)
    send_ref[GROUP:] = pieces_of(part[GROUP : GROUP + GROUP_HEADS])


def pieces_of(logs):
    pieces = []
    for _ in range(3):
        short = logs.astype(BF16).astype(F32)
        logs = logs - short
        pieces.append(short)
    pieces.append(jnp.zeros((STATS - 3 * GROUP_HEADS, AGENTS), F32))
    return jnp.concatenate(pieces, axis=0).astype(BF16)


def logs_of(pieces):
    n = GROUP_HEADS
    pieces = pieces.astype(F32)
    return pieces[:n] + pieces[n : 2 * n] + pieces[2 * n : 3 * n]


def blend_kernel(keep_ref, came_ref, cross_ref, out_ref, long_ref):
    ours, theirs = keep_ref[GROUP : GROUP + GROUP_HEADS, :], logs_of(came_ref[GROUP:, :])
    peak = jnp.maximum(ours, theirs)
    left, right = jnp.exp(ours - peak), jnp.exp(theirs - peak)
    whole = left + right
    left, right = left / whole, right / whole
    stats = pieces_of(peak + jnp.log(whole))
    for h in range(GROUP_HEADS):
        rows = slice(h * HEAD_DIM, (h + 1) * HEAD_DIM)
        part = keep_ref[rows, :] * left[h : h + 1] + came_ref[rows, :].astype(F32) * right[h : h + 1]
        part = part.astype(BF16)
        out_ref[rows, :] = part
        long_ref[rows, :] = part
    out_ref[GROUP:, :] = stats
    long_ref[GROUP : GROUP + STATS, :] = stats
    for n in range(2):
        lanes = slice(n * TOKENS, (n + 1) * TOKENS)
        long_ref[GROUP + STATS :, lanes] = cross_ref[n * GROUP // 2 : (n + 1) * GROUP // 2, :]


def comb_kernel(*refs):
    parts, out_ref = refs[:PAIRS], refs[PAIRS]
    logs = [logs_of(part[GROUP : GROUP + STATS, :]) for part in parts]
    peak = logs[0]
    for log in logs[1:]:
        peak = jnp.maximum(peak, log)
    shares = [jnp.exp(log - peak) for log in logs]
    whole = sum(shares[1:], shares[0])
    shares = [share / whole for share in shares]
    for h in range(GROUP_HEADS):
        rows = slice(h * HEAD_DIM, (h + 1) * HEAD_DIM)
        terms = [
            part[rows, :].astype(F32) * share[h : h + 1]
            for part, share in zip(parts, shares, strict=True)
        ]
        out_ref[rows, :] = sum(terms[1:], terms[0]).astype(BF16)


def taps_kernel(tile_ref, w_ref, out_ref):
    for tile in range(TILES):

        @pl.when(tile_ref[0] == tile)
        def _(tile=tile):
            lanes = slice(tile * GROUP, (tile + 1) * GROUP)
            rows = [w_ref[i, j, :, lanes] for i in range(3) for j in range(3)]
            rows.append(jnp.zeros((5, GROUP), F32))
            out_ref[...] = jnp.concatenate(rows, axis=0).T


def edge_kernel(tm_ref, z_ref, x_ref, near_ref, far_ref, q_ref):
    q_ref[...] = rows_of(x_ref, 0, GROUP)
    spot = lax.broadcasted_iota(jnp.int32, (GROUP, TOKENS), 1) // COLUMNS
    for block in range(EDGE // TOKENS):
        last = first = jnp.zeros((GROUP, TOKENS), F32)
        for j in range(FRAMES):
            cells = x_ref[block * FRAMES + j, V_ROW:, :].astype(F32)
            late = cells if j == FRAMES - 1 else pltpu.roll(cells, (j + 1) * COLUMNS, 1)
            early = cells if j == 0 else pltpu.roll(cells, j * COLUMNS, 1)
            last = jnp.where(spot == j, late, last)
            first = jnp.where(spot == j, early, first)
        lanes = slice(block * TOKENS, (block + 1) * TOKENS)
        last, first = last.astype(BF16), first.astype(BF16)

        @pl.when(lax.rem(tm_ref[0], 2) == 0)
        def _(last=last, first=first, lanes=lanes):
            near_ref[:, lanes] = last
            far_ref[:, lanes] = first

        @pl.when(lax.rem(tm_ref[0], 2) != 0)
        def _(last=last, first=first, lanes=lanes):
            near_ref[:, lanes] = first
            far_ref[:, lanes] = last


TALL = 16


def turned(cells, by):
    by %= TOKENS
    return cells if by == 0 else pltpu.roll(cells, by, 1)


def frames_of(r, at, even, x_ref, near_ref, far_ref, tall=TALL):
    lane = lax.broadcasted_iota(jnp.int32, (tall, TOKENS), 1)
    cells = x_ref[r, pl.ds(V_ROW + at, tall), :].astype(F32)
    block, j = divmod(r, FRAMES)
    lanes = slice(block * TOKENS, (block + 1) * TOKENS)
    near = near_ref[pl.ds(at, tall), lanes].astype(F32)
    far = far_ref[pl.ds(at, tall), lanes].astype(F32)
    before = turned(jnp.where(even, far, near), -j * COLUMNS)
    after = turned(jnp.where(even, near, far), (FRAMES - 1 - j) * COLUMNS)
    return (
        jnp.where(lane < COLUMNS, before, turned(cells, COLUMNS)),
        cells,
        jnp.where(lane >= TOKENS - COLUMNS, after, turned(cells, -COLUMNS)),
    )


def taps_of(w_ref, at, rows=range(3), tall=TALL):
    w = w_ref[pl.ds(at, tall), :]
    return {
        (i, j, k): jnp.broadcast_to(w[:, n : n + 1], (tall, TOKENS))
        for i in range(3)
        for j in rows
        for k in range(3)
        for n in (i * 9 + j * 3 + k,)
    }


def stencil(rows, taps):
    shape = next(iter(rows.values()))[1].shape
    column = lax.broadcasted_iota(jnp.int32, shape, 1) % COLUMNS
    sums = []
    for k in range(3):
        total = None
        for j, frames in rows.items():
            for i in range(3):
                term = frames[i] * taps[i, j, k]
                total = term if total is None else total + term
        sums.append(total)
    left = jnp.where(column == 0, 0.0, pltpu.roll(sums[0], 1, 1))
    right = jnp.where(column == COLUMNS - 1, 0.0, pltpu.roll(sums[2], TOKENS - 1, 1))
    return left + sums[1] + right


def rim_kernel(tm_ref, z_ref, x_ref, near_ref, far_ref, w_ref, cross_ref, kin_ref):
    even, second = lax.rem(tm_ref[0], 2) == 0, lax.rem(z_ref[0], 2) == 1
    tall = GROUP // 2
    for at in range(0, GROUP, tall):
        sums = []
        for r, j in ((TILES - 1, 0), (0, 2)):
            frames = frames_of(r, at, even, x_ref, near_ref, far_ref, tall)
            sums.append(stencil({j: frames}, taps_of(w_ref, at, (j,), tall)).astype(BF16))
        cross_ref[pl.ds(at, tall), :] = jnp.where(second, sums[0], sums[1])
        kin_ref[pl.ds(at, tall), :] = jnp.where(second, sums[1], sums[0])


def conv_kernel(tm_ref, z_ref, x_ref, near_ref, far_ref, w_ref, out_ref):
    even = lax.rem(tm_ref[0], 2) == 0

    def step(n, carry):
        at = pl.multiple_of(n * TALL, TALL)
        taps = taps_of(w_ref, at)
        rows = {0: frames_of(0, at, even, x_ref, near_ref, far_ref)}
        for r in range(TILES):
            if r + 1 < TILES:
                rows[r + 1] = frames_of(r + 1, at, even, x_ref, near_ref, far_ref)
            near = {j: rows[r + j - 1] for j in range(3) if r + j - 1 in rows}
            out_ref[r, pl.ds(at, TALL), :] = stencil(near, taps)
            rows.pop(r - 1, None)
        return carry

    lax.fori_loop(0, GROUP // TALL, step, 0)


def query_kernel(a_ref, q_ref, e_ref, total_ref):
    agents = a_ref[...].reshape(AGENTS, GROUP)
    for h in range(GROUP_HEADS):
        rows = slice(h * HEAD_DIM, (h + 1) * HEAD_DIM)
        scores = jnp.dot(agents[:, rows], q_ref[rows, :], preferred_element_type=F32) * INV_ROOT
        weights = jnp.exp(scores - jnp.max(scores, axis=0, keepdims=True))
        total_ref[h : h + 1, :] = jnp.sum(weights, axis=0, keepdims=True)
        e_ref[h] = weights.astype(BF16)


def mix_kernel(tm_ref, z_ref, e_ref, total_ref, values_ref, one_ref, three_ref, kin_ref, local_ref, out_ref):
    second = lax.rem(z_ref[0], 2) == 1
    odd = lax.rem(tm_ref[0], 2)
    first, last = z_ref[0] == (PLANES - 1) * odd, z_ref[0] == PLANES - 1 - odd
    kin = kin_ref[...].astype(F32)
    one, three = (
        jnp.concatenate(
            [ref[GROUP + STATS :, :TOKENS], ref[GROUP + STATS :, TOKENS:]], axis=0
        ).astype(F32)
        for ref in (one_ref, three_ref)
    )
    above, below = jnp.where(odd == 1, three, one), jnp.where(odd == 1, one, three)
    above = jnp.where(first, 0.0, jnp.where(second, kin, above))
    below = jnp.where(last, 0.0, jnp.where(second, below, kin))
    for h in range(GROUP_HEADS):
        rows = slice(h * HEAD_DIM, (h + 1) * HEAD_DIM)
        mixed = jnp.dot(values_ref[rows, :], e_ref[h], preferred_element_type=F32)
        mixed = mixed / total_ref[h : h + 1, :]
        for s in range(TILES):
            cells = mixed[:, s * TOKENS : (s + 1) * TOKENS] + local_ref[s, rows, :]
            if s == 0:
                cells += above[rows]
            if s == TILES - 1:
                cells += below[rows]
            out_ref[s, rows, :] = cells.astype(BF16)


def unpack_kernel(x_ref, out_ref, back, sems):
    pieces, stores = TILES // 2, []
    wide = D // pieces
    for n in range(pieces):
        back[n] = x_ref[2 * n : 2 * n + 2].reshape(wide, TOKENS).T
        store = pltpu.make_async_copy(back.at[n], out_ref.at[:, pl.ds(n * wide, wide)], sems.at[n])
        store.start()
        stores.append(store)
    for store in stores:
        store.wait()


LINE = ("tm", "zh", "zl")


def along(step):
    pairs = []
    for group in range(lax.axis_size("tm")):
        odd = group % 2
        for z in range(PLANES):
            to = (step((z - odd) % PLANES, odd) + odd) % PLANES
            pairs.append((group * PLANES + z, group * PLANES + to))
    return pairs


def pair_plane(at, odd):
    return at ^ 1


def same_side(at, n):
    return 2 * ((at // 2 + n) % PAIRS) + at % 2


def other_side(at, n):
    return 2 * ((at // 2 + n) % PAIRS) + (at + n) % 2


def scalar(x):
    return x.astype(jnp.int32).reshape(1)


def body(queries, key_states, value_states, conv_weight):
    q = queries.reshape(TOKENS, D)
    k = key_states.reshape(TOKENS, D)
    v = value_states.reshape(TOKENS, D)
    shape = jax.ShapeDtypeStruct
    packed, pooled = call(
        pack_kernel,
        (shape((TILES, SENT, TOKENS), BF16), shape((SLOT, D), BF16)),
        3.0,
        q,
        k,
        v,
        scratch=(
            pltpu.VMEM((3, TOKENS, D), BF16),
            pltpu.VMEM((3, TILES, GROUP, TOKENS), BF16),
            pltpu.SemaphoreType.DMA((3,)),
            pltpu.SemaphoreType.DMA((3,)),
        ),
        far=True,
        far_out=True,
    )
    x = exchange(packed, "xy")
    tile = scalar(lax.axis_index("xy"))
    taps = call(taps_kernel, shape((GROUP, 32), F32), 1.0, conv_weight, scalars=(tile,))

    tm = lax.axis_index("tm")
    where = (
        scalar(tm),
        scalar((2 * lax.axis_index("zh") + lax.axis_index("zl") + 7 * (tm & 1)) & 7),
    )
    met = lax.ppermute(pooled, LINE, along(pair_plane))
    couple = call(couple_kernel, shape((SLOT, D), BF16), 1.0, pooled, met, scalars=where[1:])
    came = [couple]
    for n in range(1, PAIRS):
        came.append(lax.ppermute(couple, LINE, along(lambda at, odd: same_side(at, n))))
    by_tile = shape((TILES, PAIRS * SLOT, GROUP), BF16)
    routed = call(route_kernel, by_tile, 1.0, *came, scalars=where[1:])
    agents = exchange(routed, "xy")
    edges = shape((GROUP, EDGE), BF16)
    near, far, turned_q = call(
        edge_kernel, (edges, edges, shape((GROUP, TILES * TOKENS), BF16)), 1.0, x, scalars=where
    )
    groups = lax.axis_size("tm")
    pairs = [(i, i + 1) for i in range(0, groups - 1, 2)]
    near = lax.ppermute(near, "tm", pairs + [(b, a) for a, b in pairs])
    pairs = [(i, i + 1) for i in range(1, groups - 1, 2)]
    far = lax.ppermute(far, "tm", pairs + [(b, a) for a, b in pairs])
    keep, send = call(
        agent_kernel,
        (shape((GROUP + 8, AGENTS), F32), shape((GROUP + STATS, AGENTS), BF16)),
        3.0,
        agents,
        x,
    )
    theirs = lax.ppermute(send, LINE, along(pair_plane))
    row = shape((GROUP, TOKENS), BF16)
    cross, kin = call(rim_kernel, (row, row), 1.0, x, near, far, taps, scalars=where)
    blended, longer = call(
        blend_kernel,
        (shape((GROUP + STATS, AGENTS), BF16), shape((GROUP + STATS + GROUP // 2, AGENTS), BF16)),
        1.0,
        keep,
        theirs,
        cross,
    )
    parts = [blended]
    for n in range(1, PAIRS):
        moved = longer if n % 2 else blended
        parts.append(
            lax.ppermute(moved, LINE, along(lambda at, odd: other_side(at, -n if odd else n)))
        )
    kin = lax.ppermute(kin, LINE, along(pair_plane))
    local = call(
        conv_kernel, shape((TILES, GROUP, TOKENS), F32), 5.0, x, near, far, taps, scalars=where
    )
    values = call(comb_kernel, shape((GROUP, AGENTS), BF16), 1.0, *parts)
    weights, totals = call(
        query_kernel,
        (shape((GROUP_HEADS, AGENTS, TILES * TOKENS), BF16), shape((8, TILES * TOKENS), F32)),
        2.0,
        agents,
        turned_q,
    )
    mixed = call(
        mix_kernel,
        shape((TILES, GROUP, TOKENS), BF16),
        1.0,
        weights,
        totals,
        values,
        parts[1],
        parts[3],
        kin,
        local,
        scalars=where,
    )
    mine = exchange(mixed, "xy")
    pieces = TILES // 2
    out = call(
        unpack_kernel,
        shape((TOKENS, D), BF16),
        1.0,
        mine,
        scratch=(
            pltpu.VMEM((pieces, TOKENS, D // pieces), BF16),
            pltpu.SemaphoreType.DMA((pieces,)),
        ),
        far_out=True,
    )
    return out.reshape(value_states.shape)


def solution(mesh):
    devices = mesh.devices
    fine = Mesh(devices.reshape(devices.shape[0], PAIRS, 2, TILES), ("tm", "zh", "zl", "xy"))
    spec = P("tm", None, ("zh", "zl", "xy"), None, None)
    return jax.shard_map(
        body,
        mesh=fine,
        in_specs=(spec, spec, spec, P()),
        out_specs=spec,
        check_vma=False,
    )
```

```python
import jax
import jax.numpy as jnp
from jax import lax
from jax.experimental import pallas as pl
from jax.experimental.pallas import tpu as pltpu
from jax.sharding import Mesh
from jax.sharding import PartitionSpec as P


HEADS = 24
HEAD_DIM = 64
D = 1536
FRAMES = 4
COLUMNS = 32
TOKENS = FRAMES * COLUMNS
AGENT_DEV = 4
PAIRS = 4
PLANES = 2 * PAIRS
TILES = 8
AGENTS = 256
SLOT = 8
GROUP_HEADS = HEADS // TILES
GROUP = GROUP_HEADS * HEAD_DIM
K_ROW = GROUP
V_ROW = 2 * GROUP
SENT = 3 * GROUP
EDGE = TILES * COLUMNS
STATS = 16
GRANT = 6 * 1024 * 1024
ALL = 60 * 1024 * 1024
INV_ROOT = HEAD_DIM ** (-0.5)
F32 = jnp.float32
BF16 = jnp.bfloat16


VMEM = pl.BlockSpec(memory_space=pltpu.VMEM)

SMEM = pl.BlockSpec(memory_space=pltpu.SMEM)
HBM = pl.BlockSpec(memory_space=pltpu.HBM)


def call(kernel, out_shape, us, *args, scalars=(), scratch=(), far=False, far_out=False):
    cost = pl.CostEstimate(flops=int(us * 3.0e8), bytes_accessed=int(us * 2.0e6), transcendentals=0)
    first = HBM if far_out else VMEM
    several = isinstance(out_shape, tuple)
    return pl.pallas_call(
        kernel,
        out_shape=out_shape,
        in_specs=[SMEM] * len(scalars) + [HBM if far else VMEM] * len(args),
        out_specs=(first,) + (VMEM,) * (len(out_shape) - 1) if several else first,
        scratch_shapes=list(scratch),
        cost_estimate=cost,
        compiler_params=pltpu.CompilerParams(vmem_limit_bytes=ALL if far else GRANT),
    )(*scalars, *args)


def exchange(x, axes):
    return lax.all_to_all(x, axes, 0, 0)


def pack_kernel(q_ref, k_ref, v_ref, out_ref, pooled_ref, came, turned, in_sems, out_sems):
    refs = (q_ref, k_ref, v_ref)
    loads = [pltpu.make_async_copy(ref, came.at[n], in_sems.at[n]) for n, ref in enumerate(refs)]
    for load in loads:
        load.start()
    stores = []
    for n, load in enumerate(loads):
        load.wait()
        flipped = came[n].T
        for tile in range(TILES):
            turned[n, tile] = flipped[tile * GROUP : (tile + 1) * GROUP]
        rows = pl.ds(n * GROUP, GROUP)
        store = pltpu.make_async_copy(turned.at[n], out_ref.at[:, rows, :], out_sems.at[n])
        store.start()
        stores.append(store)
    width = COLUMNS // AGENT_DEV
    cells = came[0].astype(F32).reshape(FRAMES, AGENT_DEV, width, D)
    means = jnp.sum(jnp.sum(cells, axis=0), axis=1) * (1.0 / (FRAMES * width))
    pooled_ref[...] = jnp.concatenate([means, jnp.zeros_like(means)], axis=0).astype(BF16)
    for store in stores:
        store.wait()


def rows_of(x_ref, start, size):
    return jnp.concatenate([x_ref[s, start : start + size, :] for s in range(TILES)], axis=1)


def couple_kernel(z_ref, ours_ref, theirs_ref, out_ref):
    ours, theirs = ours_ref[...].astype(F32), theirs_ref[...].astype(F32)
    second = lax.rem(z_ref[0], 2) == 1
    low, high = jnp.where(second, theirs, ours), jnp.where(second, ours, theirs)
    out_ref[...] = (low + pltpu.roll(high, AGENT_DEV, 0)).astype(BF16)


def route_kernel(z_ref, *refs):
    came, out_ref = refs[:PAIRS], refs[PAIRS]
    slots = [ref[...].astype(F32) for ref in came]
    rows = []
    for pair in range(PAIRS):
        hop = (z_ref[0] // 2 + PAIRS - pair) % PAIRS
        row = slots[0]
        for n in range(1, PAIRS):
            row = jnp.where(hop == n, slots[n], row)
        rows.append(row)
    agents = jnp.concatenate(rows, axis=0).astype(BF16)
    for tile in range(TILES):
        out_ref[tile] = agents[:, tile * GROUP : (tile + 1) * GROUP]


def agent_kernel(a_ref, x_ref, keep_ref, send_ref):
    everyone = a_ref[...].reshape(AGENTS, GROUP)
    columns = []
    logs = []
    for h in range(GROUP_HEADS):
        keys = rows_of(x_ref, K_ROW + h * HEAD_DIM, HEAD_DIM)
        values = rows_of(x_ref, V_ROW + h * HEAD_DIM, HEAD_DIM)
        agents = everyone[:, h * HEAD_DIM : (h + 1) * HEAD_DIM]
        scores = jnp.dot(agents, keys, preferred_element_type=F32) * INV_ROOT
        peak = jnp.max(scores, axis=1, keepdims=True)
        weights = jnp.exp(scores - peak)
        total = jnp.sum(weights, axis=1, keepdims=True)
        acc = lax.dot_general(
            weights.astype(BF16), values, (((1,), (1,)), ((), ())), preferred_element_type=F32
        )
        columns.append(acc / total)
        logs.append(peak + jnp.log(total))
    lane = lax.broadcasted_iota(jnp.int32, (AGENTS, HEAD_DIM), 1)
    stats = jnp.zeros((AGENTS, HEAD_DIM), F32)
    for h, log in enumerate(logs):
        stats = jnp.where(lane == h, log, stats)
    part = jnp.concatenate(columns + [stats], axis=1).T
    keep_ref[...] = part[: GROUP + 8]
    send_ref[:GROUP] = part[:GROUP].astype(BF16)
    send_ref[GROUP:] = pieces_of(part[GROUP : GROUP + GROUP_HEADS])


def pieces_of(logs):
    pieces = []
    for _ in range(3):
        short = logs.astype(BF16).astype(F32)
        logs = logs - short
        pieces.append(short)
    pieces.append(jnp.zeros((STATS - 3 * GROUP_HEADS, AGENTS), F32))
    return jnp.concatenate(pieces, axis=0).astype(BF16)


def logs_of(pieces):
    n = GROUP_HEADS
    pieces = pieces.astype(F32)
    return pieces[:n] + pieces[n : 2 * n] + pieces[2 * n : 3 * n]


def blend_kernel(keep_ref, came_ref, out_ref):
    ours, theirs = keep_ref[GROUP : GROUP + GROUP_HEADS, :], logs_of(came_ref[GROUP:, :])
    peak = jnp.maximum(ours, theirs)
    left, right = jnp.exp(ours - peak), jnp.exp(theirs - peak)
    whole = left + right
    left, right = left / whole, right / whole
    stats = pieces_of(peak + jnp.log(whole))
    for h in range(GROUP_HEADS):
        rows = slice(h * HEAD_DIM, (h + 1) * HEAD_DIM)
        part = keep_ref[rows, :] * left[h : h + 1] + came_ref[rows, :].astype(F32) * right[h : h + 1]
        part = part.astype(BF16)
        out_ref[rows, :] = part
    out_ref[GROUP:, :] = stats


def comb_kernel(*refs):
    parts, out_ref = refs[:PAIRS], refs[PAIRS]
    logs = [logs_of(part[GROUP : GROUP + STATS, :]) for part in parts]
    peak = logs[0]
    for log in logs[1:]:
        peak = jnp.maximum(peak, log)
    shares = [jnp.exp(log - peak) for log in logs]
    whole = sum(shares[1:], shares[0])
    shares = [share / whole for share in shares]
    for h in range(GROUP_HEADS):
        rows = slice(h * HEAD_DIM, (h + 1) * HEAD_DIM)
        terms = [
            part[rows, :].astype(F32) * share[h : h + 1]
            for part, share in zip(parts, shares, strict=True)
        ]
        out_ref[rows, :] = sum(terms[1:], terms[0]).astype(BF16)


def taps_kernel(tile_ref, w_ref, out_ref):
    for tile in range(TILES):

        @pl.when(tile_ref[0] == tile)
        def _(tile=tile):
            lanes = slice(tile * GROUP, (tile + 1) * GROUP)
            rows = [w_ref[i, j, :, lanes] for i in range(3) for j in range(3)]
            rows.append(jnp.zeros((5, GROUP), F32))
            out_ref[...] = jnp.concatenate(rows, axis=0).T


def edge_kernel(tm_ref, z_ref, x_ref, near_ref, far_ref, q_ref):
    q_ref[...] = rows_of(x_ref, 0, GROUP)
    spot = lax.broadcasted_iota(jnp.int32, (GROUP, TOKENS), 1) // COLUMNS
    for block in range(EDGE // TOKENS):
        last = first = jnp.zeros((GROUP, TOKENS), F32)
        for j in range(FRAMES):
            cells = x_ref[block * FRAMES + j, V_ROW:, :].astype(F32)
            late = cells if j == FRAMES - 1 else pltpu.roll(cells, (j + 1) * COLUMNS, 1)
            early = cells if j == 0 else pltpu.roll(cells, j * COLUMNS, 1)
            last = jnp.where(spot == j, late, last)
            first = jnp.where(spot == j, early, first)
        lanes = slice(block * TOKENS, (block + 1) * TOKENS)
        last, first = last.astype(BF16), first.astype(BF16)

        @pl.when(lax.rem(tm_ref[0], 2) == 0)
        def _(last=last, first=first, lanes=lanes):
            near_ref[:, lanes] = last
            far_ref[:, lanes] = first

        @pl.when(lax.rem(tm_ref[0], 2) != 0)
        def _(last=last, first=first, lanes=lanes):
            near_ref[:, lanes] = first
            far_ref[:, lanes] = last


TALL = 16


def turned(cells, by):
    by %= TOKENS
    return cells if by == 0 else pltpu.roll(cells, by, 1)


def frames_of(r, at, even, x_ref, near_ref, far_ref, tall=TALL):
    lane = lax.broadcasted_iota(jnp.int32, (tall, TOKENS), 1)
    cells = x_ref[r, pl.ds(V_ROW + at, tall), :].astype(F32)
    block, j = divmod(r, FRAMES)
    lanes = slice(block * TOKENS, (block + 1) * TOKENS)
    near = near_ref[pl.ds(at, tall), lanes].astype(F32)
    far = far_ref[pl.ds(at, tall), lanes].astype(F32)
    before = turned(jnp.where(even, far, near), -j * COLUMNS)
    after = turned(jnp.where(even, near, far), (FRAMES - 1 - j) * COLUMNS)
    return (
        jnp.where(lane < COLUMNS, before, turned(cells, COLUMNS)),
        cells,
        jnp.where(lane >= TOKENS - COLUMNS, after, turned(cells, -COLUMNS)),
    )


def taps_of(w_ref, at, rows=range(3), tall=TALL):
    w = w_ref[pl.ds(at, tall), :]
    return {
        (i, j, k): jnp.broadcast_to(w[:, n : n + 1], (tall, TOKENS))
        for i in range(3)
        for j in rows
        for k in range(3)
        for n in (i * 9 + j * 3 + k,)
    }


def stencil(rows, taps):
    shape = next(iter(rows.values()))[1].shape
    column = lax.broadcasted_iota(jnp.int32, shape, 1) % COLUMNS
    sums = []
    for k in range(3):
        total = None
        for j, frames in rows.items():
            for i in range(3):
                term = frames[i] * taps[i, j, k]
                total = term if total is None else total + term
        sums.append(total)
    left = jnp.where(column == 0, 0.0, pltpu.roll(sums[0], 1, 1))
    right = jnp.where(column == COLUMNS - 1, 0.0, pltpu.roll(sums[2], TOKENS - 1, 1))
    return left + sums[1] + right


def rim_kernel(tm_ref, z_ref, x_ref, near_ref, far_ref, w_ref, cross_ref, kin_ref):
    even, second = lax.rem(tm_ref[0], 2) == 0, lax.rem(z_ref[0], 2) == 1
    tall = GROUP // 2
    for at in range(0, GROUP, tall):
        sums = []
        for r, j in ((TILES - 1, 0), (0, 2)):
            frames = frames_of(r, at, even, x_ref, near_ref, far_ref, tall)
            sums.append(stencil({j: frames}, taps_of(w_ref, at, (j,), tall)).astype(BF16))
        cross_ref[pl.ds(at, tall), :] = jnp.where(second, sums[0], sums[1])
        kin_ref[pl.ds(at, tall), :] = jnp.where(second, sums[1], sums[0])


def conv_kernel(tm_ref, z_ref, x_ref, near_ref, far_ref, w_ref, out_ref):
    even = lax.rem(tm_ref[0], 2) == 0

    def step(n, carry):
        at = pl.multiple_of(n * TALL, TALL)
        taps = taps_of(w_ref, at)
        rows = {0: frames_of(0, at, even, x_ref, near_ref, far_ref)}
        for r in range(TILES):
            if r + 1 < TILES:
                rows[r + 1] = frames_of(r + 1, at, even, x_ref, near_ref, far_ref)
            near = {j: rows[r + j - 1] for j in range(3) if r + j - 1 in rows}
            out_ref[r, pl.ds(at, TALL), :] = stencil(near, taps)
            rows.pop(r - 1, None)
        return carry

    lax.fori_loop(0, GROUP // TALL, step, 0)


def query_kernel(a_ref, q_ref, e_ref, total_ref):
    agents = a_ref[...].reshape(AGENTS, GROUP)
    for h in range(GROUP_HEADS):
        rows = slice(h * HEAD_DIM, (h + 1) * HEAD_DIM)
        scores = jnp.dot(agents[:, rows], q_ref[rows, :], preferred_element_type=F32) * INV_ROOT
        weights = jnp.exp(scores - jnp.max(scores, axis=0, keepdims=True))
        total_ref[h : h + 1, :] = jnp.sum(weights, axis=0, keepdims=True)
        e_ref[h] = weights.astype(BF16)


def mix_kernel(tm_ref, z_ref, e_ref, total_ref, values_ref, cross_ref, kin_ref, local_ref, out_ref):
    second = lax.rem(z_ref[0], 2) == 1
    odd = lax.rem(tm_ref[0], 2)
    first, last = z_ref[0] == (PLANES - 1) * odd, z_ref[0] == PLANES - 1 - odd
    kin = kin_ref[...].astype(F32)
    across = cross_ref[...].astype(F32)
    above = jnp.where(first, 0.0, jnp.where(second, kin, across))
    below = jnp.where(last, 0.0, jnp.where(second, across, kin))
    for h in range(GROUP_HEADS):
        rows = slice(h * HEAD_DIM, (h + 1) * HEAD_DIM)
        mixed = jnp.dot(values_ref[rows, :], e_ref[h], preferred_element_type=F32)
        mixed = mixed / total_ref[h : h + 1, :]
        for s in range(TILES):
            cells = mixed[:, s * TOKENS : (s + 1) * TOKENS] + local_ref[s, rows, :]
            if s == 0:
                cells += above[rows]
            if s == TILES - 1:
                cells += below[rows]
            out_ref[s, rows, :] = cells.astype(BF16)


def unpack_kernel(x_ref, out_ref, back, sems):
    pieces, stores = TILES // 2, []
    wide = D // pieces
    for n in range(pieces):
        back[n] = x_ref[2 * n : 2 * n + 2].reshape(wide, TOKENS).T
        store = pltpu.make_async_copy(back.at[n], out_ref.at[:, pl.ds(n * wide, wide)], sems.at[n])
        store.start()
        stores.append(store)
    for store in stores:
        store.wait()


LINE = ("tm", "zh", "zl")


def along(step):
    pairs = []
    for group in range(lax.axis_size("tm")):
        odd = group % 2
        for z in range(PLANES):
            to = (step((z - odd) % PLANES, odd) + odd) % PLANES
            pairs.append((group * PLANES + z, group * PLANES + to))
    return pairs


def pair_plane(at, odd):
    return at ^ 1


def same_side(at, n):
    return 2 * ((at // 2 + n) % PAIRS) + at % 2


def plane_across(at, odd):
    return (at + 1 if at % 2 else at - 1) % PLANES


def scalar(x):
    return x.astype(jnp.int32).reshape(1)


def body(queries, key_states, value_states, conv_weight):
    q = queries.reshape(TOKENS, D)
    k = key_states.reshape(TOKENS, D)
    v = value_states.reshape(TOKENS, D)
    shape = jax.ShapeDtypeStruct
    packed, pooled = call(
        pack_kernel,
        (shape((TILES, SENT, TOKENS), BF16), shape((SLOT, D), BF16)),
        3.0,
        q,
        k,
        v,
        scratch=(
            pltpu.VMEM((3, TOKENS, D), BF16),
            pltpu.VMEM((3, TILES, GROUP, TOKENS), BF16),
            pltpu.SemaphoreType.DMA((3,)),
            pltpu.SemaphoreType.DMA((3,)),
        ),
        far=True,
        far_out=True,
    )
    x = exchange(packed, "xy")
    tile = scalar(lax.axis_index("xy"))
    taps = call(taps_kernel, shape((GROUP, 32), F32), 1.0, conv_weight, scalars=(tile,))

    tm = lax.axis_index("tm")
    where = (
        scalar(tm),
        scalar((2 * lax.axis_index("zh") + lax.axis_index("zl") + 7 * (tm & 1)) & 7),
    )
    met = lax.ppermute(pooled, LINE, along(pair_plane))
    couple = call(couple_kernel, shape((SLOT, D), BF16), 1.0, pooled, met, scalars=where[1:])
    came = [couple]
    for n in range(1, PAIRS):
        came.append(lax.ppermute(couple, LINE, along(lambda at, odd: same_side(at, n))))
    by_tile = shape((TILES, PAIRS * SLOT, GROUP), BF16)
    routed = call(route_kernel, by_tile, 1.0, *came, scalars=where[1:])
    agents = exchange(routed, "xy")
    edges = shape((GROUP, EDGE), BF16)
    near, far, turned_q = call(
        edge_kernel, (edges, edges, shape((GROUP, TILES * TOKENS), BF16)), 1.0, x, scalars=where
    )
    groups = lax.axis_size("tm")
    pairs = [(i, i + 1) for i in range(0, groups - 1, 2)]
    near = lax.ppermute(near, "tm", pairs + [(b, a) for a, b in pairs])
    pairs = [(i, i + 1) for i in range(1, groups - 1, 2)]
    far = lax.ppermute(far, "tm", pairs + [(b, a) for a, b in pairs])
    keep, send = call(
        agent_kernel,
        (shape((GROUP + 8, AGENTS), F32), shape((GROUP + STATS, AGENTS), BF16)),
        3.0,
        agents,
        x,
    )
    theirs = lax.ppermute(send, LINE, along(pair_plane))
    row = shape((GROUP, TOKENS), BF16)
    cross, kin = call(rim_kernel, (row, row), 1.0, x, near, far, taps, scalars=where)
    blended = call(blend_kernel, shape((GROUP + STATS, AGENTS), BF16), 1.0, keep, theirs)
    cross = lax.ppermute(cross, LINE, along(plane_across))
    parts = [blended]
    for n in range(1, PAIRS):
        parts.append(
            lax.ppermute(blended, LINE, along(lambda at, odd: same_side(at, -n if odd else n)))
        )
    kin = lax.ppermute(kin, LINE, along(pair_plane))
    local = call(
        conv_kernel, shape((TILES, GROUP, TOKENS), F32), 5.0, x, near, far, taps, scalars=where
    )
    values = call(comb_kernel, shape((GROUP, AGENTS), BF16), 1.0, *parts)
    weights, totals = call(
        query_kernel,
        (shape((GROUP_HEADS, AGENTS, TILES * TOKENS), BF16), shape((8, TILES * TOKENS), F32)),
        2.0,
        agents,
        turned_q,
    )
    mixed = call(
        mix_kernel,
        shape((TILES, GROUP, TOKENS), BF16),
        1.0,
        weights,
        totals,
        values,
        cross,
        kin,
        local,
        scalars=where,
    )
    mine = exchange(mixed, "xy")
    pieces = TILES // 2
    out = call(
        unpack_kernel,
        shape((TOKENS, D), BF16),
        1.0,
        mine,
        scratch=(
            pltpu.VMEM((pieces, TOKENS, D // pieces), BF16),
            pltpu.SemaphoreType.DMA((pieces,)),
        ),
        far_out=True,
    )
    return out.reshape(value_states.shape)


def solution(mesh):
    devices = mesh.devices
    fine = Mesh(devices.reshape(devices.shape[0], PAIRS, 2, TILES), ("tm", "zh", "zl", "xy"))
    spec = P("tm", None, ("zh", "zl", "xy"), None, None)
    return jax.shard_map(
        body,
        mesh=fine,
        in_specs=(spec, spec, spec, P()),
        out_specs=spec,
        check_vma=False,
    )
```
